256 devices in a mesh: song: 4 (over y), seq: 64 (over z, x, core).
Axes of the slice: x: 4, y: 4, z: 8, core: 2. Of those that a mesh axis runs over, the one named last changes fastest.
Arguments:
- queries: bfloat16 [4, 8192, 2048], P('song', 'seq'), may hold values from -64 to 64
- keys: bfloat16 [4, 8192, 2048], P('song', 'seq'), may hold values from -64 to 64
- values: bfloat16 [4, 8192, 2048], P('song', 'seq'), may hold values from -6 to 6
- lyric_keys: bfloat16 [4, 384, 2048], P('song', 'seq'), may hold values from -64 to 64
- lyric_values: bfloat16 [4, 384, 2048], P('song', 'seq'), may hold values from -6 to 6
- q_gain: float32 [128], replicated, may hold values from 0.5 to 1.5
- k_gain: float32 [128], replicated, may hold values from 0.5 to 1.5
- cotangent: bfloat16 [4, 8192, 2048], P('song', 'seq'), may hold values from -12 to 12
- alignment: int32 [4, 64, 2], P('song', 'seq'), may hold values from -1 to 2, as said below
- lyric_len: int32 [4], P('song'), may hold values from 192 to 384
Outputs:
- attn_out: bfloat16 [4, 8192, 2048], P('song', 'seq')
- grad_queries: bfloat16 [4, 8192, 2048], P('song', 'seq')
- grad_keys: bfloat16 [4, 8192, 2048], P('song', 'seq')
- grad_values: bfloat16 [4, 8192, 2048], P('song', 'seq')
- grad_lyric_keys: bfloat16 [4, 384, 2048], P('song', 'seq')
- grad_lyric_values: bfloat16 [4, 384, 2048], P('song', 'seq')
- grad_q_gain: float32 [128], replicated
- grad_k_gain: float32 [128], replicated
The draws below stay inside these ranges and needn't reach their ends.
Inputs may be any that keep to these rules, and one draw needn't show every extreme that they name: `alignment`: in each row the entries that are not -1 are distinct.
All inputs are finite; a program needn't handle non-finite values.
Results may differ from the reference program's by a relative error of at most 0.01.
Values may be sent and summed in bfloat16 or wider, within the bound.
A program may use at most 128 MiB of HBM per device.

```python
import jax
import jax.numpy as jnp
from jax import lax

H = 16
HD = 128
MODEL_DIM = 2048
BLK = 128
WIN = 1
TILES = 2
LYRIC_TOKENS = 384
SONGS = 4
AUDIO_FRAMES = 8192
NAB = 64
NLB = 3


def scaled_draw(key, song_count, row_count):
    first_key, second_key, third_key = jax.random.split(key, 3)
    shape = (song_count, row_count, H, HD)
    base = jnp.clip(jax.random.normal(first_key, shape, jnp.float32), -6.0, 6.0)
    row_scale = 10.0 ** jax.random.uniform(second_key, (song_count, row_count, H, 1), jnp.float32, -0.5, 0.5)
    col_scale = 10.0 ** jax.random.uniform(third_key, (HD,), jnp.float32, -0.5, 0.5)
    return (base * row_scale * col_scale).reshape(song_count, row_count, H * HD).astype(jnp.bfloat16)


def draw_queries(key, part):
    return scaled_draw(jax.random.fold_in(key, 11), SONGS, AUDIO_FRAMES)


def draw_keys(key, part):
    return scaled_draw(jax.random.fold_in(key, 12), SONGS, AUDIO_FRAMES)


def draw_lyric_keys(key, part):
    return scaled_draw(jax.random.fold_in(key, 13), SONGS, LYRIC_TOKENS)


def draw_cotangent(key, part):
    first_key = jax.random.fold_in(jax.random.fold_in(key, 14), 0)
    shape = (SONGS, AUDIO_FRAMES, H * HD)
    ramp = 0.5 + lax.broadcasted_iota(jnp.float32, (1, AUDIO_FRAMES, 1), 1) / AUDIO_FRAMES
    noise = jnp.clip(jax.random.normal(first_key, shape, jnp.float32), -6.0, 6.0)
    return (noise * ramp).astype(jnp.bfloat16)


def draw_alignment(key, part):
    first_key, second_key = jax.random.split(jax.random.fold_in(key, 15))
    grid = (SONGS, NAB, NLB)
    ranking = jax.random.randint(first_key, grid, 0, 1 << 20) * NLB + lax.broadcasted_iota(jnp.int32, grid, 2)
    order = jnp.argsort(ranking, axis=-1)
    picked = order[..., :TILES].astype(jnp.int32)
    dropped = jax.random.randint(second_key, (SONGS, NAB, TILES), 0, 4) == 0
    return jnp.where(dropped, -1, picked).astype(jnp.int32)


def set_ends(result, stream_key, smallest, largest):
    dims = result.shape
    spot = [jax.random.randint(jax.random.fold_in(stream_key, axis), (), 0, dims[axis]) for axis in range(len(dims))]
    result = result.at[tuple(spot)].set(smallest)
    longest = dims.index(max(dims))
    spot[longest] = (spot[longest] + 1) % dims[longest]
    return result.at[tuple(spot)].set(largest)


def level_of(stream_key, shape, cuts, smallest, top_value):
    def one(dim, parts):
        heights = jax.random.uniform(jax.random.fold_in(jax.random.fold_in(stream_key, 6), dim), (parts,), jnp.float32, smallest / len(cuts), top_value / len(cuts))
        return jnp.repeat(jnp.exp(heights), shape[dim] // parts).reshape((-1,) + (1,) * (len(shape) - dim - 1))

    gain = one(*cuts[0])
    for cut in cuts[1:]:
        gain = gain * one(*cut)
    return gain


def scatter_about(own_key, shape, width, limit, shards=(), kind=jnp.bfloat16):
    loudness = level_of(own_key, shape, shards, -0.22, 0.18) if shards else 1.0
    entries = jax.random.normal(own_key, shape, jnp.float32) * width * loudness
    return jnp.minimum(jnp.maximum(entries, -limit), limit).astype(kind)


def setup_inputs(seed: int = 0) -> dict:
    arg_keys = jax.random.split(jax.random.key(seed), 11)
    queries = draw_queries(jax.random.fold_in(arg_keys[10], 71), 0)
    keys = draw_keys(jax.random.fold_in(arg_keys[10], 71), 0)
    values = scatter_about(arg_keys[2], (SONGS, AUDIO_FRAMES, MODEL_DIM), 1.0, 6.0, ((0, 4), (1, 64)))
    lyric_keys = draw_lyric_keys(jax.random.fold_in(arg_keys[10], 71), 0)
    lyric_values = scatter_about(arg_keys[4], (SONGS, LYRIC_TOKENS, MODEL_DIM), 1.0, 6.0, ((0, 4), (1, 64)))
    q_gain = jnp.clip(1.0 + 0.1 * jax.random.normal(arg_keys[5], (HD,), jnp.float32), 0.5, 1.5)
    k_gain = jnp.clip(1.0 + 0.1 * jax.random.normal(arg_keys[6], (HD,), jnp.float32), 0.5, 1.5)
    cotangent = draw_cotangent(jax.random.fold_in(arg_keys[10], 71), 0)
    alignment = draw_alignment(jax.random.fold_in(arg_keys[10], 71), 0)
    lyric_len = set_ends(jax.random.randint(arg_keys[9], (SONGS,), LYRIC_TOKENS // 2, LYRIC_TOKENS + 1), jax.random.fold_in(arg_keys[9], 1), LYRIC_TOKENS // 2, LYRIC_TOKENS).astype(jnp.int32)
    return dict(queries=queries, keys=keys, values=values, lyric_keys=lyric_keys, lyric_values=lyric_values, q_gain=q_gain, k_gain=k_gain, cotangent=cotangent, alignment=alignment, lyric_len=lyric_len)


NORM_EPS = 1e-06

def norm_heads(inputs, norm_gain):
    row_values = inputs.astype(jnp.float32).reshape(inputs.shape[0], -1, norm_gain.shape[0])
    inverse = lax.rsqrt(lax.optimization_barrier(jnp.mean(row_values * row_values, axis=-1, keepdims=True)) + NORM_EPS)
    return (row_values * inverse * norm_gain, inverse)

def norm_back(inputs, inverse, norm_gain, grad_out):
    row_values = inputs.astype(jnp.float32).reshape(grad_out.shape)
    scaled = grad_out * norm_gain
    grad_input = inverse * scaled - row_values * inverse * inverse * inverse * lax.optimization_barrier(jnp.mean(scaled * row_values, axis=-1, keepdims=True))
    grad_gain = lax.optimization_barrier(jnp.sum(grad_out * row_values * inverse, axis=(0, 1)))
    return (grad_input.reshape(inputs.shape), grad_gain)

def block_pass(query_rows, key_rows, value_rows, keep_mask, grad_rows, score_scale):
    query_f = query_rows.astype(jnp.float32)
    key_f = key_rows.astype(jnp.float32)
    value_f = value_rows.astype(jnp.float32)
    grad_f = grad_rows.astype(jnp.float32)
    scores = jnp.einsum('qhd,khd->hqk', query_f, key_f) * score_scale
    exp_scores = jnp.where(keep_mask[None, None, :], jnp.exp(scores), jnp.float32(0.0))
    totals = lax.optimization_barrier(jnp.sum(exp_scores, axis=2))
    prob_full = exp_scores / totals[:, :, None]
    prob_low = prob_full.astype(jnp.bfloat16)
    block_output = jnp.einsum('hqk,khd->qhd', prob_low.astype(jnp.float32), value_f).astype(jnp.bfloat16)
    delta_rows = lax.optimization_barrier(jnp.sum(grad_f * block_output.astype(jnp.float32), axis=2))
    grad_prob = jnp.einsum('qhd,khd->hqk', grad_f, value_f)
    grad_score = (prob_full * (grad_prob - delta_rows.T[:, :, None])).astype(jnp.bfloat16).astype(jnp.float32)
    query_gradient = jnp.einsum('hqk,khd->qhd', grad_score, key_f) * score_scale
    grad_key = jnp.einsum('hqk,qhd->khd', grad_score, query_f) * score_scale
    value_gradient = jnp.einsum('hqk,qhd->khd', prob_low.astype(jnp.float32), grad_f)
    return (block_output, query_gradient, grad_key, value_gradient)

def reference(queries, keys, values, lyric_keys, lyric_values, q_gain, k_gain, cotangent, alignment, lyric_len):
    score_scale = HD ** (-0.5)
    border_rows = WIN * BLK
    window_extent = (2 * WIN + 1) * BLK

    def one_song(song_args):
        query_raw, key_raw, value_raw, lyric_raw, lyric_vals, grad_raw, align_rows, length = song_args
        query_full, query_inv = norm_heads(query_raw, q_gain)
        key_full, key_inv = norm_heads(key_raw, k_gain)
        lyric_full, lyric_inv = norm_heads(lyric_raw, k_gain)
        query_norm = query_full.astype(jnp.bfloat16)
        key_norm = key_full.astype(jnp.bfloat16)
        lyric_norm = lyric_full.astype(jnp.bfloat16)
        lyric_vh = lyric_vals.reshape(LYRIC_TOKENS, H, HD)
        padding = ((border_rows, border_rows), (0, 0), (0, 0))
        key_pad = jnp.pad(key_norm, padding)
        value_pad = jnp.pad(value_raw.reshape(AUDIO_FRAMES, H, HD), padding)
        grad_heads = grad_raw.reshape(AUDIO_FRAMES, H, HD)

        def scan_step(carried_state, block_id):
            padded_key_gradient, padded_value_gradient, lyric_key_gradient, lyric_value_gradient = carried_state
            start_offset = block_id * BLK
            query_rows = lax.dynamic_slice_in_dim(query_norm, start_offset, BLK, 0)
            grad_rows = lax.dynamic_slice_in_dim(grad_heads, start_offset, BLK, 0)
            audio_keys = lax.dynamic_slice_in_dim(key_pad, start_offset, window_extent, 0)
            audio_vals = lax.dynamic_slice_in_dim(value_pad, start_offset, window_extent, 0)
            position = start_offset - border_rows + jnp.arange(window_extent, dtype=jnp.int32)
            audio_mask = (position >= 0) & (position < AUDIO_FRAMES)
            tile_ids = align_rows[block_id]
            row_grid = (jnp.maximum(tile_ids, 0) * BLK)[:, None] + jnp.arange(BLK, dtype=jnp.int32)[None, :]
            lyric_mask = ((tile_ids >= 0)[:, None] & (row_grid < length)).reshape(-1)
            row_index = row_grid.reshape(-1)
            all_keys = jnp.concatenate([audio_keys, lyric_norm[row_index]], axis=0)
            all_vals = jnp.concatenate([audio_vals, lyric_vh[row_index]], axis=0)
            keep_mask = jnp.concatenate([audio_mask, lyric_mask], axis=0)
            block_output, query_gradient, grad_key, value_gradient = block_pass(query_rows, all_keys, all_vals, keep_mask, grad_rows, score_scale)
            padded_key_gradient = lax.dynamic_update_slice_in_dim(padded_key_gradient, lax.dynamic_slice_in_dim(padded_key_gradient, start_offset, window_extent, 0) + grad_key[:window_extent], start_offset, 0)
            padded_value_gradient = lax.dynamic_update_slice_in_dim(padded_value_gradient, lax.dynamic_slice_in_dim(padded_value_gradient, start_offset, window_extent, 0) + value_gradient[:window_extent], start_offset, 0)
            lyric_key_gradient = lyric_key_gradient.at[row_index].add(grad_key[window_extent:])
            lyric_value_gradient = lyric_value_gradient.at[row_index].add(value_gradient[window_extent:])
            return ((padded_key_gradient, padded_value_gradient, lyric_key_gradient, lyric_value_gradient), (block_output, query_gradient))
        zeros_pad = jnp.zeros((AUDIO_FRAMES + 2 * border_rows, H, HD), jnp.float32)
        zeros_lyric = jnp.zeros((LYRIC_TOKENS, H, HD), jnp.float32)
        carried_state, stacked = lax.scan(scan_step, (zeros_pad, zeros_pad, zeros_lyric, zeros_lyric), jnp.arange(NAB, dtype=jnp.int32))
        padded_key_gradient, padded_value_gradient, lyric_key_gradient, lyric_value_gradient = carried_state
        output_list, grad_qn = stacked
        unnormed_query_gradient, query_gain_vector = norm_back(query_raw, query_inv, q_gain, grad_qn.reshape(AUDIO_FRAMES, H, HD))
        unnormed_key_gradient, key_gain_vector = norm_back(key_raw, key_inv, k_gain, padded_key_gradient[border_rows:border_rows + AUDIO_FRAMES])
        unnormed_lyric_gradient, lyric_gain_vector = norm_back(lyric_raw, lyric_inv, k_gain, lyric_key_gradient)
        return (output_list.reshape(AUDIO_FRAMES, MODEL_DIM), unnormed_query_gradient.astype(jnp.bfloat16), unnormed_key_gradient.astype(jnp.bfloat16), padded_value_gradient[border_rows:border_rows + AUDIO_FRAMES].reshape(AUDIO_FRAMES, MODEL_DIM).astype(jnp.bfloat16), unnormed_lyric_gradient.astype(jnp.bfloat16), lyric_value_gradient.reshape(LYRIC_TOKENS, MODEL_DIM).astype(jnp.bfloat16), query_gain_vector, key_gain_vector + lyric_gain_vector)
    results = lax.map(one_song, (queries, keys, values, lyric_keys, lyric_values, cotangent, alignment, lyric_len))
    return (results[0], results[1], results[2], results[3], results[4], results[5], lax.optimization_barrier(jnp.sum(results[6], axis=0)), lax.optimization_barrier(jnp.sum(results[7], axis=0)))
```

```python
import jax
import jax.numpy as jnp
from jax import lax
from jax.sharding import PartitionSpec as P

BLK = 128
WIN = 1
TILES = 2


NORM_EPS = 1e-06


def extended_2(block, sides, width):
    for axis, dim in sides:
        count = lax.axis_size(axis)
        forward = [(i, i + 1) for i in range(count - 1)]
        backward = [(target, source) for source, target in forward]
        low = lax.ppermute(
            lax.slice_in_dim(block, block.shape[dim] - width, None, axis=dim), axis, forward
        )
        high = lax.ppermute(lax.slice_in_dim(block, 0, width, axis=dim), axis, backward)
        block = jnp.concatenate([low, block, high], axis=dim)
    return block


def norm_heads(inputs, norm_gain):
    row_values = inputs.astype(jnp.float32).reshape(inputs.shape[0], -1, norm_gain.shape[0])
    inverse = lax.rsqrt(jnp.mean(row_values * row_values, axis=-1, keepdims=True) + NORM_EPS)
    return (row_values * inverse * norm_gain, inverse)


def norm_back(inputs, inverse, norm_gain, grad_out):
    row_values = inputs.astype(jnp.float32).reshape(grad_out.shape)
    scaled = grad_out * norm_gain
    grad_input = inverse * scaled - row_values * inverse * inverse * inverse * jnp.mean(
        scaled * row_values, axis=-1, keepdims=True
    )
    grad_gain = jnp.sum(grad_out * row_values * inverse, axis=(0, 1))
    return (grad_input.reshape(inputs.shape), grad_gain)


def block_pass(query_rows, key_rows, value_rows, keep_mask, grad_rows, score_scale):
    scores = (
        jnp.einsum("qhd,khd->hqk", query_rows, key_rows, preferred_element_type=jnp.float32)
        * score_scale
    )
    exp_scores = jnp.where(keep_mask[None, None, :], jnp.exp(scores), 0.0)
    totals = jnp.sum(exp_scores, axis=2)
    prob_full = exp_scores / totals[:, :, None]
    prob_low = prob_full.astype(jnp.bfloat16)
    block_output = jnp.einsum(
        "hqk,khd->qhd", prob_low, value_rows, preferred_element_type=jnp.float32
    ).astype(jnp.bfloat16)
    delta_rows = jnp.sum(grad_rows.astype(jnp.float32) * block_output.astype(jnp.float32), axis=2).T
    grad_prob = jnp.einsum(
        "qhd,khd->hqk", grad_rows, value_rows, preferred_element_type=jnp.float32
    )
    grad_score = (prob_full * (grad_prob - delta_rows[:, :, None])).astype(jnp.bfloat16)
    query_gradient = (
        jnp.einsum("hqk,khd->qhd", grad_score, key_rows, preferred_element_type=jnp.float32)
        * score_scale
    )
    grad_key = (
        jnp.einsum("hqk,qhd->khd", grad_score, query_rows, preferred_element_type=jnp.float32)
        * score_scale
    )
    value_gradient = jnp.einsum(
        "hqk,qhd->khd", prob_low, grad_rows, preferred_element_type=jnp.float32
    )
    return (block_output, query_gradient, grad_key, value_gradient)


def body(
    queries, keys, values, lyric_keys, lyric_values, q_gain, k_gain, cotangent, alignment, lyric_len
):
    head_size = q_gain.shape[0]
    model_width = queries.shape[2]
    head_count = model_width // head_size
    frames = queries.shape[1]
    lyric_local = lyric_keys.shape[1]
    seq_count = lax.axis_size("seq")
    border_rows = WIN * BLK
    window_extent = (2 * WIN + 1) * BLK
    score_scale = head_size ** (-0.5)
    total_frames = frames * seq_count
    first_frame = lax.axis_index("seq") * frames
    lyric_total = lyric_local * seq_count
    lyric_blocks = lyric_total // BLK

    lyric_pair = jnp.stack([lyric_keys[0], lyric_values[0]])
    lyric_all = lax.all_gather(lyric_pair, "seq", axis=1, tiled=True)
    lyric_raw_all = lyric_all[0]
    lyric_val_all = lyric_all[1].reshape(lyric_total, head_count, head_size)

    query_raw = queries[0]
    key_raw = keys[0]
    query_full, query_inv = norm_heads(query_raw, q_gain)
    key_full, key_inv = norm_heads(key_raw, k_gain)
    lyric_full_all, lyric_inv_all = norm_heads(lyric_raw_all, k_gain)
    lyric_inv = norm_heads(lyric_keys[0], k_gain)[1]
    query_norm = query_full.astype(jnp.bfloat16)
    key_norm = key_full.astype(jnp.bfloat16)
    lyric_key_all = lyric_full_all.astype(jnp.bfloat16)

    stacked = jnp.stack([key_norm.reshape(frames, model_width), values[0]])
    extended = extended_2(stacked, (("seq", 1),), border_rows)
    ext_keys = extended[0].reshape(frames + 2 * border_rows, head_count, head_size)
    ext_vals = extended[1].reshape(frames + 2 * border_rows, head_count, head_size)
    grad_heads = cotangent[0].reshape(frames, head_count, head_size)
    length = lyric_len[0]

    position = first_frame - border_rows + jnp.arange(window_extent, dtype=jnp.int32)
    audio_mask = (position >= 0) & (position < total_frames)
    tile_ids = alignment[0, 0]
    starts = [jnp.maximum(tile_ids[s], 0) * BLK for s in range(TILES)]
    slot_keys = [lax.dynamic_slice_in_dim(lyric_key_all, st, BLK, 0) for st in starts]
    slot_vals = [lax.dynamic_slice_in_dim(lyric_val_all, st, BLK, 0) for st in starts]
    lyric_mask = jnp.concatenate(
        [(tile_ids[s] >= 0) & (starts[s] + jnp.arange(BLK, dtype=jnp.int32) < length) for s in range(TILES)]
    )
    all_keys = jnp.concatenate([ext_keys] + slot_keys, axis=0)
    all_vals = jnp.concatenate([ext_vals] + slot_vals, axis=0)
    keep_mask = jnp.concatenate([audio_mask, lyric_mask], axis=0)
    block_output, grad_qn, grad_key, value_gradient = block_pass(
        query_norm, all_keys, all_vals, keep_mask, grad_heads, score_scale
    )

    lyric_gk = grad_key[window_extent:].reshape(TILES, BLK, head_count, head_size)
    lyric_gv = value_gradient[window_extent:].reshape(TILES, BLK, head_count, head_size)
    block_ids = jnp.arange(lyric_blocks, dtype=jnp.int32)
    pick = [(tile_ids[s] == block_ids)[:, None, None, None] for s in range(TILES)]
    part_gk = sum(jnp.where(pick[s], lyric_gk[s][None], 0.0) for s in range(TILES))
    part_gv = sum(jnp.where(pick[s], lyric_gv[s][None], 0.0) for s in range(TILES))

    lyric_scaled_all = lyric_raw_all.astype(jnp.float32).reshape(lyric_blocks, BLK, head_count, head_size) * (
        lyric_inv_all.reshape(lyric_blocks, BLK, head_count, 1)
    )
    lyric_gain_vector = jnp.sum(part_gk * lyric_scaled_all, axis=(0, 1, 2))

    parts = jnp.stack([part_gk, part_gv]).reshape(2, seq_count, lyric_local * model_width)
    summed = lax.psum_scatter(parts, "seq", scatter_dimension=1, tiled=True)
    summed_key = summed[0].reshape(lyric_local, head_count, head_size)
    summed_val = summed[1].reshape(lyric_local, model_width)

    ext_grad_key = grad_key[:window_extent]
    ext_grad_val = value_gradient[:window_extent]
    own_grad_key = ext_grad_key[border_rows : border_rows + frames]
    own_grad_val = ext_grad_val[border_rows : border_rows + frames]
    rims = jnp.stack(
        [
            jnp.concatenate(
                [ext_grad_key[:border_rows], ext_grad_key[border_rows + frames :]], axis=0
            ).reshape(2 * border_rows, model_width),
            jnp.concatenate(
                [ext_grad_val[:border_rows], ext_grad_val[border_rows + frames :]], axis=0
            ).reshape(2 * border_rows, model_width),
        ]
    )
    received = extended_2(rims.astype(jnp.bfloat16), (("seq", 1),), border_rows).astype(rims.dtype)
    from_left = received[:, :border_rows].reshape(2, border_rows, head_count, head_size)
    from_right = received[:, 3 * border_rows :].reshape(2, border_rows, head_count, head_size)
    own_grad_key = (
        own_grad_key.at[:border_rows]
        .add(from_left[0])
        .at[frames - border_rows :]
        .add(from_right[0])
    )
    own_grad_val = (
        own_grad_val.at[:border_rows]
        .add(from_left[1])
        .at[frames - border_rows :]
        .add(from_right[1])
    )
    unnormed_query_gradient, query_gain_vector = norm_back(
        query_raw, query_inv, q_gain, grad_qn.reshape(frames, head_count, head_size)
    )
    unnormed_key_gradient, key_gain_vector = norm_back(key_raw, key_inv, k_gain, own_grad_key)
    total_gains = lax.psum(
        jnp.stack([query_gain_vector, key_gain_vector + lyric_gain_vector]), ("song", "seq")
    )
    unnormed_lyric_gradient = norm_back(lyric_keys[0], lyric_inv, k_gain, summed_key)[0]
    return (
        block_output.reshape(1, frames, model_width),
        unnormed_query_gradient.astype(jnp.bfloat16)[None],
        unnormed_key_gradient.astype(jnp.bfloat16)[None],
        own_grad_val.reshape(1, frames, model_width).astype(jnp.bfloat16),
        unnormed_lyric_gradient.astype(jnp.bfloat16)[None],
        summed_val.astype(jnp.bfloat16)[None],
        total_gains[0],
        total_gains[1],
    )


def solution(mesh):
    in_specs = (
        P("song", "seq", None),
        P("song", "seq", None),
        P("song", "seq", None),
        P("song", "seq", None),
        P("song", "seq", None),
        P(),
        P(),
        P("song", "seq", None),
        P("song", "seq", None),
        P("song"),
    )
    out_specs = (
        P("song", "seq", None),
        P("song", "seq", None),
        P("song", "seq", None),
        P("song", "seq", None),
        P("song", "seq", None),
        P("song", "seq", None),
        P(),
        P(),
    )
    return jax.shard_map(body, mesh=mesh, in_specs=in_specs, out_specs=out_specs, check_vma=False)
```

```python
import jax
import jax.numpy as jnp
from jax import lax
from jax.sharding import PartitionSpec as P

BLK = 128
WIN = 1
TILES = 2


NORM_EPS = 1e-06


def extended_2(block, sides, width):
    for axis, dim in sides:
        count = lax.axis_size(axis)
        forward = [(i, i + 1) for i in range(count - 1)]
        backward = [(target, source) for source, target in forward]
        low = lax.ppermute(
            lax.slice_in_dim(block, block.shape[dim] - width, None, axis=dim), axis, forward
        )
        high = lax.ppermute(lax.slice_in_dim(block, 0, width, axis=dim), axis, backward)
        block = jnp.concatenate([low, block, high], axis=dim)
    return block


def seq_masks(count):
    masks = []
    m = 1
    while m < count:
        masks.append(m)
        m *= 2
    return masks


def swap_with(x, axis, mask):
    count = lax.axis_size(axis)
    return lax.ppermute(x, axis, [(i, i ^ mask) for i in range(count)])


def gather_doubling(chunk, axis, order):
    idx = lax.axis_index(axis)
    buf = chunk[None]
    for mask in order:
        other = swap_with(buf, axis, mask)
        high = (idx & mask) != 0
        buf = jnp.where(high, jnp.concatenate([other, buf]), jnp.concatenate([buf, other]))
    steps = len(order)
    buf = buf.reshape((2,) * steps + chunk.shape)
    held = [order[steps - 1 - k] for k in range(steps)]
    perm = sorted(range(steps), key=lambda k: -held[k])
    buf = jnp.transpose(buf, perm + list(range(steps, buf.ndim)))
    return buf.reshape((2 ** steps,) + chunk.shape)


def scatter_halving(parts, axis, order):
    idx = lax.axis_index(axis)
    count = parts.shape[0]
    steps = len(order)
    buf = parts.reshape((2,) * steps + parts.shape[1:])
    held = sorted(order, reverse=True)
    for mask in order:
        a = held.index(mask)
        high = ((idx & mask) != 0).astype(jnp.int32)
        keep = lax.dynamic_index_in_dim(buf, high, axis=a, keepdims=False)
        send = lax.dynamic_index_in_dim(buf, 1 - high, axis=a, keepdims=False)
        buf = keep + swap_with(send, axis, mask)
        held.pop(a)
    return buf


def sum_doubling(x, axes):
    for axis in axes:
        for mask in seq_masks(lax.axis_size(axis)):
            x = x + swap_with(x, axis, mask)
    return x


def norm_heads(inputs, norm_gain):
    row_values = inputs.astype(jnp.float32).reshape(inputs.shape[0], -1, norm_gain.shape[0])
    inverse = lax.rsqrt(jnp.mean(row_values * row_values, axis=-1, keepdims=True) + NORM_EPS)
    return (row_values * inverse * norm_gain, inverse)


def norm_back(inputs, inverse, norm_gain, grad_out):
    row_values = inputs.astype(jnp.float32).reshape(grad_out.shape)
    scaled = grad_out * norm_gain
    grad_input = inverse * scaled - row_values * inverse * inverse * inverse * jnp.mean(
        scaled * row_values, axis=-1, keepdims=True
    )
    grad_gain = jnp.sum(grad_out * row_values * inverse, axis=(0, 1))
    return (grad_input.reshape(inputs.shape), grad_gain)


def block_pass(query_rows, key_rows, value_rows, keep_mask, grad_rows, score_scale):
    scores = (
        jnp.einsum("qhd,khd->hqk", query_rows, key_rows, preferred_element_type=jnp.float32)
        * score_scale
    )
    exp_scores = jnp.where(keep_mask[None, None, :], jnp.exp(scores), 0.0)
    totals = jnp.sum(exp_scores, axis=2)
    prob_full = exp_scores / totals[:, :, None]
    prob_low = prob_full.astype(jnp.bfloat16)
    block_output = jnp.einsum(
        "hqk,khd->qhd", prob_low, value_rows, preferred_element_type=jnp.float32
    ).astype(jnp.bfloat16)
    delta_rows = jnp.sum(grad_rows.astype(jnp.float32) * block_output.astype(jnp.float32), axis=2).T
    grad_prob = jnp.einsum(
        "qhd,khd->hqk", grad_rows, value_rows, preferred_element_type=jnp.float32
    )
    grad_score = (prob_full * (grad_prob - delta_rows[:, :, None])).astype(jnp.bfloat16)
    query_gradient = (
        jnp.einsum("hqk,khd->qhd", grad_score, key_rows, preferred_element_type=jnp.float32)
        * score_scale
    )
    grad_key = (
        jnp.einsum("hqk,qhd->khd", grad_score, query_rows, preferred_element_type=jnp.float32)
        * score_scale
    )
    value_gradient = jnp.einsum(
        "hqk,qhd->khd", prob_low, grad_rows, preferred_element_type=jnp.float32
    )
    return (block_output, query_gradient, grad_key, value_gradient)


def body(
    queries, keys, values, lyric_keys, lyric_values, q_gain, k_gain, cotangent, alignment, lyric_len
):
    head_size = q_gain.shape[0]
    model_width = queries.shape[2]
    head_count = model_width // head_size
    frames = queries.shape[1]
    lyric_local = lyric_keys.shape[1]
    seq_count = lax.axis_size("seq")
    border_rows = WIN * BLK
    window_extent = (2 * WIN + 1) * BLK
    score_scale = head_size ** (-0.5)
    total_frames = frames * seq_count
    first_frame = lax.axis_index("seq") * frames
    lyric_total = lyric_local * seq_count
    lyric_blocks = lyric_total // BLK
    masks = seq_masks(seq_count)

    lyric_pair = jnp.stack([lyric_keys[0], lyric_values[0]])
    lyric_all = gather_doubling(lyric_pair, "seq", masks[::-1])
    lyric_all = jnp.swapaxes(lyric_all, 0, 1).reshape(2, lyric_total, model_width)
    lyric_raw_all = lyric_all[0]
    lyric_val_all = lyric_all[1].reshape(lyric_total, head_count, head_size)

    query_raw = queries[0]
    query_full, query_inv = norm_heads(query_raw, q_gain)
    query_norm = query_full.astype(jnp.bfloat16)
    lyric_full_all, lyric_inv_all = norm_heads(lyric_raw_all, k_gain)
    lyric_inv = norm_heads(lyric_keys[0], k_gain)[1]
    lyric_key_all = lyric_full_all.astype(jnp.bfloat16)

    stacked = jnp.stack([keys[0], values[0]])
    extended = extended_2(stacked, (("seq", 1),), border_rows)
    ext_raw = extended[0]
    ext_full, ext_inv = norm_heads(ext_raw, k_gain)
    ext_keys = ext_full.astype(jnp.bfloat16)
    ext_vals = extended[1].reshape(frames + 2 * border_rows, head_count, head_size)
    key_raw = keys[0]
    key_inv = ext_inv[border_rows : border_rows + frames]
    grad_heads = cotangent[0].reshape(frames, head_count, head_size)
    length = lyric_len[0]

    position = first_frame - border_rows + jnp.arange(window_extent, dtype=jnp.int32)
    audio_mask = (position >= 0) & (position < total_frames)
    tile_ids = alignment[0, 0]
    starts = [jnp.maximum(tile_ids[s], 0) * BLK for s in range(TILES)]
    slot_keys = [lax.dynamic_slice_in_dim(lyric_key_all, st, BLK, 0) for st in starts]
    slot_vals = [lax.dynamic_slice_in_dim(lyric_val_all, st, BLK, 0) for st in starts]
    lyric_mask = jnp.concatenate(
        [(tile_ids[s] >= 0) & (starts[s] + jnp.arange(BLK, dtype=jnp.int32) < length) for s in range(TILES)]
    )
    all_keys = jnp.concatenate([ext_keys] + slot_keys, axis=0)
    all_vals = jnp.concatenate([ext_vals] + slot_vals, axis=0)
    keep_mask = jnp.concatenate([audio_mask, lyric_mask], axis=0)
    block_output, grad_qn, grad_key, value_gradient = block_pass(
        query_norm, all_keys, all_vals, keep_mask, grad_heads, score_scale
    )

    lyric_gk = grad_key[window_extent:].reshape(TILES, BLK, head_count, head_size)
    lyric_gv = value_gradient[window_extent:].reshape(TILES, BLK, head_count, head_size)
    block_ids = jnp.arange(lyric_blocks, dtype=jnp.int32)
    pick = [(tile_ids[s] == block_ids)[:, None, None, None] for s in range(TILES)]
    part_gk = sum(jnp.where(pick[s], lyric_gk[s][None], 0.0) for s in range(TILES))
    part_gv = sum(jnp.where(pick[s], lyric_gv[s][None], 0.0) for s in range(TILES))

    lyric_scaled_all = lyric_raw_all.astype(jnp.float32).reshape(lyric_blocks, BLK, head_count, head_size) * (
        lyric_inv_all.reshape(lyric_blocks, BLK, head_count, 1)
    )
    lyric_gain_vector = jnp.sum(part_gk * lyric_scaled_all, axis=(0, 1, 2))
    ext_scaled = ext_raw.astype(jnp.float32).reshape(window_extent, head_count, head_size) * ext_inv
    key_gain_vector = jnp.sum(grad_key[:window_extent] * ext_scaled, axis=(0, 1))
    query_gain_vector = jnp.sum(
        grad_qn * query_raw.astype(jnp.float32).reshape(frames, head_count, head_size) * query_inv, axis=(0, 1)
    )
    total_gains = sum_doubling(
        jnp.stack([query_gain_vector, key_gain_vector + lyric_gain_vector]), ("seq", "song")
    )

    parts = jnp.stack(
        [part_gk.reshape(seq_count, lyric_local, model_width), part_gv.reshape(seq_count, lyric_local, model_width)],
        axis=1,
    )
    summed = scatter_halving(parts, "seq", masks)
    summed_key = summed[0].reshape(lyric_local, head_count, head_size)
    summed_val = summed[1]

    ext_grad_key = grad_key[:window_extent]
    ext_grad_val = value_gradient[:window_extent]
    own_grad_key = ext_grad_key[border_rows : border_rows + frames]
    own_grad_val = ext_grad_val[border_rows : border_rows + frames]
    rims = jnp.stack(
        [
            jnp.concatenate(
                [ext_grad_key[:border_rows], ext_grad_key[border_rows + frames :]], axis=0
            ).reshape(2 * border_rows, model_width),
            jnp.concatenate(
                [ext_grad_val[:border_rows], ext_grad_val[border_rows + frames :]], axis=0
            ).reshape(2 * border_rows, model_width),
        ]
    )
    received = extended_2(rims.astype(jnp.bfloat16), (("seq", 1),), border_rows).astype(rims.dtype)
    from_left = received[:, :border_rows].reshape(2, border_rows, head_count, head_size)
    from_right = received[:, 3 * border_rows :].reshape(2, border_rows, head_count, head_size)
    own_grad_key = (
        own_grad_key.at[:border_rows]
        .add(from_left[0])
        .at[frames - border_rows :]
        .add(from_right[0])
    )
    own_grad_val = (
        own_grad_val.at[:border_rows]
        .add(from_left[1])
        .at[frames - border_rows :]
        .add(from_right[1])
    )
    unnormed_query_gradient = norm_back(
        query_raw, query_inv, q_gain, grad_qn.reshape(frames, head_count, head_size)
    )[0]
    unnormed_key_gradient = norm_back(key_raw, key_inv, k_gain, own_grad_key)[0]
    unnormed_lyric_gradient = norm_back(lyric_keys[0], lyric_inv, k_gain, summed_key)[0]
    return (
        block_output.reshape(1, frames, model_width),
        unnormed_query_gradient.astype(jnp.bfloat16)[None],
        unnormed_key_gradient.astype(jnp.bfloat16)[None],
        own_grad_val.reshape(1, frames, model_width).astype(jnp.bfloat16),
        unnormed_lyric_gradient.astype(jnp.bfloat16)[None],
        summed_val.astype(jnp.bfloat16)[None],
        total_gains[0],
        total_gains[1],
    )


def solution(mesh):
    in_specs = (
        P("song", "seq", None),
        P("song", "seq", None),
        P("song", "seq", None),
        P("song", "seq", None),
        P("song", "seq", None),
        P(),
        P(),
        P("song", "seq", None),
        P("song", "seq", None),
        P("song"),
    )
    out_specs = (
        P("song", "seq", None),
        P("song", "seq", None),
        P("song", "seq", None),
        P("song", "seq", None),
        P("song", "seq", None),
        P("song", "seq", None),
        P(),
        P(),
    )
    return jax.shard_map(body, mesh=mesh, in_specs=in_specs, out_specs=out_specs, check_vma=False)
```

```python
import jax
import jax.numpy as jnp
from jax import lax
from jax.sharding import PartitionSpec as P
from jax.experimental import pallas as pl
from jax.experimental.pallas import tpu as pltpu

BLK = 128
WIN = 1
TILES = 2


NORM_EPS = 1e-06


def extended_2(block, sides, width):
    for axis, dim in sides:
        count = lax.axis_size(axis)
        forward = [(i, i + 1) for i in range(count - 1)]
        backward = [(target, source) for source, target in forward]
        low = lax.ppermute(
            lax.slice_in_dim(block, block.shape[dim] - width, None, axis=dim), axis, forward
        )
        high = lax.ppermute(lax.slice_in_dim(block, 0, width, axis=dim), axis, backward)
        block = jnp.concatenate([low, block, high], axis=dim)
    return block


def seq_masks(count):
    masks = []
    m = 1
    while m < count:
        masks.append(m)
        m *= 2
    return masks


def swap_with(x, axis, mask):
    count = lax.axis_size(axis)
    return lax.ppermute(x, axis, [(i, i ^ mask) for i in range(count)])


def gather_doubling(chunk, axis, order):
    idx = lax.axis_index(axis)
    buf = chunk[None]
    for mask in order:
        other = swap_with(buf, axis, mask)
        high = (idx & mask) != 0
        buf = jnp.where(high, jnp.concatenate([other, buf]), jnp.concatenate([buf, other]))
    steps = len(order)
    buf = buf.reshape((2,) * steps + chunk.shape)
    held = [order[steps - 1 - k] for k in range(steps)]
    perm = sorted(range(steps), key=lambda k: -held[k])
    buf = jnp.transpose(buf, perm + list(range(steps, buf.ndim)))
    return buf.reshape((2 ** steps,) + chunk.shape)


def scatter_halving(parts, axis, order):
    idx = lax.axis_index(axis)
    count = parts.shape[0]
    steps = len(order)
    buf = parts.reshape((2,) * steps + parts.shape[1:])
    held = sorted(order, reverse=True)
    for mask in order:
        a = held.index(mask)
        high = ((idx & mask) != 0).astype(jnp.int32)
        keep = lax.dynamic_index_in_dim(buf, high, axis=a, keepdims=False)
        send = lax.dynamic_index_in_dim(buf, 1 - high, axis=a, keepdims=False)
        buf = keep + swap_with(send, axis, mask)
        held.pop(a)
    return buf


def sum_doubling(x, axes):
    for axis in axes:
        for mask in seq_masks(lax.axis_size(axis)):
            x = x + swap_with(x, axis, mask)
    return x


def norm_heads(inputs, norm_gain):
    row_values = inputs.astype(jnp.float32).reshape(inputs.shape[0], -1, norm_gain.shape[0])
    inverse = lax.rsqrt(jnp.mean(row_values * row_values, axis=-1, keepdims=True) + NORM_EPS)
    return (row_values * inverse * norm_gain, inverse)


def norm_back(inputs, inverse, norm_gain, grad_out):
    row_values = inputs.astype(jnp.float32).reshape(grad_out.shape)
    scaled = grad_out * norm_gain
    grad_input = inverse * scaled - row_values * inverse * inverse * inverse * jnp.mean(
        scaled * row_values, axis=-1, keepdims=True
    )
    grad_gain = jnp.sum(grad_out * row_values * inverse, axis=(0, 1))
    return (grad_input.reshape(inputs.shape), grad_gain)


def block_pass(query_rows, key_rows, value_rows, keep_mask, grad_rows, score_scale):
    scores = (
        jnp.einsum("qhd,khd->hqk", query_rows, key_rows, preferred_element_type=jnp.float32)
        * score_scale
    )
    exp_scores = jnp.where(keep_mask[None, None, :], jnp.exp(scores), 0.0)
    totals = jnp.sum(exp_scores, axis=2)
    prob_full = exp_scores / totals[:, :, None]
    prob_low = prob_full.astype(jnp.bfloat16)
    block_output = jnp.einsum(
        "hqk,khd->qhd", prob_low, value_rows, preferred_element_type=jnp.float32
    ).astype(jnp.bfloat16)
    delta_rows = jnp.sum(grad_rows.astype(jnp.float32) * block_output.astype(jnp.float32), axis=2).T
    grad_prob = jnp.einsum(
        "qhd,khd->hqk", grad_rows, value_rows, preferred_element_type=jnp.float32
    )
    grad_score = (prob_full * (grad_prob - delta_rows[:, :, None])).astype(jnp.bfloat16)
    query_gradient = (
        jnp.einsum("hqk,khd->qhd", grad_score, key_rows, preferred_element_type=jnp.float32)
        * score_scale
    )
    grad_key = (
        jnp.einsum("hqk,qhd->khd", grad_score, query_rows, preferred_element_type=jnp.float32)
        * score_scale
    )
    value_gradient = jnp.einsum(
        "hqk,qhd->khd", prob_low, grad_rows, preferred_element_type=jnp.float32
    )
    return (block_output, query_gradient, grad_key, value_gradient)


def attention_kernel(
    tiles_ref, q_ref, ek_ref, ev_ref, lk0_ref, lk1_ref, lv0_ref, lv1_ref, g_ref, m_ref,
    o_ref, dq_ref, dke_ref, dve_ref, dkl_ref, dvl_ref, *, scale
):
    f32 = jnp.float32
    window = ek_ref.shape[0]
    q = q_ref[...]
    g = g_ref[...]
    k = jnp.concatenate([ek_ref[...], lk0_ref[...], lk1_ref[...]], axis=0)
    v = jnp.concatenate([ev_ref[...], lv0_ref[...], lv1_ref[...]], axis=0)
    keep = m_ref[...] > 0.0
    nt = (((1,), (1,)), ((), ()))
    tn = (((0,), (0,)), ((), ()))
    s = lax.dot_general(q, k, nt, preferred_element_type=f32) * scale
    e = jnp.where(keep, jnp.exp(s), 0.0)
    tot = jnp.sum(e, axis=1, keepdims=True)
    p = e / tot
    p_low = p.astype(jnp.bfloat16)
    o = jnp.dot(p_low, v, preferred_element_type=f32).astype(jnp.bfloat16)
    o_ref[...] = o
    delta = jnp.sum(g.astype(f32) * o.astype(f32), axis=1, keepdims=True)
    dp = lax.dot_general(g, v, nt, preferred_element_type=f32)
    ds = (p * (dp - delta)).astype(jnp.bfloat16)
    dq_ref[...] = jnp.dot(ds, k, preferred_element_type=f32) * scale
    dk = lax.dot_general(ds, q, tn, preferred_element_type=f32) * scale
    dv = lax.dot_general(p_low, g, tn, preferred_element_type=f32)
    dke_ref[...] = dk[:window]
    dve_ref[...] = dv[:window]
    dkl_ref[...] = dk[window:]
    dvl_ref[...] = dv[window:]


def attention_block(tiles, q, ek, ev, lk, lv, g, keep, head_size, scale):
    rows, width = q.shape
    window = ek.shape[0]
    slots = tiles.shape[0]
    heads = width // head_size
    f32 = jnp.float32

    def col(r):
        return pl.BlockSpec((r, head_size), lambda h, t: (0, h))

    def slot(s):
        return pl.BlockSpec((BLK, head_size), lambda h, t: (t[s], h))

    grid_spec = pltpu.PrefetchScalarGridSpec(
        num_scalar_prefetch=1,
        grid=(heads,),
        in_specs=[col(rows), col(window), col(window), slot(0), slot(1), slot(0), slot(1), col(rows),
                  pl.BlockSpec((1, keep.shape[1]), lambda h, t: (0, 0))],
        out_specs=[col(rows), col(rows), col(window), col(window), col(slots * BLK), col(slots * BLK)],
    )
    return pl.pallas_call(
        lambda *refs: attention_kernel(*refs, scale=scale),
        grid_spec=grid_spec,
        out_shape=[
            jax.ShapeDtypeStruct((rows, width), jnp.bfloat16),
            jax.ShapeDtypeStruct((rows, width), f32),
            jax.ShapeDtypeStruct((window, width), f32),
            jax.ShapeDtypeStruct((window, width), f32),
            jax.ShapeDtypeStruct((slots * BLK, width), f32),
            jax.ShapeDtypeStruct((slots * BLK, width), f32),
        ],
    )(tiles, q, ek, ev, lk, lk, lv, lv, g, keep)


def body(
    queries, keys, values, lyric_keys, lyric_values, q_gain, k_gain, cotangent, alignment, lyric_len
):
    head_size = q_gain.shape[0]
    model_width = queries.shape[2]
    head_count = model_width // head_size
    frames = queries.shape[1]
    lyric_local = lyric_keys.shape[1]
    seq_count = lax.axis_size("seq")
    border_rows = WIN * BLK
    window_extent = (2 * WIN + 1) * BLK
    score_scale = head_size ** (-0.5)
    total_frames = frames * seq_count
    first_frame = lax.axis_index("seq") * frames
    lyric_total = lyric_local * seq_count
    lyric_blocks = lyric_total // BLK
    masks = seq_masks(seq_count)

    lyric_pair = jnp.stack([lyric_keys[0], lyric_values[0]])
    lyric_all = gather_doubling(lyric_pair, "seq", masks[::-1])
    lyric_all = jnp.swapaxes(lyric_all, 0, 1).reshape(2, lyric_total, model_width)
    lyric_raw_all = lyric_all[0]
    lyric_val_all = lyric_all[1].reshape(lyric_total, head_count, head_size)

    query_raw = queries[0]
    query_full, query_inv = norm_heads(query_raw, q_gain)
    query_norm = query_full.astype(jnp.bfloat16)
    lyric_full_all, lyric_inv_all = norm_heads(lyric_raw_all, k_gain)
    lyric_inv = norm_heads(lyric_keys[0], k_gain)[1]
    lyric_key_all = lyric_full_all.astype(jnp.bfloat16)

    stacked = jnp.stack([keys[0], values[0]])
    extended = extended_2(stacked, (("seq", 1),), border_rows)
    ext_raw = extended[0]
    ext_full, ext_inv = norm_heads(ext_raw, k_gain)
    ext_keys = ext_full.astype(jnp.bfloat16)
    ext_vals = extended[1].reshape(frames + 2 * border_rows, head_count, head_size)
    key_raw = keys[0]
    key_inv = ext_inv[border_rows : border_rows + frames]
    grad_heads = cotangent[0].reshape(frames, head_count, head_size)
    length = lyric_len[0]

    position = first_frame - border_rows + jnp.arange(window_extent, dtype=jnp.int32)
    audio_mask = (position >= 0) & (position < total_frames)
    tile_ids = alignment[0, 0]
    tiles = jnp.maximum(tile_ids, 0)
    lyric_mask = jnp.concatenate(
        [(tile_ids[s] >= 0) & (tiles[s] * BLK + jnp.arange(BLK, dtype=jnp.int32) < length) for s in range(TILES)]
    )
    keep_mask = jnp.concatenate([audio_mask, lyric_mask], axis=0).astype(jnp.float32)[None]
    block_output, grad_qn, ext_grad_key, ext_grad_val, slot_gk, slot_gv = attention_block(
        tiles,
        query_norm.reshape(frames, model_width),
        ext_keys.reshape(window_extent, model_width),
        extended[1],
        lyric_key_all.reshape(lyric_total, model_width),
        lyric_all[1],
        cotangent[0],
        keep_mask,
        head_size,
        score_scale,
    )
    grad_qn = grad_qn.reshape(frames, head_count, head_size)
    ext_grad_key = ext_grad_key.reshape(window_extent, head_count, head_size)
    ext_grad_val = ext_grad_val.reshape(window_extent, head_count, head_size)

    lyric_gk = slot_gk.reshape(TILES, BLK, head_count, head_size)
    lyric_gv = slot_gv.reshape(TILES, BLK, head_count, head_size)
    block_ids = jnp.arange(lyric_blocks, dtype=jnp.int32)
    pick = [(tile_ids[s] == block_ids)[:, None, None, None] for s in range(TILES)]
    part_gk = sum(jnp.where(pick[s], lyric_gk[s][None], 0.0) for s in range(TILES))
    part_gv = sum(jnp.where(pick[s], lyric_gv[s][None], 0.0) for s in range(TILES))

    lyric_scaled_all = lyric_raw_all.astype(jnp.float32).reshape(lyric_blocks, BLK, head_count, head_size) * (
        lyric_inv_all.reshape(lyric_blocks, BLK, head_count, 1)
    )
    lyric_gain_vector = jnp.sum(part_gk * lyric_scaled_all, axis=(0, 1, 2))
    ext_scaled = ext_raw.astype(jnp.float32).reshape(window_extent, head_count, head_size) * ext_inv
    key_gain_vector = jnp.sum(ext_grad_key * ext_scaled, axis=(0, 1))
    query_gain_vector = jnp.sum(
        grad_qn * query_raw.astype(jnp.float32).reshape(frames, head_count, head_size) * query_inv, axis=(0, 1)
    )
    total_gains = sum_doubling(
        jnp.stack([query_gain_vector, key_gain_vector + lyric_gain_vector]), ("seq", "song")
    )

    parts = jnp.stack(
        [part_gk.reshape(seq_count, lyric_local, model_width), part_gv.reshape(seq_count, lyric_local, model_width)],
        axis=1,
    )
    summed = scatter_halving(parts, "seq", masks)
    summed_key = summed[0].reshape(lyric_local, head_count, head_size)
    summed_val = summed[1]

    own_grad_key = ext_grad_key[border_rows : border_rows + frames]
    own_grad_val = ext_grad_val[border_rows : border_rows + frames]
    rims = jnp.stack(
        [
            jnp.concatenate(
                [ext_grad_key[:border_rows], ext_grad_key[border_rows + frames :]], axis=0
            ).reshape(2 * border_rows, model_width),
            jnp.concatenate(
                [ext_grad_val[:border_rows], ext_grad_val[border_rows + frames :]], axis=0
            ).reshape(2 * border_rows, model_width),
        ]
    )
    received = extended_2(rims.astype(jnp.bfloat16), (("seq", 1),), border_rows).astype(rims.dtype)
    from_left = received[:, :border_rows].reshape(2, border_rows, head_count, head_size)
    from_right = received[:, 3 * border_rows :].reshape(2, border_rows, head_count, head_size)
    own_grad_key = (
        own_grad_key.at[:border_rows]
        .add(from_left[0])
        .at[frames - border_rows :]
        .add(from_right[0])
    )
    own_grad_val = (
        own_grad_val.at[:border_rows]
        .add(from_left[1])
        .at[frames - border_rows :]
        .add(from_right[1])
    )
    unnormed_query_gradient = norm_back(
        query_raw, query_inv, q_gain, grad_qn.reshape(frames, head_count, head_size)
    )[0]
    unnormed_key_gradient = norm_back(key_raw, key_inv, k_gain, own_grad_key)[0]
    unnormed_lyric_gradient = norm_back(lyric_keys[0], lyric_inv, k_gain, summed_key)[0]
    return (
        block_output.reshape(1, frames, model_width),
        unnormed_query_gradient.astype(jnp.bfloat16)[None],
        unnormed_key_gradient.astype(jnp.bfloat16)[None],
        own_grad_val.reshape(1, frames, model_width).astype(jnp.bfloat16),
        unnormed_lyric_gradient.astype(jnp.bfloat16)[None],
        summed_val.astype(jnp.bfloat16)[None],
        total_gains[0],
        total_gains[1],
    )


def solution(mesh):
    in_specs = (
        P("song", "seq", None),
        P("song", "seq", None),
        P("song", "seq", None),
        P("song", "seq", None),
        P("song", "seq", None),
        P(),
        P(),
        P("song", "seq", None),
        P("song", "seq", None),
        P("song"),
    )
    out_specs = (
        P("song", "seq", None),
        P("song", "seq", None),
        P("song", "seq", None),
        P("song", "seq", None),
        P("song", "seq", None),
        P("song", "seq", None),
        P(),
        P(),
    )
    return jax.shard_map(body, mesh=mesh, in_specs=in_specs, out_specs=out_specs, check_vma=False)
```

```python
import jax
import jax.numpy as jnp
from jax import lax
from jax.sharding import PartitionSpec as P
from jax.experimental import pallas as pl
from jax.experimental.pallas import tpu as pltpu

BLK = 128
WIN = 1
TILES = 2


NORM_EPS = 1e-06


def extended_2(block, sides, width):
    for axis, dim in sides:
        count = lax.axis_size(axis)
        forward = [(i, i + 1) for i in range(count - 1)]
        backward = [(target, source) for source, target in forward]
        low = lax.ppermute(
            lax.slice_in_dim(block, block.shape[dim] - width, None, axis=dim), axis, forward
        )
        high = lax.ppermute(lax.slice_in_dim(block, 0, width, axis=dim), axis, backward)
        block = jnp.concatenate([low, block, high], axis=dim)
    return block


def seq_masks(count):
    masks = []
    m = 1
    while m < count:
        masks.append(m)
        m *= 2
    return masks


def swap_with(x, axis, mask):
    count = lax.axis_size(axis)
    return lax.ppermute(x, axis, [(i, i ^ mask) for i in range(count)])


def gather_doubling(chunk, axis, order):
    idx = lax.axis_index(axis)
    buf = chunk[None]
    for mask in order:
        other = swap_with(buf, axis, mask)
        high = (idx & mask) != 0
        buf = jnp.where(high, jnp.concatenate([other, buf]), jnp.concatenate([buf, other]))
    steps = len(order)
    buf = buf.reshape((2,) * steps + chunk.shape)
    held = [order[steps - 1 - k] for k in range(steps)]
    perm = sorted(range(steps), key=lambda k: -held[k])
    buf = jnp.transpose(buf, perm + list(range(steps, buf.ndim)))
    return buf.reshape((2 ** steps,) + chunk.shape)


def scatter_halving(parts, axis, order):
    idx = lax.axis_index(axis)
    count = parts.shape[0]
    steps = len(order)
    buf = parts.reshape((2,) * steps + parts.shape[1:])
    held = sorted(order, reverse=True)
    for mask in order:
        a = held.index(mask)
        high = ((idx & mask) != 0).astype(jnp.int32)
        keep = lax.dynamic_index_in_dim(buf, high, axis=a, keepdims=False)
        send = lax.dynamic_index_in_dim(buf, 1 - high, axis=a, keepdims=False)
        buf = keep + swap_with(send.astype(jnp.bfloat16), axis, mask).astype(keep.dtype)
        held.pop(a)
    return buf


def sum_doubling(x, axes):
    for axis in axes:
        for mask in seq_masks(lax.axis_size(axis)):
            x = x + swap_with(x, axis, mask)
    return x


def norm_heads(inputs, norm_gain):
    row_values = inputs.astype(jnp.float32).reshape(inputs.shape[0], -1, norm_gain.shape[0])
    inverse = lax.rsqrt(jnp.mean(row_values * row_values, axis=-1, keepdims=True) + NORM_EPS)
    return (row_values * inverse * norm_gain, inverse)


def norm_back(inputs, inverse, norm_gain, grad_out):
    row_values = inputs.astype(jnp.float32).reshape(grad_out.shape)
    scaled = grad_out * norm_gain
    grad_input = inverse * scaled - row_values * inverse * inverse * inverse * jnp.mean(
        scaled * row_values, axis=-1, keepdims=True
    )
    grad_gain = jnp.sum(grad_out * row_values * inverse, axis=(0, 1))
    return (grad_input.reshape(inputs.shape), grad_gain)


def block_pass(query_rows, key_rows, value_rows, keep_mask, grad_rows, score_scale):
    scores = (
        jnp.einsum("qhd,khd->hqk", query_rows, key_rows, preferred_element_type=jnp.float32)
        * score_scale
    )
    exp_scores = jnp.where(keep_mask[None, None, :], jnp.exp(scores), 0.0)
    totals = jnp.sum(exp_scores, axis=2)
    prob_full = exp_scores / totals[:, :, None]
    prob_low = prob_full.astype(jnp.bfloat16)
    block_output = jnp.einsum(
        "hqk,khd->qhd", prob_low, value_rows, preferred_element_type=jnp.float32
    ).astype(jnp.bfloat16)
    delta_rows = jnp.sum(grad_rows.astype(jnp.float32) * block_output.astype(jnp.float32), axis=2).T
    grad_prob = jnp.einsum(
        "qhd,khd->hqk", grad_rows, value_rows, preferred_element_type=jnp.float32
    )
    grad_score = (prob_full * (grad_prob - delta_rows[:, :, None])).astype(jnp.bfloat16)
    query_gradient = (
        jnp.einsum("hqk,khd->qhd", grad_score, key_rows, preferred_element_type=jnp.float32)
        * score_scale
    )
    grad_key = (
        jnp.einsum("hqk,qhd->khd", grad_score, query_rows, preferred_element_type=jnp.float32)
        * score_scale
    )
    value_gradient = jnp.einsum(
        "hqk,qhd->khd", prob_low, grad_rows, preferred_element_type=jnp.float32
    )
    return (block_output, query_gradient, grad_key, value_gradient)


def attention_kernel(
    tiles_ref, q_ref, ek_ref, ev_ref, lk0_ref, lk1_ref, lv0_ref, lv1_ref, g_ref, m_ref, qg_ref, kg_ref,
    o_ref, dqi_ref, dke_ref, dve_ref, dkl_ref, dvl_ref, gain_ref, *, scale
):
    f32 = jnp.float32
    window = ek_ref.shape[0]
    q_gain = qg_ref[...]
    k_gain = kg_ref[...]

    def normed(x_ref, gain):
        x = x_ref[...].astype(f32)
        inv = lax.rsqrt(jnp.mean(x * x, axis=1, keepdims=True) + NORM_EPS)
        return x, inv, (x * inv * gain).astype(jnp.bfloat16)

    qx, qinv, q = normed(q_ref, q_gain)
    kx, kinv, kn = normed(ek_ref, k_gain)
    lx0, linv0, ln0 = normed(lk0_ref, k_gain)
    lx1, linv1, ln1 = normed(lk1_ref, k_gain)
    g = g_ref[...]
    k = jnp.concatenate([kn, ln0, ln1], axis=0)
    v = jnp.concatenate([ev_ref[...], lv0_ref[...], lv1_ref[...]], axis=0)
    keep = m_ref[...] > 0.0
    nt = (((1,), (1,)), ((), ()))
    tn = (((0,), (0,)), ((), ()))
    s = lax.dot_general(q, k, nt, preferred_element_type=f32) * scale
    e = jnp.where(keep, jnp.exp(s), 0.0)
    tot = jnp.sum(e, axis=1, keepdims=True)
    p = e / tot
    p_low = p.astype(jnp.bfloat16)
    o = jnp.dot(p_low, v, preferred_element_type=f32).astype(jnp.bfloat16)
    o_ref[...] = o
    delta = jnp.sum(g.astype(f32) * o.astype(f32), axis=1, keepdims=True)
    dp = lax.dot_general(g, v, nt, preferred_element_type=f32)
    ds = (p * (dp - delta)).astype(jnp.bfloat16)
    dq = jnp.dot(ds, k, preferred_element_type=f32) * scale
    dk = lax.dot_general(ds, q, tn, preferred_element_type=f32) * scale
    dv = lax.dot_general(p_low, g, tn, preferred_element_type=f32)
    scaled = dq * q_gain
    dqi_ref[...] = (
        qinv * scaled - qx * qinv * qinv * qinv * jnp.mean(scaled * qx, axis=1, keepdims=True)
    ).astype(jnp.bfloat16)
    dke_ref[...] = dk[:window]
    dve_ref[...] = dv[:window]
    dkl_ref[...] = dk[window:]
    dvl_ref[...] = dv[window:]
    gq = jnp.sum(dq * qx * qinv, axis=0, keepdims=True)
    gk = (
        jnp.sum(dk[:window] * kx * kinv, axis=0, keepdims=True)
        + jnp.sum(dk[window : window + BLK] * lx0 * linv0, axis=0, keepdims=True)
        + jnp.sum(dk[window + BLK :] * lx1 * linv1, axis=0, keepdims=True)
    )
    gain_ref[...] = jnp.concatenate([gq, gk, jnp.zeros((6, gq.shape[1]), f32)], axis=0)


def attention_block(tiles, q, ek, ev, lk, lv, g, keep, q_gain, k_gain, scale):
    rows, width = q.shape
    head_size = q_gain.shape[0]
    window = ek.shape[0]
    slots = tiles.shape[0]
    heads = width // head_size
    f32 = jnp.float32

    def col(r):
        return pl.BlockSpec((r, head_size), lambda h, t: (0, h))

    def slot(s):
        return pl.BlockSpec((BLK, head_size), lambda h, t: (t[s], h))

    whole = pl.BlockSpec((1, head_size), lambda h, t: (0, 0))
    grid_spec = pltpu.PrefetchScalarGridSpec(
        num_scalar_prefetch=1,
        grid=(heads,),
        in_specs=[col(rows), col(window), col(window), slot(0), slot(1), slot(0), slot(1), col(rows),
                  pl.BlockSpec((1, keep.shape[1]), lambda h, t: (0, 0)), whole, whole],
        out_specs=[col(rows), col(rows), col(window), col(window), col(slots * BLK), col(slots * BLK), col(8)],
    )
    return pl.pallas_call(
        lambda *refs: attention_kernel(*refs, scale=scale),
        grid_spec=grid_spec,
        out_shape=[
            jax.ShapeDtypeStruct((rows, width), jnp.bfloat16),
            jax.ShapeDtypeStruct((rows, width), jnp.bfloat16),
            jax.ShapeDtypeStruct((window, width), f32),
            jax.ShapeDtypeStruct((window, width), f32),
            jax.ShapeDtypeStruct((slots * BLK, width), f32),
            jax.ShapeDtypeStruct((slots * BLK, width), f32),
            jax.ShapeDtypeStruct((8, width), f32),
        ],
    )(tiles, q, ek, ev, lk, lk, lv, lv, g, keep, q_gain.reshape(1, head_size), k_gain.reshape(1, head_size))


def body(
    queries, keys, values, lyric_keys, lyric_values, q_gain, k_gain, cotangent, alignment, lyric_len
):
    head_size = q_gain.shape[0]
    model_width = queries.shape[2]
    head_count = model_width // head_size
    frames = queries.shape[1]
    lyric_local = lyric_keys.shape[1]
    seq_count = lax.axis_size("seq")
    border_rows = WIN * BLK
    window_extent = (2 * WIN + 1) * BLK
    score_scale = head_size ** (-0.5)
    total_frames = frames * seq_count
    first_frame = lax.axis_index("seq") * frames
    lyric_total = lyric_local * seq_count
    lyric_blocks = lyric_total // BLK
    masks = seq_masks(seq_count)

    lyric_pair = jnp.stack([lyric_keys[0], lyric_values[0]])
    lyric_all = gather_doubling(lyric_pair, "seq", masks[::-1])
    lyric_all = jnp.swapaxes(lyric_all, 0, 1).reshape(2, lyric_total, model_width)

    query_raw = queries[0]
    lyric_inv = norm_heads(lyric_keys[0], k_gain)[1]

    stacked = jnp.stack([keys[0], values[0]])
    extended = extended_2(stacked, (("seq", 1),), border_rows)
    key_raw = keys[0]
    key_inv = norm_heads(key_raw, k_gain)[1]
    length = lyric_len[0]

    position = first_frame - border_rows + jnp.arange(window_extent, dtype=jnp.int32)
    audio_mask = (position >= 0) & (position < total_frames)
    tile_ids = alignment[0, 0]
    tiles = jnp.maximum(tile_ids, 0)
    lyric_mask = jnp.concatenate(
        [(tile_ids[s] >= 0) & (tiles[s] * BLK + jnp.arange(BLK, dtype=jnp.int32) < length) for s in range(TILES)]
    )
    keep_mask = jnp.concatenate([audio_mask, lyric_mask], axis=0).astype(jnp.float32)[None]
    block_output, unnormed_query_gradient, ext_grad_key, ext_grad_val, slot_gk, slot_gv, gain_rows = attention_block(
        tiles,
        query_raw,
        extended[0],
        extended[1],
        lyric_all[0],
        lyric_all[1],
        cotangent[0],
        keep_mask,
        q_gain,
        k_gain,
        score_scale,
    )
    ext_grad_key = ext_grad_key.reshape(window_extent, head_count, head_size)
    ext_grad_val = ext_grad_val.reshape(window_extent, head_count, head_size)
    total_gains = sum_doubling(
        jnp.sum(gain_rows[:2].reshape(2, head_count, head_size), axis=1), ("seq", "song")
    )

    lyric_gk = slot_gk.reshape(TILES, BLK, head_count, head_size)
    lyric_gv = slot_gv.reshape(TILES, BLK, head_count, head_size)
    block_ids = jnp.arange(lyric_blocks, dtype=jnp.int32)
    pick = [(tile_ids[s] == block_ids)[:, None, None, None] for s in range(TILES)]
    part_gk = sum(jnp.where(pick[s], lyric_gk[s][None], 0.0) for s in range(TILES))
    part_gv = sum(jnp.where(pick[s], lyric_gv[s][None], 0.0) for s in range(TILES))

    parts = jnp.stack(
        [part_gk.reshape(seq_count, lyric_local, model_width), part_gv.reshape(seq_count, lyric_local, model_width)],
        axis=1,
    )
    summed = scatter_halving(parts, "seq", masks)
    summed_key = summed[0].reshape(lyric_local, head_count, head_size)
    summed_val = summed[1]

    own_grad_key = ext_grad_key[border_rows : border_rows + frames]
    own_grad_val = ext_grad_val[border_rows : border_rows + frames]
    rims = jnp.stack(
        [
            jnp.concatenate(
                [ext_grad_key[:border_rows], ext_grad_key[border_rows + frames :]], axis=0
            ).reshape(2 * border_rows, model_width),
            jnp.concatenate(
                [ext_grad_val[:border_rows], ext_grad_val[border_rows + frames :]], axis=0
            ).reshape(2 * border_rows, model_width),
        ]
    )
    received = extended_2(rims.astype(jnp.bfloat16), (("seq", 1),), border_rows).astype(rims.dtype)
    from_left = received[:, :border_rows].reshape(2, border_rows, head_count, head_size)
    from_right = received[:, 3 * border_rows :].reshape(2, border_rows, head_count, head_size)
    own_grad_key = (
        own_grad_key.at[:border_rows]
        .add(from_left[0])
        .at[frames - border_rows :]
        .add(from_right[0])
    )
    own_grad_val = (
        own_grad_val.at[:border_rows]
        .add(from_left[1])
        .at[frames - border_rows :]
        .add(from_right[1])
    )
    unnormed_key_gradient = norm_back(key_raw, key_inv, k_gain, own_grad_key)[0]
    unnormed_lyric_gradient = norm_back(lyric_keys[0], lyric_inv, k_gain, summed_key)[0]
    return (
        block_output.reshape(1, frames, model_width),
        unnormed_query_gradient[None],
        unnormed_key_gradient.astype(jnp.bfloat16)[None],
        own_grad_val.reshape(1, frames, model_width).astype(jnp.bfloat16),
        unnormed_lyric_gradient.astype(jnp.bfloat16)[None],
        summed_val.astype(jnp.bfloat16)[None],
        total_gains[0],
        total_gains[1],
    )


def solution(mesh):
    in_specs = (
        P("song", "seq", None),
        P("song", "seq", None),
        P("song", "seq", None),
        P("song", "seq", None),
        P("song", "seq", None),
        P(),
        P(),
        P("song", "seq", None),
        P("song", "seq", None),
        P("song"),
    )
    out_specs = (
        P("song", "seq", None),
        P("song", "seq", None),
        P("song", "seq", None),
        P("song", "seq", None),
        P("song", "seq", None),
        P("song", "seq", None),
        P(),
        P(),
    )
    return jax.shard_map(body, mesh=mesh, in_specs=in_specs, out_specs=out_specs, check_vma=False)
```

```python
import jax
import jax.numpy as jnp
from jax import lax
from jax.sharding import PartitionSpec as P
from jax.experimental import pallas as pl
from jax.experimental.pallas import tpu as pltpu

BLK = 128
WIN = 1
TILES = 2


NORM_EPS = 1e-06


def extended_2(block, sides, width):
    for axis, dim in sides:
        count = lax.axis_size(axis)
        forward = [(i, i + 1) for i in range(count - 1)]
        backward = [(target, source) for source, target in forward]
        low = lax.ppermute(
            lax.slice_in_dim(block, block.shape[dim] - width, None, axis=dim), axis, forward
        )
        high = lax.ppermute(lax.slice_in_dim(block, 0, width, axis=dim), axis, backward)
        block = jnp.concatenate([low, block, high], axis=dim)
    return block


def seq_masks(count):
    masks = []
    m = 1
    while m < count:
        masks.append(m)
        m *= 2
    return masks


def swap_with(x, axis, mask):
    count = lax.axis_size(axis)
    return lax.ppermute(x, axis, [(i, i ^ mask) for i in range(count)])


def gather_doubling(chunk, axis, order):
    idx = lax.axis_index(axis)
    buf = chunk[None]
    for mask in order:
        other = swap_with(buf, axis, mask)
        high = (idx & mask) != 0
        buf = jnp.where(high, jnp.concatenate([other, buf]), jnp.concatenate([buf, other]))
    steps = len(order)
    buf = buf.reshape((2,) * steps + chunk.shape)
    held = [order[steps - 1 - k] for k in range(steps)]
    perm = sorted(range(steps), key=lambda k: -held[k])
    buf = jnp.transpose(buf, perm + list(range(steps, buf.ndim)))
    return buf.reshape((2 ** steps,) + chunk.shape)


def scatter_halving(parts, axis, order, rider):
    idx = lax.axis_index(axis)
    steps = len(order)
    buf = parts.reshape(parts.shape[:1] + (2,) * steps + parts.shape[2:])
    held = sorted(order, reverse=True)
    for mask in order:
        a = held.index(mask) + 1
        high = ((idx & mask) != 0).astype(jnp.int32)
        keep = lax.dynamic_index_in_dim(buf, high, axis=a, keepdims=False)
        send = lax.dynamic_index_in_dim(buf, 1 - high, axis=a, keepdims=False)
        got, other = swap_with((send.astype(jnp.bfloat16), rider), axis, mask)
        buf = keep + got.astype(keep.dtype)
        rider = rider + other
        held.pop(a - 1)
    return buf, rider


def sum_doubling(x, axes):
    for axis in axes:
        for mask in seq_masks(lax.axis_size(axis)):
            x = x + swap_with(x, axis, mask)
    return x


def norm_heads(inputs, norm_gain):
    row_values = inputs.astype(jnp.float32).reshape(inputs.shape[0], -1, norm_gain.shape[0])
    inverse = lax.rsqrt(jnp.mean(row_values * row_values, axis=-1, keepdims=True) + NORM_EPS)
    return (row_values * inverse * norm_gain, inverse)


def norm_back(inputs, inverse, norm_gain, grad_out):
    row_values = inputs.astype(jnp.float32).reshape(grad_out.shape)
    scaled = grad_out * norm_gain
    grad_input = inverse * scaled - row_values * inverse * inverse * inverse * jnp.mean(
        scaled * row_values, axis=-1, keepdims=True
    )
    grad_gain = jnp.sum(grad_out * row_values * inverse, axis=(0, 1))
    return (grad_input.reshape(inputs.shape), grad_gain)


def block_pass(query_rows, key_rows, value_rows, keep_mask, grad_rows, score_scale):
    scores = (
        jnp.einsum("qhd,khd->hqk", query_rows, key_rows, preferred_element_type=jnp.float32)
        * score_scale
    )
    exp_scores = jnp.where(keep_mask[None, None, :], jnp.exp(scores), 0.0)
    totals = jnp.sum(exp_scores, axis=2)
    prob_full = exp_scores / totals[:, :, None]
    prob_low = prob_full.astype(jnp.bfloat16)
    block_output = jnp.einsum(
        "hqk,khd->qhd", prob_low, value_rows, preferred_element_type=jnp.float32
    ).astype(jnp.bfloat16)
    delta_rows = jnp.sum(grad_rows.astype(jnp.float32) * block_output.astype(jnp.float32), axis=2).T
    grad_prob = jnp.einsum(
        "qhd,khd->hqk", grad_rows, value_rows, preferred_element_type=jnp.float32
    )
    grad_score = (prob_full * (grad_prob - delta_rows[:, :, None])).astype(jnp.bfloat16)
    query_gradient = (
        jnp.einsum("hqk,khd->qhd", grad_score, key_rows, preferred_element_type=jnp.float32)
        * score_scale
    )
    grad_key = (
        jnp.einsum("hqk,qhd->khd", grad_score, query_rows, preferred_element_type=jnp.float32)
        * score_scale
    )
    value_gradient = jnp.einsum(
        "hqk,qhd->khd", prob_low, grad_rows, preferred_element_type=jnp.float32
    )
    return (block_output, query_gradient, grad_key, value_gradient)


def attention_kernel(
    tiles_ref, q_ref, ek_ref, ev_ref, lk0_ref, lk1_ref, lv0_ref, lv1_ref, g_ref, m_ref, qg_ref, kg_ref,
    o_ref, dqi_ref, dke_ref, dve_ref, part_ref, gain_ref, *, scale
):
    f32 = jnp.float32
    window = ek_ref.shape[0]
    q_gain = qg_ref[...]
    k_gain = kg_ref[...]

    def normed(x_ref, gain):
        x = x_ref[...].astype(f32)
        inv = lax.rsqrt(jnp.mean(x * x, axis=1, keepdims=True) + NORM_EPS)
        return x, inv, (x * inv * gain).astype(jnp.bfloat16)

    qx, qinv, q = normed(q_ref, q_gain)
    kx, kinv, kn = normed(ek_ref, k_gain)
    lx0, linv0, ln0 = normed(lk0_ref, k_gain)
    lx1, linv1, ln1 = normed(lk1_ref, k_gain)
    g = g_ref[...]
    k = jnp.concatenate([kn, ln0, ln1], axis=0)
    v = jnp.concatenate([ev_ref[...], lv0_ref[...], lv1_ref[...]], axis=0)
    keep = m_ref[...] > 0.0
    nt = (((1,), (1,)), ((), ()))
    tn = (((0,), (0,)), ((), ()))
    s = lax.dot_general(q, k, nt, preferred_element_type=f32) * scale
    e = jnp.where(keep, jnp.exp(s), 0.0)
    tot = jnp.sum(e, axis=1, keepdims=True)
    p = e / tot
    p_low = p.astype(jnp.bfloat16)
    o = jnp.dot(p_low, v, preferred_element_type=f32).astype(jnp.bfloat16)
    o_ref[...] = o
    delta = jnp.sum(g.astype(f32) * o.astype(f32), axis=1, keepdims=True)
    dp = lax.dot_general(g, v, nt, preferred_element_type=f32)
    ds = (p * (dp - delta)).astype(jnp.bfloat16)
    dq = jnp.dot(ds, k, preferred_element_type=f32) * scale
    dk = lax.dot_general(ds, q, tn, preferred_element_type=f32) * scale
    dv = lax.dot_general(p_low, g, tn, preferred_element_type=f32)
    scaled = dq * q_gain
    dqi_ref[...] = (
        qinv * scaled - qx * qinv * qinv * qinv * jnp.mean(scaled * qx, axis=1, keepdims=True)
    ).astype(jnp.bfloat16)
    dke_ref[...] = dk[:window]
    dve_ref[...] = dv[:window]
    for j in range(part_ref.shape[1] // BLK):
        for c, d in enumerate((dk, dv)):
            placed = jnp.zeros((BLK, d.shape[1]), f32)
            for s in range(tiles_ref.shape[0]):
                rows = d[window + s * BLK : window + (s + 1) * BLK]
                placed = placed + jnp.where(tiles_ref[s] == j, rows, 0.0)
            part_ref[c, j * BLK : (j + 1) * BLK, :] = placed
    gq = jnp.sum(dq * qx * qinv, axis=0, keepdims=True)
    gk = (
        jnp.sum(dk[:window] * kx * kinv, axis=0, keepdims=True)
        + jnp.sum(dk[window : window + BLK] * lx0 * linv0, axis=0, keepdims=True)
        + jnp.sum(dk[window + BLK :] * lx1 * linv1, axis=0, keepdims=True)
    )
    gain_ref[...] = jnp.concatenate([gq, gk, jnp.zeros((6, gq.shape[1]), f32)], axis=0)


def attention_block(tiles, q, ek, ev, lk, lv, g, keep, q_gain, k_gain, scale):
    lyric_rows = lk.shape[0]
    rows, width = q.shape
    head_size = q_gain.shape[0]
    window = ek.shape[0]
    slots = tiles.shape[0]
    heads = width // head_size
    f32 = jnp.float32

    def col(r):
        return pl.BlockSpec((r, head_size), lambda h, t: (0, h))

    def slot(s):
        return pl.BlockSpec((BLK, head_size), lambda h, t: (jnp.maximum(t[s], 0), h))

    whole = pl.BlockSpec((1, head_size), lambda h, t: (0, 0))
    grid_spec = pltpu.PrefetchScalarGridSpec(
        num_scalar_prefetch=1,
        grid=(heads,),
        in_specs=[col(rows), col(window), col(window), slot(0), slot(1), slot(0), slot(1), col(rows),
                  pl.BlockSpec((1, keep.shape[1]), lambda h, t: (0, 0)), whole, whole],
        out_specs=[col(rows), col(rows), col(window), col(window),
                   pl.BlockSpec((2, lyric_rows, head_size), lambda h, t: (0, 0, h)), col(8)],
    )
    return pl.pallas_call(
        lambda *refs: attention_kernel(*refs, scale=scale),
        grid_spec=grid_spec,
        out_shape=[
            jax.ShapeDtypeStruct((rows, width), jnp.bfloat16),
            jax.ShapeDtypeStruct((rows, width), jnp.bfloat16),
            jax.ShapeDtypeStruct((window, width), f32),
            jax.ShapeDtypeStruct((window, width), f32),
            jax.ShapeDtypeStruct((2, lyric_rows, width), f32),
            jax.ShapeDtypeStruct((8, width), f32),
        ],
    )(tiles, q, ek, ev, lk, lk, lv, lv, g, keep, q_gain.reshape(1, head_size), k_gain.reshape(1, head_size))


def body(
    queries, keys, values, lyric_keys, lyric_values, q_gain, k_gain, cotangent, alignment, lyric_len
):
    head_size = q_gain.shape[0]
    model_width = queries.shape[2]
    head_count = model_width // head_size
    frames = queries.shape[1]
    lyric_local = lyric_keys.shape[1]
    seq_count = lax.axis_size("seq")
    border_rows = WIN * BLK
    window_extent = (2 * WIN + 1) * BLK
    score_scale = head_size ** (-0.5)
    total_frames = frames * seq_count
    first_frame = lax.axis_index("seq") * frames
    lyric_total = lyric_local * seq_count
    lyric_blocks = lyric_total // BLK
    masks = seq_masks(seq_count)

    lyric_pair = jnp.stack([lyric_keys[0], lyric_values[0]])
    lyric_all = gather_doubling(lyric_pair, "seq", masks[::-1])
    lyric_all = jnp.swapaxes(lyric_all, 0, 1).reshape(2, lyric_total, model_width)

    query_raw = queries[0]
    lyric_inv = norm_heads(lyric_keys[0], k_gain)[1]

    stacked = jnp.stack([keys[0], values[0]])
    extended = extended_2(stacked, (("seq", 1),), border_rows)
    key_raw = keys[0]
    key_inv = norm_heads(key_raw, k_gain)[1]
    length = lyric_len[0]

    position = first_frame - border_rows + jnp.arange(window_extent, dtype=jnp.int32)
    audio_mask = (position >= 0) & (position < total_frames)
    tile_ids = alignment[0, 0]
    tiles = jnp.maximum(tile_ids, 0)
    lyric_mask = jnp.concatenate(
        [(tile_ids[s] >= 0) & (tiles[s] * BLK + jnp.arange(BLK, dtype=jnp.int32) < length) for s in range(TILES)]
    )
    keep_mask = jnp.concatenate([audio_mask, lyric_mask], axis=0).astype(jnp.float32)[None]
    block_output, unnormed_query_gradient, ext_grad_key, ext_grad_val, parts, gain_rows = attention_block(
        tile_ids,
        query_raw,
        extended[0],
        extended[1],
        lyric_all[0],
        lyric_all[1],
        cotangent[0],
        keep_mask,
        q_gain,
        k_gain,
        score_scale,
    )
    ext_grad_key = ext_grad_key.reshape(window_extent, head_count, head_size)
    ext_grad_val = ext_grad_val.reshape(window_extent, head_count, head_size)
    gains = jnp.sum(gain_rows[:2].reshape(2, head_count, head_size), axis=1)
    summed, gains = scatter_halving(parts.reshape(2, seq_count, lyric_local, model_width), "seq", masks, gains)
    total_gains = sum_doubling(gains, ("song",))
    summed_key = summed[0].reshape(lyric_local, head_count, head_size)
    summed_val = summed[1]

    own_grad_key = ext_grad_key[border_rows : border_rows + frames]
    own_grad_val = ext_grad_val[border_rows : border_rows + frames]
    rims = jnp.stack(
        [
            jnp.concatenate(
                [ext_grad_key[:border_rows], ext_grad_key[border_rows + frames :]], axis=0
            ).reshape(2 * border_rows, model_width),
            jnp.concatenate(
                [ext_grad_val[:border_rows], ext_grad_val[border_rows + frames :]], axis=0
            ).reshape(2 * border_rows, model_width),
        ]
    )
    received = extended_2(rims.astype(jnp.bfloat16), (("seq", 1),), border_rows).astype(rims.dtype)
    from_left = received[:, :border_rows].reshape(2, border_rows, head_count, head_size)
    from_right = received[:, 3 * border_rows :].reshape(2, border_rows, head_count, head_size)
    own_grad_key = (
        own_grad_key.at[:border_rows]
        .add(from_left[0])
        .at[frames - border_rows :]
        .add(from_right[0])
    )
    own_grad_val = (
        own_grad_val.at[:border_rows]
        .add(from_left[1])
        .at[frames - border_rows :]
        .add(from_right[1])
    )
    unnormed_key_gradient = norm_back(key_raw, key_inv, k_gain, own_grad_key)[0]
    unnormed_lyric_gradient = norm_back(lyric_keys[0], lyric_inv, k_gain, summed_key)[0]
    return (
        block_output.reshape(1, frames, model_width),
        unnormed_query_gradient[None],
        unnormed_key_gradient.astype(jnp.bfloat16)[None],
        own_grad_val.reshape(1, frames, model_width).astype(jnp.bfloat16),
        unnormed_lyric_gradient.astype(jnp.bfloat16)[None],
        summed_val.astype(jnp.bfloat16)[None],
        total_gains[0],
        total_gains[1],
    )


def solution(mesh):
    in_specs = (
        P("song", "seq", None),
        P("song", "seq", None),
        P("song", "seq", None),
        P("song", "seq", None),
        P("song", "seq", None),
        P(),
        P(),
        P("song", "seq", None),
        P("song", "seq", None),
        P("song"),
    )
    out_specs = (
        P("song", "seq", None),
        P("song", "seq", None),
        P("song", "seq", None),
        P("song", "seq", None),
        P("song", "seq", None),
        P("song", "seq", None),
        P(),
        P(),
    )
    return jax.shard_map(body, mesh=mesh, in_specs=in_specs, out_specs=out_specs, check_vma=False)
```

```python
import functools

import jax
import jax.numpy as jnp
from jax import lax
from jax.sharding import PartitionSpec as P
from jax.experimental import pallas as pl
from jax.experimental.pallas import tpu as pltpu

BLK = 128
WIN = 1
TILES = 2


NORM_EPS = 1e-06


def extended_2(block, sides, width):
    for axis, dim in sides:
        count = lax.axis_size(axis)
        forward = [(i, i + 1) for i in range(count - 1)]
        backward = [(target, source) for source, target in forward]
        low = lax.ppermute(
            lax.slice_in_dim(block, block.shape[dim] - width, None, axis=dim), axis, forward
        )
        high = lax.ppermute(lax.slice_in_dim(block, 0, width, axis=dim), axis, backward)
        block = jnp.concatenate([low, block, high], axis=dim)
    return block


def seq_masks(count):
    masks = []
    m = 1
    while m < count:
        masks.append(m)
        m *= 2
    return masks


def swap_with(x, axis, mask):
    count = lax.axis_size(axis)
    return lax.ppermute(x, axis, [(i, i ^ mask) for i in range(count)])


def flip_bit(h, mask):
    return h + mask - 2 * mask * ((h // mask) % 2)


def gather_kernel(masks, x_ref, out_ref, local_sem, send_sem, recv_sem):
    me = lax.axis_index("seq")
    song = lax.axis_index("song")
    mesh_ids = pl.DeviceIdType.MESH
    barrier = pltpu.get_barrier_semaphore()
    for m in masks:
        pl.semaphore_signal(barrier, inc=1, device_id=(song, flip_bit(me, m)), device_id_type=mesh_ids)
    pl.semaphore_wait(barrier, len(masks))
    own = pltpu.make_async_copy(x_ref, out_ref.at[me], local_sem.at[0])
    own.start()
    own.wait()
    held = [me]
    idx = 0
    for m in masks:
        partner = flip_bit(me, m)
        copies = []
        for h in held:
            c = pltpu.make_async_remote_copy(
                src_ref=out_ref.at[h],
                dst_ref=out_ref.at[h],
                send_sem=send_sem.at[idx],
                recv_sem=recv_sem.at[idx],
                device_id=(song, partner),
                device_id_type=mesh_ids,
            )
            c.start()
            copies.append(c)
            idx += 1
        for c in copies:
            c.wait()
        held = held + [flip_bit(h, m) for h in held]


def gather_chunks(x, count, masks):
    return pl.pallas_call(
        functools.partial(gather_kernel, masks),
        out_shape=jax.ShapeDtypeStruct((count,) + x.shape, x.dtype),
        in_specs=[pl.BlockSpec(memory_space=pl.ANY)],
        out_specs=pl.BlockSpec(memory_space=pl.ANY),
        scratch_shapes=[
            pltpu.SemaphoreType.DMA((1,)),
            pltpu.SemaphoreType.DMA((count - 1,)),
            pltpu.SemaphoreType.DMA((count - 1,)),
        ],
        compiler_params=pltpu.CompilerParams(collective_id=0, has_side_effects=True),
    )(x)


def scatter_halving(parts, axis, order, rider):
    idx = lax.axis_index(axis)
    steps = len(order)
    buf = parts.reshape(parts.shape[:1] + (2,) * steps + parts.shape[2:])
    held = sorted(order, reverse=True)
    for mask in order:
        a = held.index(mask) + 1
        high = ((idx & mask) != 0).astype(jnp.int32)
        keep = lax.dynamic_index_in_dim(buf, high, axis=a, keepdims=False)
        send = lax.dynamic_index_in_dim(buf, 1 - high, axis=a, keepdims=False)
        got, other = swap_with((send.astype(jnp.bfloat16), rider), axis, mask)
        buf = keep + got.astype(keep.dtype)
        rider = rider + other
        held.pop(a - 1)
    return buf, rider


def sum_doubling(x, axes):
    for axis in axes:
        for mask in seq_masks(lax.axis_size(axis)):
            x = x + swap_with(x, axis, mask)
    return x


def norm_heads(inputs, norm_gain):
    row_values = inputs.astype(jnp.float32).reshape(inputs.shape[0], -1, norm_gain.shape[0])
    inverse = lax.rsqrt(jnp.mean(row_values * row_values, axis=-1, keepdims=True) + NORM_EPS)
    return (row_values * inverse * norm_gain, inverse)


def norm_back(inputs, inverse, norm_gain, grad_out):
    row_values = inputs.astype(jnp.float32).reshape(grad_out.shape)
    scaled = grad_out * norm_gain
    grad_input = inverse * scaled - row_values * inverse * inverse * inverse * jnp.mean(
        scaled * row_values, axis=-1, keepdims=True
    )
    grad_gain = jnp.sum(grad_out * row_values * inverse, axis=(0, 1))
    return (grad_input.reshape(inputs.shape), grad_gain)


def block_pass(query_rows, key_rows, value_rows, keep_mask, grad_rows, score_scale):
    scores = (
        jnp.einsum("qhd,khd->hqk", query_rows, key_rows, preferred_element_type=jnp.float32)
        * score_scale
    )
    exp_scores = jnp.where(keep_mask[None, None, :], jnp.exp(scores), 0.0)
    totals = jnp.sum(exp_scores, axis=2)
    prob_full = exp_scores / totals[:, :, None]
    prob_low = prob_full.astype(jnp.bfloat16)
    block_output = jnp.einsum(
        "hqk,khd->qhd", prob_low, value_rows, preferred_element_type=jnp.float32
    ).astype(jnp.bfloat16)
    delta_rows = jnp.sum(grad_rows.astype(jnp.float32) * block_output.astype(jnp.float32), axis=2).T
    grad_prob = jnp.einsum(
        "qhd,khd->hqk", grad_rows, value_rows, preferred_element_type=jnp.float32
    )
    grad_score = (prob_full * (grad_prob - delta_rows[:, :, None])).astype(jnp.bfloat16)
    query_gradient = (
        jnp.einsum("hqk,khd->qhd", grad_score, key_rows, preferred_element_type=jnp.float32)
        * score_scale
    )
    grad_key = (
        jnp.einsum("hqk,qhd->khd", grad_score, query_rows, preferred_element_type=jnp.float32)
        * score_scale
    )
    value_gradient = jnp.einsum(
        "hqk,qhd->khd", prob_low, grad_rows, preferred_element_type=jnp.float32
    )
    return (block_output, query_gradient, grad_key, value_gradient)


def attention_kernel(
    tiles_ref, q_ref, ek_ref, ev_ref, lk0_ref, lk1_ref, lv0_ref, lv1_ref, g_ref, m_ref, qg_ref, kg_ref,
    o_ref, dqi_ref, dke_ref, dve_ref, part_ref, gain_ref, *, scale
):
    f32 = jnp.float32
    window = ek_ref.shape[0]
    q_gain = qg_ref[...]
    k_gain = kg_ref[...]

    def normed(x_ref, gain):
        x = x_ref[...].astype(f32)
        inv = lax.rsqrt(jnp.mean(x * x, axis=1, keepdims=True) + NORM_EPS)
        return x, inv, (x * inv * gain).astype(jnp.bfloat16)

    qx, qinv, q = normed(q_ref, q_gain)
    kx, kinv, kn = normed(ek_ref, k_gain)
    lx0, linv0, ln0 = normed(lk0_ref, k_gain)
    lx1, linv1, ln1 = normed(lk1_ref, k_gain)
    g = g_ref[...]
    k = jnp.concatenate([kn, ln0, ln1], axis=0)
    v = jnp.concatenate([ev_ref[...], lv0_ref[...], lv1_ref[...]], axis=0)
    keep = m_ref[...] > 0.0
    nt = (((1,), (1,)), ((), ()))
    tn = (((0,), (0,)), ((), ()))
    s = lax.dot_general(q, k, nt, preferred_element_type=f32) * scale
    e = jnp.where(keep, jnp.exp(s), 0.0)
    tot = jnp.sum(e, axis=1, keepdims=True)
    p = e / tot
    p_low = p.astype(jnp.bfloat16)
    o = jnp.dot(p_low, v, preferred_element_type=f32).astype(jnp.bfloat16)
    o_ref[...] = o
    delta = jnp.sum(g.astype(f32) * o.astype(f32), axis=1, keepdims=True)
    dp = lax.dot_general(g, v, nt, preferred_element_type=f32)
    ds = (p * (dp - delta)).astype(jnp.bfloat16)
    dq = jnp.dot(ds, k, preferred_element_type=f32) * scale
    dk = lax.dot_general(ds, q, tn, preferred_element_type=f32) * scale
    dv = lax.dot_general(p_low, g, tn, preferred_element_type=f32)
    scaled = dq * q_gain
    dqi_ref[...] = (
        qinv * scaled - qx * qinv * qinv * qinv * jnp.mean(scaled * qx, axis=1, keepdims=True)
    ).astype(jnp.bfloat16)
    dke_ref[...] = dk[:window]
    dve_ref[...] = dv[:window]
    for j in range(part_ref.shape[1] // BLK):
        for c, d in enumerate((dk, dv)):
            placed = jnp.zeros((BLK, d.shape[1]), f32)
            for s in range(tiles_ref.shape[0]):
                rows = d[window + s * BLK : window + (s + 1) * BLK]
                placed = placed + jnp.where(tiles_ref[s] == j, rows, 0.0)
            part_ref[c, j * BLK : (j + 1) * BLK, :] = placed
    gq = jnp.sum(dq * qx * qinv, axis=0, keepdims=True)
    gk = (
        jnp.sum(dk[:window] * kx * kinv, axis=0, keepdims=True)
        + jnp.sum(dk[window : window + BLK] * lx0 * linv0, axis=0, keepdims=True)
        + jnp.sum(dk[window + BLK :] * lx1 * linv1, axis=0, keepdims=True)
    )
    gain_ref[...] = jnp.concatenate([gq, gk, jnp.zeros((6, gq.shape[1]), f32)], axis=0)


def attention_block(tiles, q, ek, ev, lk, lv, g, keep, q_gain, k_gain, scale):
    lyric_rows = lk.shape[0]
    rows, width = q.shape
    head_size = q_gain.shape[0]
    window = ek.shape[0]
    slots = tiles.shape[0]
    heads = width // head_size
    f32 = jnp.float32

    def col(r):
        return pl.BlockSpec((r, head_size), lambda h, t: (0, h))

    def slot(s):
        return pl.BlockSpec((BLK, head_size), lambda h, t: (jnp.maximum(t[s], 0), h))

    whole = pl.BlockSpec((1, head_size), lambda h, t: (0, 0))
    grid_spec = pltpu.PrefetchScalarGridSpec(
        num_scalar_prefetch=1,
        grid=(heads,),
        in_specs=[col(rows), col(window), col(window), slot(0), slot(1), slot(0), slot(1), col(rows),
                  pl.BlockSpec((1, keep.shape[1]), lambda h, t: (0, 0)), whole, whole],
        out_specs=[col(rows), col(rows), col(window), col(window),
                   pl.BlockSpec((2, lyric_rows, head_size), lambda h, t: (0, 0, h)), col(8)],
    )
    return pl.pallas_call(
        lambda *refs: attention_kernel(*refs, scale=scale),
        grid_spec=grid_spec,
        out_shape=[
            jax.ShapeDtypeStruct((rows, width), jnp.bfloat16),
            jax.ShapeDtypeStruct((rows, width), jnp.bfloat16),
            jax.ShapeDtypeStruct((window, width), f32),
            jax.ShapeDtypeStruct((window, width), f32),
            jax.ShapeDtypeStruct((2, lyric_rows, width), f32),
            jax.ShapeDtypeStruct((8, width), f32),
        ],
    )(tiles, q, ek, ev, lk, lk, lv, lv, g, keep, q_gain.reshape(1, head_size), k_gain.reshape(1, head_size))


def body(
    queries, keys, values, lyric_keys, lyric_values, q_gain, k_gain, cotangent, alignment, lyric_len
):
    head_size = q_gain.shape[0]
    model_width = queries.shape[2]
    head_count = model_width // head_size
    frames = queries.shape[1]
    lyric_local = lyric_keys.shape[1]
    seq_count = lax.axis_size("seq")
    border_rows = WIN * BLK
    window_extent = (2 * WIN + 1) * BLK
    score_scale = head_size ** (-0.5)
    total_frames = frames * seq_count
    first_frame = lax.axis_index("seq") * frames
    lyric_total = lyric_local * seq_count
    lyric_blocks = lyric_total // BLK
    masks = seq_masks(seq_count)

    lyric_pair = jnp.stack([lyric_keys[0], lyric_values[0]])
    lyric_all = gather_chunks(lyric_pair, seq_count, masks[::-1])
    lyric_all = jnp.swapaxes(lyric_all, 0, 1).reshape(2, lyric_total, model_width)

    query_raw = queries[0]
    lyric_inv = norm_heads(lyric_keys[0], k_gain)[1]

    stacked = jnp.stack([keys[0], values[0]])
    extended = extended_2(stacked, (("seq", 1),), border_rows)
    key_raw = keys[0]
    key_inv = norm_heads(key_raw, k_gain)[1]
    length = lyric_len[0]

    position = first_frame - border_rows + jnp.arange(window_extent, dtype=jnp.int32)
    audio_mask = (position >= 0) & (position < total_frames)
    tile_ids = alignment[0, 0]
    tiles = jnp.maximum(tile_ids, 0)
    lyric_mask = jnp.concatenate(
        [(tile_ids[s] >= 0) & (tiles[s] * BLK + jnp.arange(BLK, dtype=jnp.int32) < length) for s in range(TILES)]
    )
    keep_mask = jnp.concatenate([audio_mask, lyric_mask], axis=0).astype(jnp.float32)[None]
    block_output, unnormed_query_gradient, ext_grad_key, ext_grad_val, parts, gain_rows = attention_block(
        tile_ids,
        query_raw,
        extended[0],
        extended[1],
        lyric_all[0],
        lyric_all[1],
        cotangent[0],
        keep_mask,
        q_gain,
        k_gain,
        score_scale,
    )
    ext_grad_key = ext_grad_key.reshape(window_extent, head_count, head_size)
    ext_grad_val = ext_grad_val.reshape(window_extent, head_count, head_size)
    gains = jnp.sum(gain_rows[:2].reshape(2, head_count, head_size), axis=1)
    summed, gains = scatter_halving(parts.reshape(2, seq_count, lyric_local, model_width), "seq", masks, gains)
    total_gains = sum_doubling(gains, ("song",))
    summed_key = summed[0].reshape(lyric_local, head_count, head_size)
    summed_val = summed[1]

    own_grad_key = ext_grad_key[border_rows : border_rows + frames]
    own_grad_val = ext_grad_val[border_rows : border_rows + frames]
    rims = jnp.stack(
        [
            jnp.concatenate(
                [ext_grad_key[:border_rows], ext_grad_key[border_rows + frames :]], axis=0
            ).reshape(2 * border_rows, model_width),
            jnp.concatenate(
                [ext_grad_val[:border_rows], ext_grad_val[border_rows + frames :]], axis=0
            ).reshape(2 * border_rows, model_width),
        ]
    )
    received = extended_2(rims.astype(jnp.bfloat16), (("seq", 1),), border_rows).astype(rims.dtype)
    from_left = received[:, :border_rows].reshape(2, border_rows, head_count, head_size)
    from_right = received[:, 3 * border_rows :].reshape(2, border_rows, head_count, head_size)
    own_grad_key = (
        own_grad_key.at[:border_rows]
        .add(from_left[0])
        .at[frames - border_rows :]
        .add(from_right[0])
    )
    own_grad_val = (
        own_grad_val.at[:border_rows]
        .add(from_left[1])
        .at[frames - border_rows :]
        .add(from_right[1])
    )
    unnormed_key_gradient = norm_back(key_raw, key_inv, k_gain, own_grad_key)[0]
    unnormed_lyric_gradient = norm_back(lyric_keys[0], lyric_inv, k_gain, summed_key)[0]
    return (
        block_output.reshape(1, frames, model_width),
        unnormed_query_gradient[None],
        unnormed_key_gradient.astype(jnp.bfloat16)[None],
        own_grad_val.reshape(1, frames, model_width).astype(jnp.bfloat16),
        unnormed_lyric_gradient.astype(jnp.bfloat16)[None],
        summed_val.astype(jnp.bfloat16)[None],
        total_gains[0],
        total_gains[1],
    )


def solution(mesh):
    in_specs = (
        P("song", "seq", None),
        P("song", "seq", None),
        P("song", "seq", None),
        P("song", "seq", None),
        P("song", "seq", None),
        P(),
        P(),
        P("song", "seq", None),
        P("song", "seq", None),
        P("song"),
    )
    out_specs = (
        P("song", "seq", None),
        P("song", "seq", None),
        P("song", "seq", None),
        P("song", "seq", None),
        P("song", "seq", None),
        P("song", "seq", None),
        P(),
        P(),
    )
    return jax.shard_map(body, mesh=mesh, in_specs=in_specs, out_specs=out_specs, check_vma=False)
```

```python
import functools

import jax
import jax.numpy as jnp
from jax import lax
from jax.sharding import PartitionSpec as P
from jax.experimental import pallas as pl
from jax.experimental.pallas import tpu as pltpu

BLK = 128
WIN = 1
TILES = 2


NORM_EPS = 1e-06


def extended_2(block, sides, width):
    for axis, dim in sides:
        count = lax.axis_size(axis)
        forward = [(i, i + 1) for i in range(count - 1)]
        backward = [(target, source) for source, target in forward]
        low = lax.ppermute(
            lax.slice_in_dim(block, block.shape[dim] - width, None, axis=dim), axis, forward
        )
        high = lax.ppermute(lax.slice_in_dim(block, 0, width, axis=dim), axis, backward)
        block = jnp.concatenate([low, block, high], axis=dim)
    return block


def seq_masks(count):
    masks = []
    m = 1
    while m < count:
        masks.append(m)
        m *= 2
    return masks


def swap_with(x, axis, mask):
    count = lax.axis_size(axis)
    return lax.ppermute(x, axis, [(i, i ^ mask) for i in range(count)])


def flip_bit(h, mask):
    return h + mask - 2 * mask * ((h // mask) % 2)


def gather_kernel(masks, x_ref, out_ref, local_sem, send_sem, recv_sem):
    me = lax.axis_index("seq")
    song = lax.axis_index("song")
    steps = len(masks)
    slot = sum(((me // m) % 2) * (2 ** k) for k, m in enumerate(masks))
    mesh_ids = pl.DeviceIdType.MESH
    barrier = pltpu.get_barrier_semaphore()
    for m in masks:
        pl.semaphore_signal(barrier, inc=1, device_id=(song, flip_bit(me, m)), device_id_type=mesh_ids)
    pl.semaphore_wait(barrier, steps)
    own = pltpu.make_async_copy(x_ref, out_ref.at[slot], local_sem.at[0])
    own.start()
    own.wait()
    for k, m in enumerate(masks):
        size = 2 ** k
        base = (slot // size) * size
        c = pltpu.make_async_remote_copy(
            src_ref=out_ref.at[pl.ds(base, size)],
            dst_ref=out_ref.at[pl.ds(base, size)],
            send_sem=send_sem.at[k],
            recv_sem=recv_sem.at[k],
            device_id=(song, flip_bit(me, m)),
            device_id_type=mesh_ids,
        )
        c.start()
        c.wait()


def gather_chunks(x, count, masks):
    return pl.pallas_call(
        functools.partial(gather_kernel, masks),
        out_shape=jax.ShapeDtypeStruct((count,) + x.shape, x.dtype),
        in_specs=[pl.BlockSpec(memory_space=pl.ANY)],
        out_specs=pl.BlockSpec(memory_space=pl.ANY),
        scratch_shapes=[
            pltpu.SemaphoreType.DMA((1,)),
            pltpu.SemaphoreType.DMA((len(masks),)),
            pltpu.SemaphoreType.DMA((len(masks),)),
        ],
        compiler_params=pltpu.CompilerParams(collective_id=0, has_side_effects=True),
    )(x)


def scatter_halving(parts, axis, order, rider):
    idx = lax.axis_index(axis)
    steps = len(order)
    buf = parts.reshape(parts.shape[:1] + (2,) * steps + parts.shape[2:])
    held = sorted(order, reverse=True)
    for mask in order:
        a = held.index(mask) + 1
        high = ((idx & mask) != 0).astype(jnp.int32)
        keep = lax.dynamic_index_in_dim(buf, high, axis=a, keepdims=False)
        send = lax.dynamic_index_in_dim(buf, 1 - high, axis=a, keepdims=False)
        got, other = swap_with((send.astype(jnp.bfloat16), rider), axis, mask)
        buf = keep + got.astype(keep.dtype)
        rider = rider + other
        held.pop(a - 1)
    return buf, rider


def sum_doubling(x, axes):
    for axis in axes:
        for mask in seq_masks(lax.axis_size(axis)):
            x = x + swap_with(x, axis, mask)
    return x


def norm_heads(inputs, norm_gain):
    row_values = inputs.astype(jnp.float32).reshape(inputs.shape[0], -1, norm_gain.shape[0])
    inverse = lax.rsqrt(jnp.mean(row_values * row_values, axis=-1, keepdims=True) + NORM_EPS)
    return (row_values * inverse * norm_gain, inverse)


def norm_back(inputs, inverse, norm_gain, grad_out):
    row_values = inputs.astype(jnp.float32).reshape(grad_out.shape)
    scaled = grad_out * norm_gain
    grad_input = inverse * scaled - row_values * inverse * inverse * inverse * jnp.mean(
        scaled * row_values, axis=-1, keepdims=True
    )
    grad_gain = jnp.sum(grad_out * row_values * inverse, axis=(0, 1))
    return (grad_input.reshape(inputs.shape), grad_gain)


def block_pass(query_rows, key_rows, value_rows, keep_mask, grad_rows, score_scale):
    scores = (
        jnp.einsum("qhd,khd->hqk", query_rows, key_rows, preferred_element_type=jnp.float32)
        * score_scale
    )
    exp_scores = jnp.where(keep_mask[None, None, :], jnp.exp(scores), 0.0)
    totals = jnp.sum(exp_scores, axis=2)
    prob_full = exp_scores / totals[:, :, None]
    prob_low = prob_full.astype(jnp.bfloat16)
    block_output = jnp.einsum(
        "hqk,khd->qhd", prob_low, value_rows, preferred_element_type=jnp.float32
    ).astype(jnp.bfloat16)
    delta_rows = jnp.sum(grad_rows.astype(jnp.float32) * block_output.astype(jnp.float32), axis=2).T
    grad_prob = jnp.einsum(
        "qhd,khd->hqk", grad_rows, value_rows, preferred_element_type=jnp.float32
    )
    grad_score = (prob_full * (grad_prob - delta_rows[:, :, None])).astype(jnp.bfloat16)
    query_gradient = (
        jnp.einsum("hqk,khd->qhd", grad_score, key_rows, preferred_element_type=jnp.float32)
        * score_scale
    )
    grad_key = (
        jnp.einsum("hqk,qhd->khd", grad_score, query_rows, preferred_element_type=jnp.float32)
        * score_scale
    )
    value_gradient = jnp.einsum(
        "hqk,qhd->khd", prob_low, grad_rows, preferred_element_type=jnp.float32
    )
    return (block_output, query_gradient, grad_key, value_gradient)


def attention_kernel(
    tiles_ref, q_ref, ek_ref, ev_ref, lk0_ref, lk1_ref, lv0_ref, lv1_ref, g_ref, m_ref, qg_ref, kg_ref,
    o_ref, dqi_ref, dke_ref, dve_ref, part_ref, gain_ref, *, scale
):
    f32 = jnp.float32
    window = ek_ref.shape[0]
    q_gain = qg_ref[...]
    k_gain = kg_ref[...]

    def normed(x_ref, gain):
        x = x_ref[...].astype(f32)
        inv = lax.rsqrt(jnp.mean(x * x, axis=1, keepdims=True) + NORM_EPS)
        return x, inv, (x * inv * gain).astype(jnp.bfloat16)

    qx, qinv, q = normed(q_ref, q_gain)
    kx, kinv, kn = normed(ek_ref, k_gain)
    lx0, linv0, ln0 = normed(lk0_ref, k_gain)
    lx1, linv1, ln1 = normed(lk1_ref, k_gain)
    g = g_ref[...]
    k = jnp.concatenate([kn, ln0, ln1], axis=0)
    v = jnp.concatenate([ev_ref[...], lv0_ref[...], lv1_ref[...]], axis=0)
    keep = m_ref[...] > 0.0
    nt = (((1,), (1,)), ((), ()))
    tn = (((0,), (0,)), ((), ()))
    s = lax.dot_general(q, k, nt, preferred_element_type=f32) * scale
    e = jnp.where(keep, jnp.exp(s), 0.0)
    tot = jnp.sum(e, axis=1, keepdims=True)
    p = e / tot
    p_low = p.astype(jnp.bfloat16)
    o = jnp.dot(p_low, v, preferred_element_type=f32).astype(jnp.bfloat16)
    o_ref[...] = o
    delta = jnp.sum(g.astype(f32) * o.astype(f32), axis=1, keepdims=True)
    dp = lax.dot_general(g, v, nt, preferred_element_type=f32)
    ds = (p * (dp - delta)).astype(jnp.bfloat16)
    dq = jnp.dot(ds, k, preferred_element_type=f32) * scale
    dk = lax.dot_general(ds, q, tn, preferred_element_type=f32) * scale
    dv = lax.dot_general(p_low, g, tn, preferred_element_type=f32)
    scaled = dq * q_gain
    dqi_ref[...] = (
        qinv * scaled - qx * qinv * qinv * qinv * jnp.mean(scaled * qx, axis=1, keepdims=True)
    ).astype(jnp.bfloat16)
    dke_ref[...] = dk[:window]
    dve_ref[...] = dv[:window]
    for j in range(part_ref.shape[1] // BLK):
        for c, d in enumerate((dk, dv)):
            placed = jnp.zeros((BLK, d.shape[1]), f32)
            for s in range(tiles_ref.shape[0]):
                rows = d[window + s * BLK : window + (s + 1) * BLK]
                placed = placed + jnp.where(tiles_ref[s] == j, rows, 0.0)
            part_ref[c, j * BLK : (j + 1) * BLK, :] = placed
    gq = jnp.sum(dq * qx * qinv, axis=0, keepdims=True)
    gk = (
        jnp.sum(dk[:window] * kx * kinv, axis=0, keepdims=True)
        + jnp.sum(dk[window : window + BLK] * lx0 * linv0, axis=0, keepdims=True)
        + jnp.sum(dk[window + BLK :] * lx1 * linv1, axis=0, keepdims=True)
    )
    gain_ref[...] = jnp.concatenate([gq, gk, jnp.zeros((6, gq.shape[1]), f32)], axis=0)


def attention_block(tiles, q, ek, ev, lk, lv, g, keep, q_gain, k_gain, scale):
    lyric_rows = lk.shape[0]
    rows, width = q.shape
    head_size = q_gain.shape[0]
    window = ek.shape[0]
    slots = tiles.shape[0]
    heads = width // head_size
    f32 = jnp.float32

    def col(r):
        return pl.BlockSpec((r, head_size), lambda h, t: (0, h))

    def slot(s):
        return pl.BlockSpec((BLK, head_size), lambda h, t: (jnp.maximum(t[s], 0), h))

    whole = pl.BlockSpec((1, head_size), lambda h, t: (0, 0))
    grid_spec = pltpu.PrefetchScalarGridSpec(
        num_scalar_prefetch=1,
        grid=(heads,),
        in_specs=[col(rows), col(window), col(window), slot(0), slot(1), slot(0), slot(1), col(rows),
                  pl.BlockSpec((1, keep.shape[1]), lambda h, t: (0, 0)), whole, whole],
        out_specs=[col(rows), col(rows), col(window), col(window),
                   pl.BlockSpec((2, lyric_rows, head_size), lambda h, t: (0, 0, h)), col(8)],
    )
    return pl.pallas_call(
        lambda *refs: attention_kernel(*refs, scale=scale),
        grid_spec=grid_spec,
        out_shape=[
            jax.ShapeDtypeStruct((rows, width), jnp.bfloat16),
            jax.ShapeDtypeStruct((rows, width), jnp.bfloat16),
            jax.ShapeDtypeStruct((window, width), f32),
            jax.ShapeDtypeStruct((window, width), f32),
            jax.ShapeDtypeStruct((2, lyric_rows, width), f32),
            jax.ShapeDtypeStruct((8, width), f32),
        ],
    )(tiles, q, ek, ev, lk, lk, lv, lv, g, keep, q_gain.reshape(1, head_size), k_gain.reshape(1, head_size))


def body(
    queries, keys, values, lyric_keys, lyric_values, q_gain, k_gain, cotangent, alignment, lyric_len
):
    head_size = q_gain.shape[0]
    model_width = queries.shape[2]
    head_count = model_width // head_size
    frames = queries.shape[1]
    lyric_local = lyric_keys.shape[1]
    seq_count = lax.axis_size("seq")
    border_rows = WIN * BLK
    window_extent = (2 * WIN + 1) * BLK
    score_scale = head_size ** (-0.5)
    total_frames = frames * seq_count
    first_frame = lax.axis_index("seq") * frames
    lyric_total = lyric_local * seq_count
    lyric_blocks = lyric_total // BLK
    masks = seq_masks(seq_count)

    lyric_pair = jnp.stack([lyric_keys[0], lyric_values[0]])
    steps = len(masks)
    lyric_all = gather_chunks(lyric_pair, seq_count, masks[::-1])
    lyric_all = lyric_all.reshape((2,) * steps + lyric_pair.shape)
    lyric_all = jnp.transpose(lyric_all, (steps,) + tuple(range(steps))[::-1] + (steps + 1, steps + 2))
    lyric_all = lyric_all.reshape(2, lyric_total, model_width)

    query_raw = queries[0]
    lyric_inv = norm_heads(lyric_keys[0], k_gain)[1]

    stacked = jnp.stack([keys[0], values[0]])
    extended = extended_2(stacked, (("seq", 1),), border_rows)
    key_raw = keys[0]
    key_inv = norm_heads(key_raw, k_gain)[1]
    length = lyric_len[0]

    position = first_frame - border_rows + jnp.arange(window_extent, dtype=jnp.int32)
    audio_mask = (position >= 0) & (position < total_frames)
    tile_ids = alignment[0, 0]
    tiles = jnp.maximum(tile_ids, 0)
    lyric_mask = jnp.concatenate(
        [(tile_ids[s] >= 0) & (tiles[s] * BLK + jnp.arange(BLK, dtype=jnp.int32) < length) for s in range(TILES)]
    )
    keep_mask = jnp.concatenate([audio_mask, lyric_mask], axis=0).astype(jnp.float32)[None]
    block_output, unnormed_query_gradient, ext_grad_key, ext_grad_val, parts, gain_rows = attention_block(
        tile_ids,
        query_raw,
        extended[0],
        extended[1],
        lyric_all[0],
        lyric_all[1],
        cotangent[0],
        keep_mask,
        q_gain,
        k_gain,
        score_scale,
    )
    ext_grad_key = ext_grad_key.reshape(window_extent, head_count, head_size)
    ext_grad_val = ext_grad_val.reshape(window_extent, head_count, head_size)
    gains = jnp.sum(gain_rows[:2].reshape(2, head_count, head_size), axis=1)
    summed, gains = scatter_halving(parts.reshape(2, seq_count, lyric_local, model_width), "seq", masks, gains)
    total_gains = sum_doubling(gains, ("song",))
    summed_key = summed[0].reshape(lyric_local, head_count, head_size)
    summed_val = summed[1]

    own_grad_key = ext_grad_key[border_rows : border_rows + frames]
    own_grad_val = ext_grad_val[border_rows : border_rows + frames]
    rims = jnp.stack(
        [
            jnp.concatenate(
                [ext_grad_key[:border_rows], ext_grad_key[border_rows + frames :]], axis=0
            ).reshape(2 * border_rows, model_width),
            jnp.concatenate(
                [ext_grad_val[:border_rows], ext_grad_val[border_rows + frames :]], axis=0
            ).reshape(2 * border_rows, model_width),
        ]
    )
    received = extended_2(rims.astype(jnp.bfloat16), (("seq", 1),), border_rows).astype(rims.dtype)
    from_left = received[:, :border_rows].reshape(2, border_rows, head_count, head_size)
    from_right = received[:, 3 * border_rows :].reshape(2, border_rows, head_count, head_size)
    own_grad_key = (
        own_grad_key.at[:border_rows]
        .add(from_left[0])
        .at[frames - border_rows :]
        .add(from_right[0])
    )
    own_grad_val = (
        own_grad_val.at[:border_rows]
        .add(from_left[1])
        .at[frames - border_rows :]
        .add(from_right[1])
    )
    unnormed_key_gradient = norm_back(key_raw, key_inv, k_gain, own_grad_key)[0]
    unnormed_lyric_gradient = norm_back(lyric_keys[0], lyric_inv, k_gain, summed_key)[0]
    return (
        block_output.reshape(1, frames, model_width),
        unnormed_query_gradient[None],
        unnormed_key_gradient.astype(jnp.bfloat16)[None],
        own_grad_val.reshape(1, frames, model_width).astype(jnp.bfloat16),
        unnormed_lyric_gradient.astype(jnp.bfloat16)[None],
        summed_val.astype(jnp.bfloat16)[None],
        total_gains[0],
        total_gains[1],
    )


def solution(mesh):
    in_specs = (
        P("song", "seq", None),
        P("song", "seq", None),
        P("song", "seq", None),
        P("song", "seq", None),
        P("song", "seq", None),
        P(),
        P(),
        P("song", "seq", None),
        P("song", "seq", None),
        P("song"),
    )
    out_specs = (
        P("song", "seq", None),
        P("song", "seq", None),
        P("song", "seq", None),
        P("song", "seq", None),
        P("song", "seq", None),
        P("song", "seq", None),
        P(),
        P(),
    )
    return jax.shard_map(body, mesh=mesh, in_specs=in_specs, out_specs=out_specs, check_vma=False)
```

```python
import jax
import jax.numpy as jnp
from jax import lax
from jax.sharding import PartitionSpec as P
from jax.experimental import pallas as pl
from jax.experimental.pallas import tpu as pltpu

BLK = 128
WIN = 1
TILES = 2


NORM_EPS = 1e-06


def extended_2(block, sides, width):
    for axis, dim in sides:
        count = lax.axis_size(axis)
        forward = [(i, i + 1) for i in range(count - 1)]
        backward = [(target, source) for source, target in forward]
        low = lax.ppermute(
            lax.slice_in_dim(block, block.shape[dim] - width, None, axis=dim), axis, forward
        )
        high = lax.ppermute(lax.slice_in_dim(block, 0, width, axis=dim), axis, backward)
        block = jnp.concatenate([low, block, high], axis=dim)
    return block


def seq_masks(count):
    masks = []
    m = 1
    while m < count:
        masks.append(m)
        m *= 2
    return masks


def swap_with(x, axis, mask):
    count = lax.axis_size(axis)
    return lax.ppermute(x, axis, [(i, i ^ mask) for i in range(count)])


def gather_doubling(chunk, axis, order):
    idx = lax.axis_index(axis)
    buf = chunk[None]
    for mask in order:
        other = swap_with(buf, axis, mask)
        high = (idx & mask) != 0
        buf = jnp.where(high, jnp.concatenate([other, buf]), jnp.concatenate([buf, other]))
    steps = len(order)
    buf = buf.reshape((2,) * steps + chunk.shape)
    held = [order[steps - 1 - k] for k in range(steps)]
    perm = sorted(range(steps), key=lambda k: -held[k])
    buf = jnp.transpose(buf, perm + list(range(steps, buf.ndim)))
    return buf.reshape((2 ** steps,) + chunk.shape)


def scatter_halving(parts, axis, order):
    idx = lax.axis_index(axis)
    steps = len(order)
    buf = parts.reshape((2,) * steps + parts.shape[1:])
    held = sorted(order, reverse=True)
    for mask in order:
        a = held.index(mask)
        high = ((idx & mask) != 0).astype(jnp.int32)
        keep = lax.dynamic_index_in_dim(buf, high, axis=a, keepdims=False)
        send = lax.dynamic_index_in_dim(buf, 1 - high, axis=a, keepdims=False)
        buf = keep + swap_with(send, axis, mask)
        held.pop(a)
    return buf


def sum_doubling(x, axes):
    for axis in axes:
        for mask in seq_masks(lax.axis_size(axis)):
            x = x + swap_with(x, axis, mask)
    return x


def norm_heads(inputs, norm_gain):
    row_values = inputs.astype(jnp.float32).reshape(inputs.shape[0], -1, norm_gain.shape[0])
    inverse = lax.rsqrt(jnp.mean(row_values * row_values, axis=-1, keepdims=True) + NORM_EPS)
    return (row_values * inverse * norm_gain, inverse)


def norm_back(inputs, inverse, norm_gain, grad_out):
    row_values = inputs.astype(jnp.float32).reshape(grad_out.shape)
    scaled = grad_out * norm_gain
    grad_input = inverse * scaled - row_values * inverse * inverse * inverse * jnp.mean(
        scaled * row_values, axis=-1, keepdims=True
    )
    grad_gain = jnp.sum(grad_out * row_values * inverse, axis=(0, 1))
    return (grad_input.reshape(inputs.shape), grad_gain)


def block_pass(query_rows, key_rows, value_rows, keep_mask, grad_rows, score_scale):
    scores = (
        jnp.einsum("qhd,khd->hqk", query_rows, key_rows, preferred_element_type=jnp.float32)
        * score_scale
    )
    exp_scores = jnp.where(keep_mask[None, None, :], jnp.exp(scores), 0.0)
    totals = jnp.sum(exp_scores, axis=2)
    prob_full = exp_scores / totals[:, :, None]
    prob_low = prob_full.astype(jnp.bfloat16)
    block_output = jnp.einsum(
        "hqk,khd->qhd", prob_low, value_rows, preferred_element_type=jnp.float32
    ).astype(jnp.bfloat16)
    delta_rows = jnp.sum(grad_rows.astype(jnp.float32) * block_output.astype(jnp.float32), axis=2).T
    grad_prob = jnp.einsum(
        "qhd,khd->hqk", grad_rows, value_rows, preferred_element_type=jnp.float32
    )
    grad_score = (prob_full * (grad_prob - delta_rows[:, :, None])).astype(jnp.bfloat16)
    query_gradient = (
        jnp.einsum("hqk,khd->qhd", grad_score, key_rows, preferred_element_type=jnp.float32)
        * score_scale
    )
    grad_key = (
        jnp.einsum("hqk,qhd->khd", grad_score, query_rows, preferred_element_type=jnp.float32)
        * score_scale
    )
    value_gradient = jnp.einsum(
        "hqk,qhd->khd", prob_low, grad_rows, preferred_element_type=jnp.float32
    )
    return (block_output, query_gradient, grad_key, value_gradient)


def attention_kernel(
    tiles_ref, q_ref, ek_ref, ev_ref, lk0_ref, lk1_ref, lv0_ref, lv1_ref, g_ref, m_ref, qg_ref, kg_ref,
    o_ref, dqi_ref, dke_ref, dve_ref, part_ref, gain_ref, *, scale
):
    f32 = jnp.float32
    window = ek_ref.shape[0]
    q_gain = qg_ref[...]
    k_gain = kg_ref[...]

    def normed(x_ref, gain):
        x = x_ref[...].astype(f32)
        inv = lax.rsqrt(jnp.mean(x * x, axis=1, keepdims=True) + NORM_EPS)
        return x, inv, (x * inv * gain).astype(jnp.bfloat16)

    qx, qinv, q = normed(q_ref, q_gain)
    kx, kinv, kn = normed(ek_ref, k_gain)
    lx0, linv0, ln0 = normed(lk0_ref, k_gain)
    lx1, linv1, ln1 = normed(lk1_ref, k_gain)
    g = g_ref[...]
    k = jnp.concatenate([kn, ln0, ln1], axis=0)
    v = jnp.concatenate([ev_ref[...], lv0_ref[...], lv1_ref[...]], axis=0)
    keep = m_ref[...] > 0.0
    nt = (((1,), (1,)), ((), ()))
    tn = (((0,), (0,)), ((), ()))
    s = lax.dot_general(q, k, nt, preferred_element_type=f32) * scale
    e = jnp.where(keep, jnp.exp(s), 0.0)
    tot = jnp.sum(e, axis=1, keepdims=True)
    p = e / tot
    p_low = p.astype(jnp.bfloat16)
    o = jnp.dot(p_low, v, preferred_element_type=f32).astype(jnp.bfloat16)
    o_ref[...] = o
    delta = jnp.sum(g.astype(f32) * o.astype(f32), axis=1, keepdims=True)
    dp = lax.dot_general(g, v, nt, preferred_element_type=f32)
    ds = (p * (dp - delta)).astype(jnp.bfloat16)
    dq = jnp.dot(ds, k, preferred_element_type=f32) * scale
    dk = lax.dot_general(ds, q, tn, preferred_element_type=f32) * scale
    dv = lax.dot_general(p_low, g, tn, preferred_element_type=f32)
    scaled = dq * q_gain
    dqi_ref[...] = (
        qinv * scaled - qx * qinv * qinv * qinv * jnp.mean(scaled * qx, axis=1, keepdims=True)
    ).astype(jnp.bfloat16)
    dke_ref[...] = dk[:window]
    dve_ref[...] = dv[:window]
    for j in range(part_ref.shape[1] // BLK):
        for c, d in enumerate((dk, dv)):
            placed = jnp.zeros((BLK, d.shape[1]), f32)
            for s in range(tiles_ref.shape[0]):
                rows = d[window + s * BLK : window + (s + 1) * BLK]
                placed = placed + jnp.where(tiles_ref[s] == j, rows, 0.0)
            part_ref[c, j * BLK : (j + 1) * BLK, :] = placed
    gq = jnp.sum(dq * qx * qinv, axis=0, keepdims=True)
    gk = (
        jnp.sum(dk[:window] * kx * kinv, axis=0, keepdims=True)
        + jnp.sum(dk[window : window + BLK] * lx0 * linv0, axis=0, keepdims=True)
        + jnp.sum(dk[window + BLK :] * lx1 * linv1, axis=0, keepdims=True)
    )
    gain_ref[...] = jnp.concatenate([gq, gk, jnp.zeros((6, gq.shape[1]), f32)], axis=0)


def attention_block(tiles, q, ek, ev, lk, lv, g, keep, q_gain, k_gain, scale):
    lyric_rows = lk.shape[0]
    rows, width = q.shape
    head_size = q_gain.shape[0]
    window = ek.shape[0]
    slots = tiles.shape[0]
    heads = width // head_size
    f32 = jnp.float32

    def col(r):
        return pl.BlockSpec((r, head_size), lambda h, t: (0, h))

    def slot(s):
        return pl.BlockSpec((BLK, head_size), lambda h, t: (jnp.maximum(t[s], 0), h))

    whole = pl.BlockSpec((1, head_size), lambda h, t: (0, 0))
    grid_spec = pltpu.PrefetchScalarGridSpec(
        num_scalar_prefetch=1,
        grid=(heads,),
        in_specs=[col(rows), col(window), col(window), slot(0), slot(1), slot(0), slot(1), col(rows),
                  pl.BlockSpec((1, keep.shape[1]), lambda h, t: (0, 0)), whole, whole],
        out_specs=[col(rows), col(rows), col(window), col(window),
                   pl.BlockSpec((2, lyric_rows, head_size), lambda h, t: (0, 0, h)), col(8)],
    )
    return pl.pallas_call(
        lambda *refs: attention_kernel(*refs, scale=scale),
        grid_spec=grid_spec,
        out_shape=[
            jax.ShapeDtypeStruct((rows, width), jnp.bfloat16),
            jax.ShapeDtypeStruct((rows, width), jnp.bfloat16),
            jax.ShapeDtypeStruct((window, width), f32),
            jax.ShapeDtypeStruct((window, width), f32),
            jax.ShapeDtypeStruct((2, lyric_rows, width), f32),
            jax.ShapeDtypeStruct((8, width), f32),
        ],
    )(tiles, q, ek, ev, lk, lk, lv, lv, g, keep, q_gain.reshape(1, head_size), k_gain.reshape(1, head_size))


def body(
    queries, keys, values, lyric_keys, lyric_values, q_gain, k_gain, cotangent, alignment, lyric_len
):
    head_size = q_gain.shape[0]
    model_width = queries.shape[2]
    head_count = model_width // head_size
    frames = queries.shape[1]
    lyric_local = lyric_keys.shape[1]
    seq_count = lax.axis_size("seq")
    border_rows = WIN * BLK
    window_extent = (2 * WIN + 1) * BLK
    score_scale = head_size ** (-0.5)
    total_frames = frames * seq_count
    first_frame = lax.axis_index("seq") * frames
    lyric_total = lyric_local * seq_count
    lyric_blocks = lyric_total // BLK
    masks = seq_masks(seq_count)

    lyric_pair = jnp.stack([lyric_keys[0], lyric_values[0]])
    lyric_all = gather_doubling(lyric_pair, "seq", masks[::-1])
    lyric_all = jnp.swapaxes(lyric_all, 0, 1).reshape(2, lyric_total, model_width)

    query_raw = queries[0]
    lyric_inv = norm_heads(lyric_keys[0], k_gain)[1]

    stacked = jnp.stack([keys[0], values[0]])
    extended = extended_2(stacked, (("seq", 1),), border_rows)
    key_raw = keys[0]
    key_inv = norm_heads(key_raw, k_gain)[1]
    length = lyric_len[0]

    position = first_frame - border_rows + jnp.arange(window_extent, dtype=jnp.int32)
    audio_mask = (position >= 0) & (position < total_frames)
    tile_ids = alignment[0, 0]
    tiles = jnp.maximum(tile_ids, 0)
    lyric_mask = jnp.concatenate(
        [(tile_ids[s] >= 0) & (tiles[s] * BLK + jnp.arange(BLK, dtype=jnp.int32) < length) for s in range(TILES)]
    )
    keep_mask = jnp.concatenate([audio_mask, lyric_mask], axis=0).astype(jnp.float32)[None]
    block_output, unnormed_query_gradient, ext_grad_key, ext_grad_val, parts, gain_rows = attention_block(
        tile_ids,
        query_raw,
        extended[0],
        extended[1],
        lyric_all[0],
        lyric_all[1],
        cotangent[0],
        keep_mask,
        q_gain,
        k_gain,
        score_scale,
    )
    ext_grad_key = ext_grad_key.reshape(window_extent, head_count, head_size)
    ext_grad_val = ext_grad_val.reshape(window_extent, head_count, head_size)
    gains = jnp.sum(gain_rows[:2].reshape(2, head_count, head_size), axis=1).reshape(1, 1, 2 * head_size)
    pad_rows = -(2 * lyric_local + 1) % 8 + 1
    gain_row = jnp.pad(gains, ((0, 0), (0, pad_rows - 1), (0, model_width - 2 * head_size)))
    payload = jnp.concatenate(
        [
            jnp.swapaxes(parts.reshape(2, seq_count, lyric_local, model_width), 0, 1).reshape(
                seq_count, 2 * lyric_local, model_width
            ),
            jnp.broadcast_to(gain_row, (seq_count, pad_rows, model_width)),
        ],
        axis=1,
    )
    summed = scatter_halving(payload, "seq", masks)
    total_gains = sum_doubling(summed[2 * lyric_local, : 2 * head_size].reshape(2, head_size), ("song",))
    summed = summed[: 2 * lyric_local].reshape(2, lyric_local, model_width)
    summed_key = summed[0].reshape(lyric_local, head_count, head_size)
    summed_val = summed[1]

    own_grad_key = ext_grad_key[border_rows : border_rows + frames]
    own_grad_val = ext_grad_val[border_rows : border_rows + frames]
    rims = jnp.stack(
        [
            jnp.concatenate(
                [ext_grad_key[:border_rows], ext_grad_key[border_rows + frames :]], axis=0
            ).reshape(2 * border_rows, model_width),
            jnp.concatenate(
                [ext_grad_val[:border_rows], ext_grad_val[border_rows + frames :]], axis=0
            ).reshape(2 * border_rows, model_width),
        ]
    )
    received = extended_2(rims.astype(jnp.bfloat16), (("seq", 1),), border_rows).astype(rims.dtype)
    from_left = received[:, :border_rows].reshape(2, border_rows, head_count, head_size)
    from_right = received[:, 3 * border_rows :].reshape(2, border_rows, head_count, head_size)
    own_grad_key = (
        own_grad_key.at[:border_rows]
        .add(from_left[0])
        .at[frames - border_rows :]
        .add(from_right[0])
    )
    own_grad_val = (
        own_grad_val.at[:border_rows]
        .add(from_left[1])
        .at[frames - border_rows :]
        .add(from_right[1])
    )
    unnormed_key_gradient = norm_back(key_raw, key_inv, k_gain, own_grad_key)[0]
    unnormed_lyric_gradient = norm_back(lyric_keys[0], lyric_inv, k_gain, summed_key)[0]
    return (
        block_output.reshape(1, frames, model_width),
        unnormed_query_gradient[None],
        unnormed_key_gradient.astype(jnp.bfloat16)[None],
        own_grad_val.reshape(1, frames, model_width).astype(jnp.bfloat16),
        unnormed_lyric_gradient.astype(jnp.bfloat16)[None],
        summed_val.astype(jnp.bfloat16)[None],
        total_gains[0],
        total_gains[1],
    )


def solution(mesh):
    in_specs = (
        P("song", "seq", None),
        P("song", "seq", None),
        P("song", "seq", None),
        P("song", "seq", None),
        P("song", "seq", None),
        P(),
        P(),
        P("song", "seq", None),
        P("song", "seq", None),
        P("song"),
    )
    out_specs = (
        P("song", "seq", None),
        P("song", "seq", None),
        P("song", "seq", None),
        P("song", "seq", None),
        P("song", "seq", None),
        P("song", "seq", None),
        P(),
        P(),
    )
    return jax.shard_map(body, mesh=mesh, in_specs=in_specs, out_specs=out_specs, check_vma=False)
```

```python
import jax
import jax.numpy as jnp
from jax import lax
from jax.sharding import PartitionSpec as P
from jax.experimental import pallas as pl
from jax.experimental.pallas import tpu as pltpu

BLK = 128
WIN = 1
TILES = 2


NORM_EPS = 1e-06


def extended_2(block, sides, width):
    for axis, dim in sides:
        count = lax.axis_size(axis)
        forward = [(i, i + 1) for i in range(count - 1)]
        backward = [(target, source) for source, target in forward]
        low = lax.ppermute(
            lax.slice_in_dim(block, block.shape[dim] - width, None, axis=dim), axis, forward
        )
        high = lax.ppermute(lax.slice_in_dim(block, 0, width, axis=dim), axis, backward)
        block = jnp.concatenate([low, block, high], axis=dim)
    return block


def seq_masks(count):
    masks = []
    m = 1
    while m < count:
        masks.append(m)
        m *= 2
    return masks


def swap_with(x, axis, mask):
    count = lax.axis_size(axis)
    return lax.ppermute(x, axis, [(i, i ^ mask) for i in range(count)])


def gather_doubling(chunk, axis, order):
    idx = lax.axis_index(axis)
    steps = len(order)
    slot = sum(((idx // m) % 2) * (2 ** k) for k, m in enumerate(order))
    buf = jnp.zeros((2 ** steps,) + chunk.shape, chunk.dtype)
    buf = lax.dynamic_update_index_in_dim(buf, chunk, slot, 0)
    for k, mask in enumerate(order):
        size = 2 ** k
        base = (slot // size) * size
        other = swap_with(lax.dynamic_slice_in_dim(buf, base, size, 0), axis, mask)
        flipped = base + size - 2 * size * ((slot // size) % 2)
        buf = lax.dynamic_update_slice_in_dim(buf, other, flipped, 0)
    buf = buf.reshape((2,) * steps + chunk.shape)
    held = [order[steps - 1 - k] for k in range(steps)]
    perm = sorted(range(steps), key=lambda k: -held[k])
    buf = jnp.transpose(buf, perm + list(range(steps, buf.ndim)))
    return buf.reshape((2 ** steps,) + chunk.shape)


def scatter_halving(parts, axis, order, rider):
    idx = lax.axis_index(axis)
    steps = len(order)
    buf = parts.reshape(parts.shape[:1] + (2,) * steps + parts.shape[2:])
    held = sorted(order, reverse=True)
    for mask in order:
        a = held.index(mask) + 1
        high = ((idx & mask) != 0).astype(jnp.int32)
        keep = lax.dynamic_index_in_dim(buf, high, axis=a, keepdims=False)
        send = lax.dynamic_index_in_dim(buf, 1 - high, axis=a, keepdims=False)
        got, other = swap_with((send.astype(jnp.bfloat16), rider), axis, mask)
        buf = keep + got.astype(keep.dtype)
        rider = rider + other
        held.pop(a - 1)
    return buf, rider


def sum_doubling(x, axes):
    for axis in axes:
        for mask in seq_masks(lax.axis_size(axis)):
            x = x + swap_with(x, axis, mask)
    return x


def norm_heads(inputs, norm_gain):
    row_values = inputs.astype(jnp.float32).reshape(inputs.shape[0], -1, norm_gain.shape[0])
    inverse = lax.rsqrt(jnp.mean(row_values * row_values, axis=-1, keepdims=True) + NORM_EPS)
    return (row_values * inverse * norm_gain, inverse)


def norm_back(inputs, inverse, norm_gain, grad_out):
    row_values = inputs.astype(jnp.float32).reshape(grad_out.shape)
    scaled = grad_out * norm_gain
    grad_input = inverse * scaled - row_values * inverse * inverse * inverse * jnp.mean(
        scaled * row_values, axis=-1, keepdims=True
    )
    grad_gain = jnp.sum(grad_out * row_values * inverse, axis=(0, 1))
    return (grad_input.reshape(inputs.shape), grad_gain)


def block_pass(query_rows, key_rows, value_rows, keep_mask, grad_rows, score_scale):
    scores = (
        jnp.einsum("qhd,khd->hqk", query_rows, key_rows, preferred_element_type=jnp.float32)
        * score_scale
    )
    exp_scores = jnp.where(keep_mask[None, None, :], jnp.exp(scores), 0.0)
    totals = jnp.sum(exp_scores, axis=2)
    prob_full = exp_scores / totals[:, :, None]
    prob_low = prob_full.astype(jnp.bfloat16)
    block_output = jnp.einsum(
        "hqk,khd->qhd", prob_low, value_rows, preferred_element_type=jnp.float32
    ).astype(jnp.bfloat16)
    delta_rows = jnp.sum(grad_rows.astype(jnp.float32) * block_output.astype(jnp.float32), axis=2).T
    grad_prob = jnp.einsum(
        "qhd,khd->hqk", grad_rows, value_rows, preferred_element_type=jnp.float32
    )
    grad_score = (prob_full * (grad_prob - delta_rows[:, :, None])).astype(jnp.bfloat16)
    query_gradient = (
        jnp.einsum("hqk,khd->qhd", grad_score, key_rows, preferred_element_type=jnp.float32)
        * score_scale
    )
    grad_key = (
        jnp.einsum("hqk,qhd->khd", grad_score, query_rows, preferred_element_type=jnp.float32)
        * score_scale
    )
    value_gradient = jnp.einsum(
        "hqk,qhd->khd", prob_low, grad_rows, preferred_element_type=jnp.float32
    )
    return (block_output, query_gradient, grad_key, value_gradient)


def attention_kernel(
    tiles_ref, q_ref, ek_ref, ev_ref, lk0_ref, lk1_ref, lv0_ref, lv1_ref, g_ref, m_ref, qg_ref, kg_ref,
    o_ref, dqi_ref, dke_ref, dve_ref, part_ref, gain_ref, *, scale
):
    f32 = jnp.float32
    window = ek_ref.shape[0]
    head_size = qg_ref.shape[1]
    q_gain = qg_ref[...]
    k_gain = kg_ref[...]
    keep = m_ref[...] > 0.0
    nt = (((1,), (1,)), ((), ()))
    tn = (((0,), (0,)), ((), ()))

    def normed(x_ref, cols, gain):
        x = x_ref[:, cols].astype(f32)
        inv = lax.rsqrt(jnp.mean(x * x, axis=1, keepdims=True) + NORM_EPS)
        return x, inv, (x * inv * gain).astype(jnp.bfloat16)

    for i in range(q_ref.shape[1] // head_size):
        cols = slice(i * head_size, (i + 1) * head_size)
        qx, qinv, q = normed(q_ref, cols, q_gain)
        kx, kinv, kn = normed(ek_ref, cols, k_gain)
        lx0, linv0, ln0 = normed(lk0_ref, cols, k_gain)
        lx1, linv1, ln1 = normed(lk1_ref, cols, k_gain)
        g = g_ref[:, cols]
        k = jnp.concatenate([kn, ln0, ln1], axis=0)
        v = jnp.concatenate([ev_ref[:, cols], lv0_ref[:, cols], lv1_ref[:, cols]], axis=0)
        s = lax.dot_general(q, k, nt, preferred_element_type=f32) * scale
        e = jnp.where(keep, jnp.exp(s), 0.0)
        tot = jnp.sum(e, axis=1, keepdims=True)
        p = e / tot
        p_low = p.astype(jnp.bfloat16)
        o = jnp.dot(p_low, v, preferred_element_type=f32).astype(jnp.bfloat16)
        o_ref[:, cols] = o
        delta = jnp.sum(g.astype(f32) * o.astype(f32), axis=1, keepdims=True)
        dp = lax.dot_general(g, v, nt, preferred_element_type=f32)
        ds = (p * (dp - delta)).astype(jnp.bfloat16)
        dq = jnp.dot(ds, k, preferred_element_type=f32) * scale
        dk = lax.dot_general(ds, q, tn, preferred_element_type=f32) * scale
        dv = lax.dot_general(p_low, g, tn, preferred_element_type=f32)
        scaled = dq * q_gain
        dqi_ref[:, cols] = (
            qinv * scaled - qx * qinv * qinv * qinv * jnp.mean(scaled * qx, axis=1, keepdims=True)
        ).astype(jnp.bfloat16)
        dke_ref[:, cols] = dk[:window]
        dve_ref[:, cols] = dv[:window]
        for j in range(part_ref.shape[1] // BLK):
            for c, d in enumerate((dk, dv)):
                placed = jnp.zeros((BLK, head_size), f32)
                for s_ in range(tiles_ref.shape[0]):
                    rows = d[window + s_ * BLK : window + (s_ + 1) * BLK]
                    placed = placed + jnp.where(tiles_ref[s_] == j, rows, 0.0)
                part_ref[c, j * BLK : (j + 1) * BLK, cols] = placed
        gq = jnp.sum(dq * qx * qinv, axis=0, keepdims=True)
        gk = (
            jnp.sum(dk[:window] * kx * kinv, axis=0, keepdims=True)
            + jnp.sum(dk[window : window + BLK] * lx0 * linv0, axis=0, keepdims=True)
            + jnp.sum(dk[window + BLK :] * lx1 * linv1, axis=0, keepdims=True)
        )
        gain_ref[:, cols] = jnp.concatenate([gq, gk, jnp.zeros((6, head_size), f32)], axis=0)


def attention_block(tiles, q, ek, ev, lk, lv, g, keep, q_gain, k_gain, scale):
    lyric_rows = lk.shape[0]
    rows, width = q.shape
    head_size = q_gain.shape[0]
    window = ek.shape[0]
    slots = tiles.shape[0]
    heads = width // head_size
    f32 = jnp.float32

    per = 2 if heads % 2 == 0 else 1
    span = per * head_size

    def col(r):
        return pl.BlockSpec((r, span), lambda h, t: (0, h))

    def slot(s):
        return pl.BlockSpec((BLK, span), lambda h, t: (jnp.maximum(t[s], 0), h))

    whole = pl.BlockSpec((1, head_size), lambda h, t: (0, 0))
    grid_spec = pltpu.PrefetchScalarGridSpec(
        num_scalar_prefetch=1,
        grid=(heads // per,),
        in_specs=[col(rows), col(window), col(window), slot(0), slot(1), slot(0), slot(1), col(rows),
                  pl.BlockSpec((1, keep.shape[1]), lambda h, t: (0, 0)), whole, whole],
        out_specs=[col(rows), col(rows), col(window), col(window),
                   pl.BlockSpec((2, lyric_rows, span), lambda h, t: (0, 0, h)), col(8)],
    )
    return pl.pallas_call(
        lambda *refs: attention_kernel(*refs, scale=scale),
        grid_spec=grid_spec,
        out_shape=[
            jax.ShapeDtypeStruct((rows, width), jnp.bfloat16),
            jax.ShapeDtypeStruct((rows, width), jnp.bfloat16),
            jax.ShapeDtypeStruct((window, width), f32),
            jax.ShapeDtypeStruct((window, width), f32),
            jax.ShapeDtypeStruct((2, lyric_rows, width), f32),
            jax.ShapeDtypeStruct((8, width), f32),
        ],
    )(tiles, q, ek, ev, lk, lk, lv, lv, g, keep, q_gain.reshape(1, head_size), k_gain.reshape(1, head_size))


def body(
    queries, keys, values, lyric_keys, lyric_values, q_gain, k_gain, cotangent, alignment, lyric_len
):
    head_size = q_gain.shape[0]
    model_width = queries.shape[2]
    head_count = model_width // head_size
    frames = queries.shape[1]
    lyric_local = lyric_keys.shape[1]
    seq_count = lax.axis_size("seq")
    border_rows = WIN * BLK
    window_extent = (2 * WIN + 1) * BLK
    score_scale = head_size ** (-0.5)
    total_frames = frames * seq_count
    first_frame = lax.axis_index("seq") * frames
    lyric_total = lyric_local * seq_count
    lyric_blocks = lyric_total // BLK
    masks = seq_masks(seq_count)

    lyric_pair = jnp.stack([lyric_keys[0], lyric_values[0]])
    lyric_all = gather_doubling(lyric_pair, "seq", masks[::-1])
    lyric_all = jnp.swapaxes(lyric_all, 0, 1).reshape(2, lyric_total, model_width)

    query_raw = queries[0]
    lyric_inv = norm_heads(lyric_keys[0], k_gain)[1]

    stacked = jnp.stack([keys[0], values[0]])
    extended = extended_2(stacked, (("seq", 1),), border_rows)
    key_raw = keys[0]
    key_inv = norm_heads(key_raw, k_gain)[1]
    length = lyric_len[0]

    position = first_frame - border_rows + jnp.arange(window_extent, dtype=jnp.int32)
    audio_mask = (position >= 0) & (position < total_frames)
    tile_ids = alignment[0, 0]
    tiles = jnp.maximum(tile_ids, 0)
    lyric_mask = jnp.concatenate(
        [(tile_ids[s] >= 0) & (tiles[s] * BLK + jnp.arange(BLK, dtype=jnp.int32) < length) for s in range(TILES)]
    )
    keep_mask = jnp.concatenate([audio_mask, lyric_mask], axis=0).astype(jnp.float32)[None]
    block_output, unnormed_query_gradient, ext_grad_key, ext_grad_val, parts, gain_rows = attention_block(
        tile_ids,
        query_raw,
        extended[0],
        extended[1],
        lyric_all[0],
        lyric_all[1],
        cotangent[0],
        keep_mask,
        q_gain,
        k_gain,
        score_scale,
    )
    ext_grad_key = ext_grad_key.reshape(window_extent, head_count, head_size)
    ext_grad_val = ext_grad_val.reshape(window_extent, head_count, head_size)
    gains = jnp.sum(gain_rows[:2].reshape(2, head_count, head_size), axis=1)
    summed, gains = scatter_halving(parts.reshape(2, seq_count, lyric_local, model_width), "seq", masks, gains)
    total_gains = sum_doubling(gains, ("song",))
    summed_key = summed[0].reshape(lyric_local, head_count, head_size)
    summed_val = summed[1]

    own_grad_key = ext_grad_key[border_rows : border_rows + frames]
    own_grad_val = ext_grad_val[border_rows : border_rows + frames]
    rims = jnp.stack(
        [
            jnp.concatenate(
                [ext_grad_key[:border_rows], ext_grad_key[border_rows + frames :]], axis=0
            ).reshape(2 * border_rows, model_width),
            jnp.concatenate(
                [ext_grad_val[:border_rows], ext_grad_val[border_rows + frames :]], axis=0
            ).reshape(2 * border_rows, model_width),
        ]
    )
    received = extended_2(rims.astype(jnp.bfloat16), (("seq", 1),), border_rows).astype(rims.dtype)
    from_left = received[:, :border_rows].reshape(2, border_rows, head_count, head_size)
    from_right = received[:, 3 * border_rows :].reshape(2, border_rows, head_count, head_size)
    own_grad_key = (
        own_grad_key.at[:border_rows]
        .add(from_left[0])
        .at[frames - border_rows :]
        .add(from_right[0])
    )
    own_grad_val = (
        own_grad_val.at[:border_rows]
        .add(from_left[1])
        .at[frames - border_rows :]
        .add(from_right[1])
    )
    unnormed_key_gradient = norm_back(key_raw, key_inv, k_gain, own_grad_key)[0]
    unnormed_lyric_gradient = norm_back(lyric_keys[0], lyric_inv, k_gain, summed_key)[0]
    return (
        block_output.reshape(1, frames, model_width),
        unnormed_query_gradient[None],
        unnormed_key_gradient.astype(jnp.bfloat16)[None],
        own_grad_val.reshape(1, frames, model_width).astype(jnp.bfloat16),
        unnormed_lyric_gradient.astype(jnp.bfloat16)[None],
        summed_val.astype(jnp.bfloat16)[None],
        total_gains[0],
        total_gains[1],
    )


def solution(mesh):
    in_specs = (
        P("song", "seq", None),
        P("song", "seq", None),
        P("song", "seq", None),
        P("song", "seq", None),
        P("song", "seq", None),
        P(),
        P(),
        P("song", "seq", None),
        P("song", "seq", None),
        P("song"),
    )
    out_specs = (
        P("song", "seq", None),
        P("song", "seq", None),
        P("song", "seq", None),
        P("song", "seq", None),
        P("song", "seq", None),
        P("song", "seq", None),
        P(),
        P(),
    )
    return jax.shard_map(body, mesh=mesh, in_specs=in_specs, out_specs=out_specs, check_vma=False)
```

```python
import jax
import jax.numpy as jnp
from jax import lax
from jax.sharding import PartitionSpec as P
from jax.experimental import pallas as pl
from jax.experimental.pallas import tpu as pltpu

BLK = 128
WIN = 1
TILES = 2


NORM_EPS = 1e-06


def extended_2(block, sides, width):
    for axis, dim in sides:
        count = lax.axis_size(axis)
        forward = [(i, i + 1) for i in range(count - 1)]
        backward = [(target, source) for source, target in forward]
        low = lax.ppermute(
            lax.slice_in_dim(block, block.shape[dim] - width, None, axis=dim), axis, forward
        )
        high = lax.ppermute(lax.slice_in_dim(block, 0, width, axis=dim), axis, backward)
        block = jnp.concatenate([low, block, high], axis=dim)
    return block


def seq_masks(count):
    masks = []
    m = 1
    while m < count:
        masks.append(m)
        m *= 2
    return masks


def swap_with(x, axis, mask):
    count = lax.axis_size(axis)
    return lax.ppermute(x, axis, [(i, i ^ mask) for i in range(count)])


def gather_doubling(chunk, axis, order):
    idx = lax.axis_index(axis)
    buf = chunk[None]
    for mask in order:
        other = swap_with(buf, axis, mask)
        high = (idx & mask) != 0
        buf = jnp.where(high, jnp.concatenate([other, buf]), jnp.concatenate([buf, other]))
    steps = len(order)
    buf = buf.reshape((2,) * steps + chunk.shape)
    held = [order[steps - 1 - k] for k in range(steps)]
    perm = sorted(range(steps), key=lambda k: -held[k])
    buf = jnp.transpose(buf, perm + list(range(steps, buf.ndim)))
    return buf.reshape((2 ** steps,) + chunk.shape)


def scatter_halving(parts, axis, order, rider):
    idx = lax.axis_index(axis)
    steps = len(order)
    buf = parts.reshape(parts.shape[:1] + (2,) * steps + parts.shape[2:])
    held = sorted(order, reverse=True)
    for mask in order:
        a = held.index(mask) + 1
        high = ((idx & mask) != 0).astype(jnp.int32)
        keep = lax.dynamic_index_in_dim(buf, high, axis=a, keepdims=False)
        send = lax.dynamic_index_in_dim(buf, 1 - high, axis=a, keepdims=False)
        got, other = swap_with((send.astype(jnp.bfloat16), rider), axis, mask)
        buf = keep + got.astype(keep.dtype)
        rider = rider + other
        held.pop(a - 1)
    return buf, rider


def sum_doubling(x, axes):
    for axis in axes:
        for mask in seq_masks(lax.axis_size(axis)):
            x = x + swap_with(x, axis, mask)
    return x


def norm_heads(inputs, norm_gain):
    row_values = inputs.astype(jnp.float32).reshape(inputs.shape[0], -1, norm_gain.shape[0])
    inverse = lax.rsqrt(jnp.mean(row_values * row_values, axis=-1, keepdims=True) + NORM_EPS)
    return (row_values * inverse * norm_gain, inverse)


def norm_back(inputs, inverse, norm_gain, grad_out):
    row_values = inputs.astype(jnp.float32).reshape(grad_out.shape)
    scaled = grad_out * norm_gain
    grad_input = inverse * scaled - row_values * inverse * inverse * inverse * jnp.mean(
        scaled * row_values, axis=-1, keepdims=True
    )
    grad_gain = jnp.sum(grad_out * row_values * inverse, axis=(0, 1))
    return (grad_input.reshape(inputs.shape), grad_gain)


def block_pass(query_rows, key_rows, value_rows, keep_mask, grad_rows, score_scale):
    scores = (
        jnp.einsum("qhd,khd->hqk", query_rows, key_rows, preferred_element_type=jnp.float32)
        * score_scale
    )
    exp_scores = jnp.where(keep_mask[None, None, :], jnp.exp(scores), 0.0)
    totals = jnp.sum(exp_scores, axis=2)
    prob_full = exp_scores / totals[:, :, None]
    prob_low = prob_full.astype(jnp.bfloat16)
    block_output = jnp.einsum(
        "hqk,khd->qhd", prob_low, value_rows, preferred_element_type=jnp.float32
    ).astype(jnp.bfloat16)
    delta_rows = jnp.sum(grad_rows.astype(jnp.float32) * block_output.astype(jnp.float32), axis=2).T
    grad_prob = jnp.einsum(
        "qhd,khd->hqk", grad_rows, value_rows, preferred_element_type=jnp.float32
    )
    grad_score = (prob_full * (grad_prob - delta_rows[:, :, None])).astype(jnp.bfloat16)
    query_gradient = (
        jnp.einsum("hqk,khd->qhd", grad_score, key_rows, preferred_element_type=jnp.float32)
        * score_scale
    )
    grad_key = (
        jnp.einsum("hqk,qhd->khd", grad_score, query_rows, preferred_element_type=jnp.float32)
        * score_scale
    )
    value_gradient = jnp.einsum(
        "hqk,qhd->khd", prob_low, grad_rows, preferred_element_type=jnp.float32
    )
    return (block_output, query_gradient, grad_key, value_gradient)


def attention_kernel(
    tiles_ref, q_ref, ek_ref, ev_ref, lk0_ref, lk1_ref, lv0_ref, lv1_ref, g_ref, m_ref, qg_ref, kg_ref,
    o_ref, dqi_ref, dke_ref, dve_ref, part_ref, gain_ref, *, scale
):
    f32 = jnp.float32
    window = ek_ref.shape[0]
    head_size = qg_ref.shape[1]
    q_gain = qg_ref[...]
    k_gain = kg_ref[...]
    keep = m_ref[...] > 0.0
    nt = (((1,), (1,)), ((), ()))
    tn = (((0,), (0,)), ((), ()))

    def normed(x_ref, cols, gain):
        x = x_ref[:, cols].astype(f32)
        inv = lax.rsqrt(jnp.mean(x * x, axis=1, keepdims=True) + NORM_EPS)
        return x, inv, (x * inv * gain).astype(jnp.bfloat16)

    for i in range(q_ref.shape[1] // head_size):
        cols = slice(i * head_size, (i + 1) * head_size)
        qx, qinv, q = normed(q_ref, cols, q_gain)
        kx, kinv, kn = normed(ek_ref, cols, k_gain)
        lx0, linv0, ln0 = normed(lk0_ref, cols, k_gain)
        lx1, linv1, ln1 = normed(lk1_ref, cols, k_gain)
        g = g_ref[:, cols]
        k = jnp.concatenate([kn, ln0, ln1], axis=0)
        v = jnp.concatenate([ev_ref[:, cols], lv0_ref[:, cols], lv1_ref[:, cols]], axis=0)
        s = lax.dot_general(q, k, nt, preferred_element_type=f32) * scale
        e = jnp.where(keep, jnp.exp(s), 0.0)
        tot = jnp.sum(e, axis=1, keepdims=True)
        p = e / tot
        p_low = p.astype(jnp.bfloat16)
        o = jnp.dot(p_low, v, preferred_element_type=f32).astype(jnp.bfloat16)
        o_ref[:, cols] = o
        delta = jnp.sum(g.astype(f32) * o.astype(f32), axis=1, keepdims=True)
        dp = lax.dot_general(g, v, nt, preferred_element_type=f32)
        ds = (p * (dp - delta)).astype(jnp.bfloat16)
        dq = jnp.dot(ds, k, preferred_element_type=f32) * scale
        dk = lax.dot_general(ds, q, tn, preferred_element_type=f32) * scale
        dv = lax.dot_general(p_low, g, tn, preferred_element_type=f32)
        scaled = dq * q_gain
        dqi_ref[:, cols] = (
            qinv * scaled - qx * qinv * qinv * qinv * jnp.mean(scaled * qx, axis=1, keepdims=True)
        ).astype(jnp.bfloat16)
        dke_ref[:, cols] = dk[:window]
        dve_ref[:, cols] = dv[:window]
        for j in range(part_ref.shape[1] // BLK):
            for c, d in enumerate((dk, dv)):
                placed = jnp.zeros((BLK, head_size), f32)
                for s_ in range(tiles_ref.shape[0]):
                    rows = d[window + s_ * BLK : window + (s_ + 1) * BLK]
                    placed = placed + jnp.where(tiles_ref[s_] == j, rows, 0.0)
                part_ref[c, j * BLK : (j + 1) * BLK, cols] = placed
        gq = jnp.sum(dq * qx * qinv, axis=0, keepdims=True)
        gk = (
            jnp.sum(dk[:window] * kx * kinv, axis=0, keepdims=True)
            + jnp.sum(dk[window : window + BLK] * lx0 * linv0, axis=0, keepdims=True)
            + jnp.sum(dk[window + BLK :] * lx1 * linv1, axis=0, keepdims=True)
        )
        gain_ref[:, cols] = jnp.concatenate([gq, gk, jnp.zeros((6, head_size), f32)], axis=0)


def attention_block(tiles, q, ek, ev, lk, lv, g, keep, q_gain, k_gain, scale):
    lyric_rows = lk.shape[0]
    rows, width = q.shape
    head_size = q_gain.shape[0]
    window = ek.shape[0]
    slots = tiles.shape[0]
    heads = width // head_size
    f32 = jnp.float32

    per = 2 if heads % 2 == 0 else 1
    span = per * head_size

    def col(r):
        return pl.BlockSpec((r, span), lambda h, t: (0, h))

    def slot(s):
        return pl.BlockSpec((BLK, span), lambda h, t: (jnp.maximum(t[s], 0), h))

    whole = pl.BlockSpec((1, head_size), lambda h, t: (0, 0))
    grid_spec = pltpu.PrefetchScalarGridSpec(
        num_scalar_prefetch=1,
        grid=(heads // per,),
        in_specs=[col(rows), col(window), col(window), slot(0), slot(1), slot(0), slot(1), col(rows),
                  pl.BlockSpec((1, keep.shape[1]), lambda h, t: (0, 0)), whole, whole],
        out_specs=[col(rows), col(rows), col(window), col(window),
                   pl.BlockSpec((2, lyric_rows, span), lambda h, t: (0, 0, h)), col(8)],
    )
    return pl.pallas_call(
        lambda *refs: attention_kernel(*refs, scale=scale),
        grid_spec=grid_spec,
        out_shape=[
            jax.ShapeDtypeStruct((rows, width), jnp.bfloat16),
            jax.ShapeDtypeStruct((rows, width), jnp.bfloat16),
            jax.ShapeDtypeStruct((window, width), f32),
            jax.ShapeDtypeStruct((window, width), f32),
            jax.ShapeDtypeStruct((2, lyric_rows, width), f32),
            jax.ShapeDtypeStruct((8, width), f32),
        ],
    )(tiles, q, ek, ev, lk, lk, lv, lv, g, keep, q_gain.reshape(1, head_size), k_gain.reshape(1, head_size))


def body(
    queries, keys, values, lyric_keys, lyric_values, q_gain, k_gain, cotangent, alignment, lyric_len
):
    head_size = q_gain.shape[0]
    model_width = queries.shape[2]
    head_count = model_width // head_size
    frames = queries.shape[1]
    lyric_local = lyric_keys.shape[1]
    seq_count = lax.axis_size("seq")
    border_rows = WIN * BLK
    window_extent = (2 * WIN + 1) * BLK
    score_scale = head_size ** (-0.5)
    total_frames = frames * seq_count
    first_frame = lax.axis_index("seq") * frames
    lyric_total = lyric_local * seq_count
    lyric_blocks = lyric_total // BLK
    masks = seq_masks(seq_count)

    lyric_pair = jnp.stack([lyric_keys[0], lyric_values[0]])
    lyric_all = gather_doubling(lyric_pair, "seq", masks[::-1])
    lyric_all = jnp.swapaxes(lyric_all, 0, 1).reshape(2, lyric_total, model_width)

    query_raw = queries[0]
    lyric_inv = norm_heads(lyric_keys[0], k_gain)[1]

    stacked = jnp.stack([keys[0], values[0]])
    extended = extended_2(stacked, (("seq", 1),), border_rows)
    key_raw = keys[0]
    key_inv = norm_heads(key_raw, k_gain)[1]
    length = lyric_len[0]

    position = first_frame - border_rows + jnp.arange(window_extent, dtype=jnp.int32)
    audio_mask = (position >= 0) & (position < total_frames)
    tile_ids = alignment[0, 0]
    tiles = jnp.maximum(tile_ids, 0)
    lyric_mask = jnp.concatenate(
        [(tile_ids[s] >= 0) & (tiles[s] * BLK + jnp.arange(BLK, dtype=jnp.int32) < length) for s in range(TILES)]
    )
    keep_mask = jnp.concatenate([audio_mask, lyric_mask], axis=0).astype(jnp.float32)[None]
    block_output, unnormed_query_gradient, ext_grad_key, ext_grad_val, parts, gain_rows = attention_block(
        tile_ids,
        query_raw,
        extended[0],
        extended[1],
        lyric_all[0],
        lyric_all[1],
        cotangent[0],
        keep_mask,
        q_gain,
        k_gain,
        score_scale,
    )
    ext_grad_key = ext_grad_key.reshape(window_extent, head_count, head_size)
    ext_grad_val = ext_grad_val.reshape(window_extent, head_count, head_size)
    gains = jnp.sum(gain_rows[:2].reshape(2, head_count, head_size), axis=1)
    summed, gains = scatter_halving(parts.reshape(2, seq_count, lyric_local, model_width), "seq", masks, gains)
    total_gains = sum_doubling(gains, ("song",))
    summed_key = summed[0].reshape(lyric_local, head_count, head_size)
    summed_val = summed[1]

    own_grad_key = ext_grad_key[border_rows : border_rows + frames]
    own_grad_val = ext_grad_val[border_rows : border_rows + frames]
    rims = jnp.stack(
        [
            jnp.concatenate(
                [ext_grad_key[:border_rows], ext_grad_key[border_rows + frames :]], axis=0
            ).reshape(2 * border_rows, model_width),
            jnp.concatenate(
                [ext_grad_val[:border_rows], ext_grad_val[border_rows + frames :]], axis=0
            ).reshape(2 * border_rows, model_width),
        ]
    )
    received = extended_2(rims.astype(jnp.bfloat16), (("seq", 1),), border_rows).astype(rims.dtype)
    from_left = received[:, :border_rows].reshape(2, border_rows, head_count, head_size)
    from_right = received[:, 3 * border_rows :].reshape(2, border_rows, head_count, head_size)
    own_grad_key = (
        own_grad_key.at[:border_rows]
        .add(from_left[0])
        .at[frames - border_rows :]
        .add(from_right[0])
    )
    own_grad_val = (
        own_grad_val.at[:border_rows]
        .add(from_left[1])
        .at[frames - border_rows :]
        .add(from_right[1])
    )
    unnormed_key_gradient = norm_back(key_raw, key_inv, k_gain, own_grad_key)[0]
    unnormed_lyric_gradient = norm_back(lyric_keys[0], lyric_inv, k_gain, summed_key)[0]
    return (
        block_output.reshape(1, frames, model_width),
        unnormed_query_gradient[None],
        unnormed_key_gradient.astype(jnp.bfloat16)[None],
        own_grad_val.reshape(1, frames, model_width).astype(jnp.bfloat16),
        unnormed_lyric_gradient.astype(jnp.bfloat16)[None],
        summed_val.astype(jnp.bfloat16)[None],
        total_gains[0],
        total_gains[1],
    )


def solution(mesh):
    in_specs = (
        P("song", "seq", None),
        P("song", "seq", None),
        P("song", "seq", None),
        P("song", "seq", None),
        P("song", "seq", None),
        P(),
        P(),
        P("song", "seq", None),
        P("song", "seq", None),
        P("song"),
    )
    out_specs = (
        P("song", "seq", None),
        P("song", "seq", None),
        P("song", "seq", None),
        P("song", "seq", None),
        P("song", "seq", None),
        P("song", "seq", None),
        P(),
        P(),
    )
    return jax.shard_map(body, mesh=mesh, in_specs=in_specs, out_specs=out_specs, check_vma=False)
```

```python
import jax
import jax.numpy as jnp
from jax import lax
from jax.sharding import PartitionSpec as P
from jax.experimental import pallas as pl
from jax.experimental.pallas import tpu as pltpu

BLK = 128
WIN = 1
TILES = 2


NORM_EPS = 1e-06


def extended_2(block, sides, width):
    for axis, dim in sides:
        count = lax.axis_size(axis)
        forward = [(i, i + 1) for i in range(count - 1)]
        backward = [(target, source) for source, target in forward]
        low = lax.ppermute(
            lax.slice_in_dim(block, block.shape[dim] - width, None, axis=dim), axis, forward
        )
        high = lax.ppermute(lax.slice_in_dim(block, 0, width, axis=dim), axis, backward)
        block = jnp.concatenate([low, block, high], axis=dim)
    return block


def seq_masks(count):
    masks = []
    m = 1
    while m < count:
        masks.append(m)
        m *= 2
    return masks


def swap_with(x, axis, mask):
    count = lax.axis_size(axis)
    return lax.ppermute(x, axis, [(i, i ^ mask) for i in range(count)])


def gather_doubling(chunk, axis, order):
    idx = lax.axis_index(axis)
    buf = chunk[None]
    for mask in order:
        other = swap_with(buf, axis, mask)
        high = (idx & mask) != 0
        buf = jnp.where(high, jnp.concatenate([other, buf]), jnp.concatenate([buf, other]))
    steps = len(order)
    buf = buf.reshape((2,) * steps + chunk.shape)
    held = [order[steps - 1 - k] for k in range(steps)]
    perm = sorted(range(steps), key=lambda k: -held[k])
    buf = jnp.transpose(buf, perm + list(range(steps, buf.ndim)))
    return buf.reshape((2 ** steps,) + chunk.shape)


def scatter_halving(parts, axis, order, rider):
    idx = lax.axis_index(axis)
    steps = len(order)
    buf = parts.reshape(parts.shape[:1] + (2,) * steps + parts.shape[2:])
    held = sorted(order, reverse=True)
    for mask in order:
        a = held.index(mask) + 1
        high = ((idx & mask) != 0).astype(jnp.int32)
        keep = lax.dynamic_index_in_dim(buf, high, axis=a, keepdims=False)
        send = lax.dynamic_index_in_dim(buf, 1 - high, axis=a, keepdims=False)
        got, other = swap_with((send.astype(jnp.bfloat16), rider), axis, mask)
        buf = keep.astype(jnp.float32) + got.astype(jnp.float32)
        rider = rider + other
        held.pop(a - 1)
    return buf, rider


def sum_doubling(x, axes):
    for axis in axes:
        for mask in seq_masks(lax.axis_size(axis)):
            x = x + swap_with(x, axis, mask)
    return x


def norm_heads(inputs, norm_gain):
    row_values = inputs.astype(jnp.float32).reshape(inputs.shape[0], -1, norm_gain.shape[0])
    inverse = lax.rsqrt(jnp.mean(row_values * row_values, axis=-1, keepdims=True) + NORM_EPS)
    return (row_values * inverse * norm_gain, inverse)


def norm_back(inputs, inverse, norm_gain, grad_out):
    row_values = inputs.astype(jnp.float32).reshape(grad_out.shape)
    scaled = grad_out * norm_gain
    grad_input = inverse * scaled - row_values * inverse * inverse * inverse * jnp.mean(
        scaled * row_values, axis=-1, keepdims=True
    )
    grad_gain = jnp.sum(grad_out * row_values * inverse, axis=(0, 1))
    return (grad_input.reshape(inputs.shape), grad_gain)


def block_pass(query_rows, key_rows, value_rows, keep_mask, grad_rows, score_scale):
    scores = (
        jnp.einsum("qhd,khd->hqk", query_rows, key_rows, preferred_element_type=jnp.float32)
        * score_scale
    )
    exp_scores = jnp.where(keep_mask[None, None, :], jnp.exp(scores), 0.0)
    totals = jnp.sum(exp_scores, axis=2)
    prob_full = exp_scores / totals[:, :, None]
    prob_low = prob_full.astype(jnp.bfloat16)
    block_output = jnp.einsum(
        "hqk,khd->qhd", prob_low, value_rows, preferred_element_type=jnp.float32
    ).astype(jnp.bfloat16)
    delta_rows = jnp.sum(grad_rows.astype(jnp.float32) * block_output.astype(jnp.float32), axis=2).T
    grad_prob = jnp.einsum(
        "qhd,khd->hqk", grad_rows, value_rows, preferred_element_type=jnp.float32
    )
    grad_score = (prob_full * (grad_prob - delta_rows[:, :, None])).astype(jnp.bfloat16)
    query_gradient = (
        jnp.einsum("hqk,khd->qhd", grad_score, key_rows, preferred_element_type=jnp.float32)
        * score_scale
    )
    grad_key = (
        jnp.einsum("hqk,qhd->khd", grad_score, query_rows, preferred_element_type=jnp.float32)
        * score_scale
    )
    value_gradient = jnp.einsum(
        "hqk,qhd->khd", prob_low, grad_rows, preferred_element_type=jnp.float32
    )
    return (block_output, query_gradient, grad_key, value_gradient)


def attention_kernel(
    tiles_ref, q_ref, ek_ref, ev_ref, lk0_ref, lk1_ref, lv0_ref, lv1_ref, g_ref, m_ref, qg_ref, kg_ref,
    o_ref, dqi_ref, dke_ref, dve_ref, part_ref, gain_ref, *, scale
):
    f32 = jnp.float32
    window = ek_ref.shape[0]
    head_size = qg_ref.shape[1]
    q_gain = qg_ref[...]
    k_gain = kg_ref[...]
    keep = m_ref[...] > 0.0
    nt = (((1,), (1,)), ((), ()))
    tn = (((0,), (0,)), ((), ()))

    def normed(x_ref, cols, gain):
        x = x_ref[:, cols].astype(f32)
        inv = lax.rsqrt(jnp.mean(x * x, axis=1, keepdims=True) + NORM_EPS)
        return x, inv, (x * inv * gain).astype(jnp.bfloat16)

    for i in range(q_ref.shape[1] // head_size):
        cols = slice(i * head_size, (i + 1) * head_size)
        qx, qinv, q = normed(q_ref, cols, q_gain)
        kx, kinv, kn = normed(ek_ref, cols, k_gain)
        lx0, linv0, ln0 = normed(lk0_ref, cols, k_gain)
        lx1, linv1, ln1 = normed(lk1_ref, cols, k_gain)
        g = g_ref[:, cols]
        k = jnp.concatenate([kn, ln0, ln1], axis=0)
        v = jnp.concatenate([ev_ref[:, cols], lv0_ref[:, cols], lv1_ref[:, cols]], axis=0)
        s = lax.dot_general(q, k, nt, preferred_element_type=f32) * scale
        e = jnp.where(keep, jnp.exp(s), 0.0)
        tot = jnp.sum(e, axis=1, keepdims=True)
        p = e / tot
        p_low = p.astype(jnp.bfloat16)
        o = jnp.dot(p_low, v, preferred_element_type=f32).astype(jnp.bfloat16)
        o_ref[:, cols] = o
        delta = jnp.sum(g.astype(f32) * o.astype(f32), axis=1, keepdims=True)
        dp = lax.dot_general(g, v, nt, preferred_element_type=f32)
        ds = (p * (dp - delta)).astype(jnp.bfloat16)
        dq = jnp.dot(ds, k, preferred_element_type=f32) * scale
        dk = lax.dot_general(ds, q, tn, preferred_element_type=f32) * scale
        dv = lax.dot_general(p_low, g, tn, preferred_element_type=f32)
        scaled = dq * q_gain
        dqi_ref[:, cols] = (
            qinv * scaled - qx * qinv * qinv * qinv * jnp.mean(scaled * qx, axis=1, keepdims=True)
        ).astype(jnp.bfloat16)
        dke_ref[:, cols] = dk[:window]
        dve_ref[:, cols] = dv[:window]
        for j in range(part_ref.shape[1] // BLK):
            for c, d in enumerate((dk, dv)):
                placed = jnp.zeros((BLK, head_size), f32)
                for s_ in range(tiles_ref.shape[0]):
                    rows = d[window + s_ * BLK : window + (s_ + 1) * BLK]
                    placed = placed + jnp.where(tiles_ref[s_] == j, rows, 0.0)
                part_ref[c, j * BLK : (j + 1) * BLK, cols] = placed.astype(part_ref.dtype)
        gq = jnp.sum(dq * qx * qinv, axis=0, keepdims=True)
        gk = (
            jnp.sum(dk[:window] * kx * kinv, axis=0, keepdims=True)
            + jnp.sum(dk[window : window + BLK] * lx0 * linv0, axis=0, keepdims=True)
            + jnp.sum(dk[window + BLK :] * lx1 * linv1, axis=0, keepdims=True)
        )
        gain_ref[:, cols] = jnp.concatenate([gq, gk, jnp.zeros((6, head_size), f32)], axis=0)


def attention_block(tiles, q, ek, ev, lk, lv, g, keep, q_gain, k_gain, scale):
    lyric_rows = lk.shape[0]
    rows, width = q.shape
    head_size = q_gain.shape[0]
    window = ek.shape[0]
    slots = tiles.shape[0]
    heads = width // head_size
    f32 = jnp.float32

    per = 4 if heads % 4 == 0 else 1
    span = per * head_size

    def col(r):
        return pl.BlockSpec((r, span), lambda h, t: (0, h))

    def slot(s):
        return pl.BlockSpec((BLK, span), lambda h, t: (jnp.maximum(t[s], 0), h))

    whole = pl.BlockSpec((1, head_size), lambda h, t: (0, 0))
    grid_spec = pltpu.PrefetchScalarGridSpec(
        num_scalar_prefetch=1,
        grid=(heads // per,),
        in_specs=[col(rows), col(window), col(window), slot(0), slot(1), slot(0), slot(1), col(rows),
                  pl.BlockSpec((1, keep.shape[1]), lambda h, t: (0, 0)), whole, whole],
        out_specs=[col(rows), col(rows), col(window), col(window),
                   pl.BlockSpec((2, lyric_rows, span), lambda h, t: (0, 0, h)), col(8)],
    )
    return pl.pallas_call(
        lambda *refs: attention_kernel(*refs, scale=scale),
        grid_spec=grid_spec,
        out_shape=[
            jax.ShapeDtypeStruct((rows, width), jnp.bfloat16),
            jax.ShapeDtypeStruct((rows, width), jnp.bfloat16),
            jax.ShapeDtypeStruct((window, width), f32),
            jax.ShapeDtypeStruct((window, width), f32),
            jax.ShapeDtypeStruct((2, lyric_rows, width), jnp.bfloat16),
            jax.ShapeDtypeStruct((8, width), f32),
        ],
    )(tiles, q, ek, ev, lk, lk, lv, lv, g, keep, q_gain.reshape(1, head_size), k_gain.reshape(1, head_size))


def body(
    queries, keys, values, lyric_keys, lyric_values, q_gain, k_gain, cotangent, alignment, lyric_len
):
    head_size = q_gain.shape[0]
    model_width = queries.shape[2]
    head_count = model_width // head_size
    frames = queries.shape[1]
    lyric_local = lyric_keys.shape[1]
    seq_count = lax.axis_size("seq")
    border_rows = WIN * BLK
    window_extent = (2 * WIN + 1) * BLK
    score_scale = head_size ** (-0.5)
    total_frames = frames * seq_count
    first_frame = lax.axis_index("seq") * frames
    lyric_total = lyric_local * seq_count
    lyric_blocks = lyric_total // BLK
    masks = seq_masks(seq_count)

    lyric_pair = jnp.stack([lyric_keys[0], lyric_values[0]])
    lyric_all = gather_doubling(lyric_pair, "seq", masks[::-1])
    lyric_all = jnp.swapaxes(lyric_all, 0, 1).reshape(2, lyric_total, model_width)

    query_raw = queries[0]
    lyric_inv = norm_heads(lyric_keys[0], k_gain)[1]

    stacked = jnp.stack([keys[0], values[0]])
    extended = extended_2(stacked, (("seq", 1),), border_rows)
    key_raw = keys[0]
    key_inv = norm_heads(key_raw, k_gain)[1]
    length = lyric_len[0]

    position = first_frame - border_rows + jnp.arange(window_extent, dtype=jnp.int32)
    audio_mask = (position >= 0) & (position < total_frames)
    tile_ids = alignment[0, 0]
    tiles = jnp.maximum(tile_ids, 0)
    lyric_mask = jnp.concatenate(
        [(tile_ids[s] >= 0) & (tiles[s] * BLK + jnp.arange(BLK, dtype=jnp.int32) < length) for s in range(TILES)]
    )
    keep_mask = jnp.concatenate([audio_mask, lyric_mask], axis=0).astype(jnp.float32)[None]
    block_output, unnormed_query_gradient, ext_grad_key, ext_grad_val, parts, gain_rows = attention_block(
        tile_ids,
        query_raw,
        extended[0],
        extended[1],
        lyric_all[0],
        lyric_all[1],
        cotangent[0],
        keep_mask,
        q_gain,
        k_gain,
        score_scale,
    )
    ext_grad_key = ext_grad_key.reshape(window_extent, head_count, head_size)
    ext_grad_val = ext_grad_val.reshape(window_extent, head_count, head_size)
    gains = jnp.sum(gain_rows[:2].reshape(2, head_count, head_size), axis=1)
    summed, gains = scatter_halving(parts.reshape(2, seq_count, lyric_local, model_width), "seq", masks, gains)
    total_gains = sum_doubling(gains, ("song",))
    summed_key = summed[0].reshape(lyric_local, head_count, head_size)
    summed_val = summed[1]

    own_grad_key = ext_grad_key[border_rows : border_rows + frames]
    own_grad_val = ext_grad_val[border_rows : border_rows + frames]
    rims = jnp.stack(
        [
            jnp.concatenate(
                [ext_grad_key[:border_rows], ext_grad_key[border_rows + frames :]], axis=0
            ).reshape(2 * border_rows, model_width),
            jnp.concatenate(
                [ext_grad_val[:border_rows], ext_grad_val[border_rows + frames :]], axis=0
            ).reshape(2 * border_rows, model_width),
        ]
    )
    received = extended_2(rims.astype(jnp.bfloat16), (("seq", 1),), border_rows).astype(rims.dtype)
    from_left = received[:, :border_rows].reshape(2, border_rows, head_count, head_size)
    from_right = received[:, 3 * border_rows :].reshape(2, border_rows, head_count, head_size)
    own_grad_key = (
        own_grad_key.at[:border_rows]
        .add(from_left[0])
        .at[frames - border_rows :]
        .add(from_right[0])
    )
    own_grad_val = (
        own_grad_val.at[:border_rows]
        .add(from_left[1])
        .at[frames - border_rows :]
        .add(from_right[1])
    )
    unnormed_key_gradient = norm_back(key_raw, key_inv, k_gain, own_grad_key)[0]
    unnormed_lyric_gradient = norm_back(lyric_keys[0], lyric_inv, k_gain, summed_key)[0]
    return (
        block_output.reshape(1, frames, model_width),
        unnormed_query_gradient[None],
        unnormed_key_gradient.astype(jnp.bfloat16)[None],
        own_grad_val.reshape(1, frames, model_width).astype(jnp.bfloat16),
        unnormed_lyric_gradient.astype(jnp.bfloat16)[None],
        summed_val.astype(jnp.bfloat16)[None],
        total_gains[0],
        total_gains[1],
    )


def solution(mesh):
    in_specs = (
        P("song", "seq", None),
        P("song", "seq", None),
        P("song", "seq", None),
        P("song", "seq", None),
        P("song", "seq", None),
        P(),
        P(),
        P("song", "seq", None),
        P("song", "seq", None),
        P("song"),
    )
    out_specs = (
        P("song", "seq", None),
        P("song", "seq", None),
        P("song", "seq", None),
        P("song", "seq", None),
        P("song", "seq", None),
        P("song", "seq", None),
        P(),
        P(),
    )
    return jax.shard_map(body, mesh=mesh, in_specs=in_specs, out_specs=out_specs, check_vma=False)
```

```python
import jax
import jax.numpy as jnp
from jax import lax
from jax.sharding import PartitionSpec as P
from jax.experimental import pallas as pl
from jax.experimental.pallas import tpu as pltpu

BLK = 128
WIN = 1
TILES = 2


NORM_EPS = 1e-06


def extended_2(block, sides, width):
    for axis, dim in sides:
        count = lax.axis_size(axis)
        forward = [(i, i + 1) for i in range(count - 1)]
        backward = [(target, source) for source, target in forward]
        low = lax.ppermute(
            lax.slice_in_dim(block, block.shape[dim] - width, None, axis=dim), axis, forward
        )
        high = lax.ppermute(lax.slice_in_dim(block, 0, width, axis=dim), axis, backward)
        block = jnp.concatenate([low, block, high], axis=dim)
    return block


def seq_masks(count):
    masks = []
    m = 1
    while m < count:
        masks.append(m)
        m *= 2
    return masks


def swap_with(x, axis, mask):
    count = lax.axis_size(axis)
    return lax.ppermute(x, axis, [(i, i ^ mask) for i in range(count)])


def gather_doubling(chunk, axis, order):
    idx = lax.axis_index(axis)
    buf = chunk[None]
    for mask in order:
        other = swap_with(buf, axis, mask)
        high = (idx & mask) != 0
        buf = jnp.where(high, jnp.concatenate([other, buf]), jnp.concatenate([buf, other]))
    steps = len(order)
    buf = buf.reshape((2,) * steps + chunk.shape)
    held = [order[steps - 1 - k] for k in range(steps)]
    perm = sorted(range(steps), key=lambda k: -held[k])
    buf = jnp.transpose(buf, perm + list(range(steps, buf.ndim)))
    return buf.reshape((2 ** steps,) + chunk.shape)


def scatter_halving(parts, axis, order, rider):
    idx = lax.axis_index(axis)
    steps = len(order)
    buf = parts.reshape(parts.shape[:1] + (2,) * steps + parts.shape[2:])
    held = sorted(order, reverse=True)
    for step, mask in enumerate(order):
        a = held.index(mask) + 1
        high = ((idx & mask) != 0).astype(jnp.int32)
        if step:
            rider, buf = lax.optimization_barrier((rider, buf))
        keep = lax.dynamic_index_in_dim(buf, high, axis=a, keepdims=False)
        send = lax.dynamic_index_in_dim(buf, 1 - high, axis=a, keepdims=False)
        got, other = swap_with((send.astype(jnp.bfloat16), rider), axis, mask)
        buf = keep.astype(jnp.float32) + got.astype(jnp.float32)
        rider = rider + other
        held.pop(a - 1)
    return buf, rider


def sum_doubling(x, axes):
    for axis in axes:
        for mask in seq_masks(lax.axis_size(axis)):
            x = x + swap_with(x, axis, mask)
    return x


def norm_heads(inputs, norm_gain):
    row_values = inputs.astype(jnp.float32).reshape(inputs.shape[0], -1, norm_gain.shape[0])
    inverse = lax.rsqrt(jnp.mean(row_values * row_values, axis=-1, keepdims=True) + NORM_EPS)
    return (row_values * inverse * norm_gain, inverse)


def norm_back(inputs, inverse, norm_gain, grad_out):
    row_values = inputs.astype(jnp.float32).reshape(grad_out.shape)
    scaled = grad_out * norm_gain
    grad_input = inverse * scaled - row_values * inverse * inverse * inverse * jnp.mean(
        scaled * row_values, axis=-1, keepdims=True
    )
    grad_gain = jnp.sum(grad_out * row_values * inverse, axis=(0, 1))
    return (grad_input.reshape(inputs.shape), grad_gain)


def block_pass(query_rows, key_rows, value_rows, keep_mask, grad_rows, score_scale):
    scores = (
        jnp.einsum("qhd,khd->hqk", query_rows, key_rows, preferred_element_type=jnp.float32)
        * score_scale
    )
    exp_scores = jnp.where(keep_mask[None, None, :], jnp.exp(scores), 0.0)
    totals = jnp.sum(exp_scores, axis=2)
    prob_full = exp_scores / totals[:, :, None]
    prob_low = prob_full.astype(jnp.bfloat16)
    block_output = jnp.einsum(
        "hqk,khd->qhd", prob_low, value_rows, preferred_element_type=jnp.float32
    ).astype(jnp.bfloat16)
    delta_rows = jnp.sum(grad_rows.astype(jnp.float32) * block_output.astype(jnp.float32), axis=2).T
    grad_prob = jnp.einsum(
        "qhd,khd->hqk", grad_rows, value_rows, preferred_element_type=jnp.float32
    )
    grad_score = (prob_full * (grad_prob - delta_rows[:, :, None])).astype(jnp.bfloat16)
    query_gradient = (
        jnp.einsum("hqk,khd->qhd", grad_score, key_rows, preferred_element_type=jnp.float32)
        * score_scale
    )
    grad_key = (
        jnp.einsum("hqk,qhd->khd", grad_score, query_rows, preferred_element_type=jnp.float32)
        * score_scale
    )
    value_gradient = jnp.einsum(
        "hqk,qhd->khd", prob_low, grad_rows, preferred_element_type=jnp.float32
    )
    return (block_output, query_gradient, grad_key, value_gradient)


def attention_kernel(
    tiles_ref, q_ref, ek_ref, ev_ref, lk0_ref, lk1_ref, lv0_ref, lv1_ref, g_ref, m_ref, qg_ref, kg_ref,
    o_ref, dqi_ref, dke_ref, dve_ref, part_ref, gain_ref, *, scale
):
    f32 = jnp.float32
    window = ek_ref.shape[0]
    head_size = qg_ref.shape[1]
    q_gain = qg_ref[...]
    k_gain = kg_ref[...]
    keep = m_ref[...] > 0.0
    nt = (((1,), (1,)), ((), ()))
    tn = (((0,), (0,)), ((), ()))

    def normed(x_ref, cols, gain):
        x = x_ref[:, cols].astype(f32)
        inv = lax.rsqrt(jnp.mean(x * x, axis=1, keepdims=True) + NORM_EPS)
        return x, inv, (x * inv * gain).astype(jnp.bfloat16)

    for i in range(q_ref.shape[1] // head_size):
        cols = slice(i * head_size, (i + 1) * head_size)
        qx, qinv, q = normed(q_ref, cols, q_gain)
        kx, kinv, kn = normed(ek_ref, cols, k_gain)
        lx0, linv0, ln0 = normed(lk0_ref, cols, k_gain)
        lx1, linv1, ln1 = normed(lk1_ref, cols, k_gain)
        g = g_ref[:, cols]
        k = jnp.concatenate([kn, ln0, ln1], axis=0)
        v = jnp.concatenate([ev_ref[:, cols], lv0_ref[:, cols], lv1_ref[:, cols]], axis=0)
        s = lax.dot_general(q, k, nt, preferred_element_type=f32) * scale
        e = jnp.where(keep, jnp.exp(s), 0.0)
        tot = jnp.sum(e, axis=1, keepdims=True)
        p = e / tot
        p_low = p.astype(jnp.bfloat16)
        o = jnp.dot(p_low, v, preferred_element_type=f32).astype(jnp.bfloat16)
        o_ref[:, cols] = o
        delta = jnp.sum(g.astype(f32) * o.astype(f32), axis=1, keepdims=True)
        dp = lax.dot_general(g, v, nt, preferred_element_type=f32)
        ds = (p * (dp - delta)).astype(jnp.bfloat16)
        dq = jnp.dot(ds, k, preferred_element_type=f32) * scale
        dk = lax.dot_general(ds, q, tn, preferred_element_type=f32) * scale
        dv = lax.dot_general(p_low, g, tn, preferred_element_type=f32)
        scaled = dq * q_gain
        dqi_ref[:, cols] = (
            qinv * scaled - qx * qinv * qinv * qinv * jnp.mean(scaled * qx, axis=1, keepdims=True)
        ).astype(jnp.bfloat16)
        dke_ref[:, cols] = dk[:window]
        dve_ref[:, cols] = dv[:window]
        for j in range(part_ref.shape[1] // BLK):
            for c, d in enumerate((dk, dv)):
                placed = jnp.zeros((BLK, head_size), f32)
                for s_ in range(tiles_ref.shape[0]):
                    rows = d[window + s_ * BLK : window + (s_ + 1) * BLK]
                    placed = placed + jnp.where(tiles_ref[s_] == j, rows, 0.0)
                part_ref[c, j * BLK : (j + 1) * BLK, cols] = placed.astype(part_ref.dtype)
        gq = jnp.sum(dq * qx * qinv, axis=0, keepdims=True)
        gk = (
            jnp.sum(dk[:window] * kx * kinv, axis=0, keepdims=True)
            + jnp.sum(dk[window : window + BLK] * lx0 * linv0, axis=0, keepdims=True)
            + jnp.sum(dk[window + BLK :] * lx1 * linv1, axis=0, keepdims=True)
        )
        gain_ref[:, cols] = jnp.concatenate([gq, gk, jnp.zeros((6, head_size), f32)], axis=0)


def attention_block(tiles, q, ek, ev, lk, lv, g, keep, q_gain, k_gain, scale):
    lyric_rows = lk.shape[0]
    rows, width = q.shape
    head_size = q_gain.shape[0]
    window = ek.shape[0]
    slots = tiles.shape[0]
    heads = width // head_size
    f32 = jnp.float32

    per = 4 if heads % 4 == 0 else 1
    span = per * head_size

    def col(r):
        return pl.BlockSpec((r, span), lambda h, t: (0, h))

    def slot(s):
        return pl.BlockSpec((BLK, span), lambda h, t: (jnp.maximum(t[s], 0), h))

    whole = pl.BlockSpec((1, head_size), lambda h, t: (0, 0))
    grid_spec = pltpu.PrefetchScalarGridSpec(
        num_scalar_prefetch=1,
        grid=(heads // per,),
        in_specs=[col(rows), col(window), col(window), slot(0), slot(1), slot(0), slot(1), col(rows),
                  pl.BlockSpec((1, keep.shape[1]), lambda h, t: (0, 0)), whole, whole],
        out_specs=[col(rows), col(rows), col(window), col(window),
                   pl.BlockSpec((2, lyric_rows, span), lambda h, t: (0, 0, h)), col(8)],
    )
    return pl.pallas_call(
        lambda *refs: attention_kernel(*refs, scale=scale),
        grid_spec=grid_spec,
        out_shape=[
            jax.ShapeDtypeStruct((rows, width), jnp.bfloat16),
            jax.ShapeDtypeStruct((rows, width), jnp.bfloat16),
            jax.ShapeDtypeStruct((window, width), f32),
            jax.ShapeDtypeStruct((window, width), f32),
            jax.ShapeDtypeStruct((2, lyric_rows, width), jnp.bfloat16),
            jax.ShapeDtypeStruct((8, width), f32),
        ],
    )(tiles, q, ek, ev, lk, lk, lv, lv, g, keep, q_gain.reshape(1, head_size), k_gain.reshape(1, head_size))


def body(
    queries, keys, values, lyric_keys, lyric_values, q_gain, k_gain, cotangent, alignment, lyric_len
):
    head_size = q_gain.shape[0]
    model_width = queries.shape[2]
    head_count = model_width // head_size
    frames = queries.shape[1]
    lyric_local = lyric_keys.shape[1]
    seq_count = lax.axis_size("seq")
    border_rows = WIN * BLK
    window_extent = (2 * WIN + 1) * BLK
    score_scale = head_size ** (-0.5)
    total_frames = frames * seq_count
    first_frame = lax.axis_index("seq") * frames
    lyric_total = lyric_local * seq_count
    lyric_blocks = lyric_total // BLK
    masks = seq_masks(seq_count)

    lyric_pair = jnp.stack([lyric_keys[0], lyric_values[0]])
    lyric_all = gather_doubling(lyric_pair, "seq", masks[::-1])
    lyric_all = jnp.swapaxes(lyric_all, 0, 1).reshape(2, lyric_total, model_width)

    query_raw = queries[0]
    lyric_inv = norm_heads(lyric_keys[0], k_gain)[1]

    stacked = jnp.stack([keys[0], values[0]])
    extended = extended_2(stacked, (("seq", 1),), border_rows)
    key_raw = keys[0]
    key_inv = norm_heads(key_raw, k_gain)[1]
    length = lyric_len[0]

    position = first_frame - border_rows + jnp.arange(window_extent, dtype=jnp.int32)
    audio_mask = (position >= 0) & (position < total_frames)
    tile_ids = alignment[0, 0]
    tiles = jnp.maximum(tile_ids, 0)
    lyric_mask = jnp.concatenate(
        [(tile_ids[s] >= 0) & (tiles[s] * BLK + jnp.arange(BLK, dtype=jnp.int32) < length) for s in range(TILES)]
    )
    keep_mask = jnp.concatenate([audio_mask, lyric_mask], axis=0).astype(jnp.float32)[None]
    block_output, unnormed_query_gradient, ext_grad_key, ext_grad_val, parts, gain_rows = attention_block(
        tile_ids,
        query_raw,
        extended[0],
        extended[1],
        lyric_all[0],
        lyric_all[1],
        cotangent[0],
        keep_mask,
        q_gain,
        k_gain,
        score_scale,
    )
    ext_grad_key = ext_grad_key.reshape(window_extent, head_count, head_size)
    ext_grad_val = ext_grad_val.reshape(window_extent, head_count, head_size)
    gains = jnp.sum(gain_rows[:2].reshape(2, head_count, head_size), axis=1)
    summed, gains = scatter_halving(parts.reshape(2, seq_count, lyric_local, model_width), "seq", masks, gains)
    total_gains = sum_doubling(gains, ("song",))
    summed_key = summed[0].reshape(lyric_local, head_count, head_size)
    summed_val = summed[1]

    own_grad_key = ext_grad_key[border_rows : border_rows + frames]
    own_grad_val = ext_grad_val[border_rows : border_rows + frames]
    rims = jnp.stack(
        [
            jnp.concatenate(
                [ext_grad_key[:border_rows], ext_grad_key[border_rows + frames :]], axis=0
            ).reshape(2 * border_rows, model_width),
            jnp.concatenate(
                [ext_grad_val[:border_rows], ext_grad_val[border_rows + frames :]], axis=0
            ).reshape(2 * border_rows, model_width),
        ]
    )
    received = extended_2(rims.astype(jnp.bfloat16), (("seq", 1),), border_rows).astype(rims.dtype)
    from_left = received[:, :border_rows].reshape(2, border_rows, head_count, head_size)
    from_right = received[:, 3 * border_rows :].reshape(2, border_rows, head_count, head_size)
    own_grad_key = (
        own_grad_key.at[:border_rows]
        .add(from_left[0])
        .at[frames - border_rows :]
        .add(from_right[0])
    )
    own_grad_val = (
        own_grad_val.at[:border_rows]
        .add(from_left[1])
        .at[frames - border_rows :]
        .add(from_right[1])
    )
    unnormed_key_gradient = norm_back(key_raw, key_inv, k_gain, own_grad_key)[0]
    unnormed_lyric_gradient = norm_back(lyric_keys[0], lyric_inv, k_gain, summed_key)[0]
    return (
        block_output.reshape(1, frames, model_width),
        unnormed_query_gradient[None],
        unnormed_key_gradient.astype(jnp.bfloat16)[None],
        own_grad_val.reshape(1, frames, model_width).astype(jnp.bfloat16),
        unnormed_lyric_gradient.astype(jnp.bfloat16)[None],
        summed_val.astype(jnp.bfloat16)[None],
        total_gains[0],
        total_gains[1],
    )


def solution(mesh):
    in_specs = (
        P("song", "seq", None),
        P("song", "seq", None),
        P("song", "seq", None),
        P("song", "seq", None),
        P("song", "seq", None),
        P(),
        P(),
        P("song", "seq", None),
        P("song", "seq", None),
        P("song"),
    )
    out_specs = (
        P("song", "seq", None),
        P("song", "seq", None),
        P("song", "seq", None),
        P("song", "seq", None),
        P("song", "seq", None),
        P("song", "seq", None),
        P(),
        P(),
    )
    return jax.shard_map(body, mesh=mesh, in_specs=in_specs, out_specs=out_specs, check_vma=False)
```

```python
import jax
import jax.numpy as jnp
from jax import lax
from jax.sharding import PartitionSpec as P
from jax.experimental import pallas as pl
from jax.experimental.pallas import tpu as pltpu

BLK = 128
WIN = 1
TILES = 2


NORM_EPS = 1e-06


def extended_2(block, sides, width):
    for axis, dim in sides:
        count = lax.axis_size(axis)
        forward = [(i, i + 1) for i in range(count - 1)]
        backward = [(target, source) for source, target in forward]
        low = lax.ppermute(
            lax.slice_in_dim(block, block.shape[dim] - width, None, axis=dim), axis, forward
        )
        high = lax.ppermute(lax.slice_in_dim(block, 0, width, axis=dim), axis, backward)
        block = jnp.concatenate([low, block, high], axis=dim)
    return block


def seq_masks(count):
    masks = []
    m = 1
    while m < count:
        masks.append(m)
        m *= 2
    return masks


def swap_with(x, axis, mask):
    count = lax.axis_size(axis)
    return lax.ppermute(x, axis, [(i, i ^ mask) for i in range(count)])


def gather_doubling(chunk, axis, order):
    idx = lax.axis_index(axis)
    buf = chunk[None]
    for mask in order:
        other = swap_with(buf, axis, mask)
        high = (idx & mask) != 0
        buf = jnp.where(high, jnp.concatenate([other, buf]), jnp.concatenate([buf, other]))
    steps = len(order)
    buf = buf.reshape((2,) * steps + chunk.shape)
    held = [order[steps - 1 - k] for k in range(steps)]
    perm = sorted(range(steps), key=lambda k: -held[k])
    buf = jnp.transpose(buf, perm + list(range(steps, buf.ndim)))
    return buf.reshape((2 ** steps,) + chunk.shape)


def scatter_halving(parts, axis, order, rider):
    idx = lax.axis_index(axis)
    steps = len(order)
    buf = parts.reshape(parts.shape[:1] + (2,) * steps + parts.shape[2:])

    def halve(buf, held, mask):
        a = held.index(mask) + 1
        high = ((idx & mask) != 0).astype(jnp.int32)
        keep = lax.dynamic_index_in_dim(buf, high, axis=a, keepdims=False)
        send = lax.dynamic_index_in_dim(buf, 1 - high, axis=a, keepdims=False)
        return keep, send, [m for m in held if m != mask]

    def add(keep, got):
        return keep.astype(jnp.float32) + got.astype(jnp.float32)

    held = sorted(order, reverse=True)
    plan = [[order[0]]]
    rest = list(order[1:])
    if len(rest) >= 3:
        plan += [[rest[0], rest[2]], [rest[2], rest[0]]]
        rest = [rest[1]] + rest[3:]
    plan += [[m] for m in rest]
    for step, masks in enumerate(plan):
        if step:
            rider, buf = lax.optimization_barrier((rider, buf))
        if len(masks) == 1:
            keep, send, held = halve(buf, held, masks[0])
            got, other = swap_with((send.astype(jnp.bfloat16), rider), axis, masks[0])
            buf = add(keep, got)
        else:
            width = buf.shape[-1] // 2
            halves = [buf[..., :width], buf[..., width:]]
            if step == 1:
                chains = []
                for part, mask in zip(halves, masks):
                    keep, send, part_held = halve(part, held, mask)
                    chains.append((keep, send, part_held, mask))
            else:
                chains = []
                for part, mask, (_, _, part_held, _) in zip(halves, masks, last):
                    keep, send, part_held = halve(part, part_held, mask)
                    chains.append((keep, send, part_held, mask))
            got0, other = swap_with((chains[0][1].astype(jnp.bfloat16), rider), axis, chains[0][3])
            got1 = swap_with(chains[1][1].astype(jnp.bfloat16), axis, chains[1][3])
            buf = jnp.concatenate([add(chains[0][0], got0), add(chains[1][0], got1)], axis=-1)
            last = chains
            held = chains[0][2]
        rider = rider + other
    return buf, rider


def sum_doubling(x, axes):
    for axis in axes:
        for mask in seq_masks(lax.axis_size(axis)):
            x = x + swap_with(x, axis, mask)
    return x


def norm_heads(inputs, norm_gain):
    row_values = inputs.astype(jnp.float32).reshape(inputs.shape[0], -1, norm_gain.shape[0])
    inverse = lax.rsqrt(jnp.mean(row_values * row_values, axis=-1, keepdims=True) + NORM_EPS)
    return (row_values * inverse * norm_gain, inverse)


def norm_back(inputs, inverse, norm_gain, grad_out):
    row_values = inputs.astype(jnp.float32).reshape(grad_out.shape)
    scaled = grad_out * norm_gain
    grad_input = inverse * scaled - row_values * inverse * inverse * inverse * jnp.mean(
        scaled * row_values, axis=-1, keepdims=True
    )
    grad_gain = jnp.sum(grad_out * row_values * inverse, axis=(0, 1))
    return (grad_input.reshape(inputs.shape), grad_gain)


def block_pass(query_rows, key_rows, value_rows, keep_mask, grad_rows, score_scale):
    scores = (
        jnp.einsum("qhd,khd->hqk", query_rows, key_rows, preferred_element_type=jnp.float32)
        * score_scale
    )
    exp_scores = jnp.where(keep_mask[None, None, :], jnp.exp(scores), 0.0)
    totals = jnp.sum(exp_scores, axis=2)
    prob_full = exp_scores / totals[:, :, None]
    prob_low = prob_full.astype(jnp.bfloat16)
    block_output = jnp.einsum(
        "hqk,khd->qhd", prob_low, value_rows, preferred_element_type=jnp.float32
    ).astype(jnp.bfloat16)
    delta_rows = jnp.sum(grad_rows.astype(jnp.float32) * block_output.astype(jnp.float32), axis=2).T
    grad_prob = jnp.einsum(
        "qhd,khd->hqk", grad_rows, value_rows, preferred_element_type=jnp.float32
    )
    grad_score = (prob_full * (grad_prob - delta_rows[:, :, None])).astype(jnp.bfloat16)
    query_gradient = (
        jnp.einsum("hqk,khd->qhd", grad_score, key_rows, preferred_element_type=jnp.float32)
        * score_scale
    )
    grad_key = (
        jnp.einsum("hqk,qhd->khd", grad_score, query_rows, preferred_element_type=jnp.float32)
        * score_scale
    )
    value_gradient = jnp.einsum(
        "hqk,qhd->khd", prob_low, grad_rows, preferred_element_type=jnp.float32
    )
    return (block_output, query_gradient, grad_key, value_gradient)


def attention_kernel(
    tiles_ref, q_ref, ek_ref, ev_ref, lk0_ref, lk1_ref, lv0_ref, lv1_ref, g_ref, m_ref, qg_ref, kg_ref,
    o_ref, dqi_ref, dke_ref, dve_ref, part_ref, gain_ref, *, scale
):
    f32 = jnp.float32
    window = ek_ref.shape[0]
    head_size = qg_ref.shape[1]
    q_gain = qg_ref[...]
    k_gain = kg_ref[...]
    keep = m_ref[...] > 0.0
    nt = (((1,), (1,)), ((), ()))
    tn = (((0,), (0,)), ((), ()))

    def normed(x_ref, cols, gain):
        x = x_ref[:, cols].astype(f32)
        inv = lax.rsqrt(jnp.mean(x * x, axis=1, keepdims=True) + NORM_EPS)
        return x, inv, (x * inv * gain).astype(jnp.bfloat16)

    for i in range(q_ref.shape[1] // head_size):
        cols = slice(i * head_size, (i + 1) * head_size)
        qx, qinv, q = normed(q_ref, cols, q_gain)
        kx, kinv, kn = normed(ek_ref, cols, k_gain)
        lx0, linv0, ln0 = normed(lk0_ref, cols, k_gain)
        lx1, linv1, ln1 = normed(lk1_ref, cols, k_gain)
        g = g_ref[:, cols]
        k = jnp.concatenate([kn, ln0, ln1], axis=0)
        v = jnp.concatenate([ev_ref[:, cols], lv0_ref[:, cols], lv1_ref[:, cols]], axis=0)
        s = lax.dot_general(q, k, nt, preferred_element_type=f32) * scale
        e = jnp.where(keep, jnp.exp(s), 0.0)
        tot = jnp.sum(e, axis=1, keepdims=True)
        p = e / tot
        p_low = p.astype(jnp.bfloat16)
        o = jnp.dot(p_low, v, preferred_element_type=f32).astype(jnp.bfloat16)
        o_ref[:, cols] = o
        delta = jnp.sum(g.astype(f32) * o.astype(f32), axis=1, keepdims=True)
        dp = lax.dot_general(g, v, nt, preferred_element_type=f32)
        ds = (p * (dp - delta)).astype(jnp.bfloat16)
        dq = jnp.dot(ds, k, preferred_element_type=f32) * scale
        dk = lax.dot_general(ds, q, tn, preferred_element_type=f32) * scale
        dv = lax.dot_general(p_low, g, tn, preferred_element_type=f32)
        scaled = dq * q_gain
        dqi_ref[:, cols] = (
            qinv * scaled - qx * qinv * qinv * qinv * jnp.mean(scaled * qx, axis=1, keepdims=True)
        ).astype(jnp.bfloat16)
        dke_ref[:, cols] = dk[:window]
        dve_ref[:, cols] = dv[:window]
        for j in range(part_ref.shape[1] // BLK):
            for c, d in enumerate((dk, dv)):
                placed = jnp.zeros((BLK, head_size), f32)
                for s_ in range(tiles_ref.shape[0]):
                    rows = d[window + s_ * BLK : window + (s_ + 1) * BLK]
                    placed = placed + jnp.where(tiles_ref[s_] == j, rows, 0.0)
                part_ref[c, j * BLK : (j + 1) * BLK, cols] = placed.astype(part_ref.dtype)
        gq = jnp.sum(dq * qx * qinv, axis=0, keepdims=True)
        gk = (
            jnp.sum(dk[:window] * kx * kinv, axis=0, keepdims=True)
            + jnp.sum(dk[window : window + BLK] * lx0 * linv0, axis=0, keepdims=True)
            + jnp.sum(dk[window + BLK :] * lx1 * linv1, axis=0, keepdims=True)
        )
        gain_ref[:, cols] = jnp.concatenate([gq, gk, jnp.zeros((6, head_size), f32)], axis=0)


def attention_block(tiles, q, ek, ev, lk, lv, g, keep, q_gain, k_gain, scale):
    lyric_rows = lk.shape[0]
    rows, width = q.shape
    head_size = q_gain.shape[0]
    window = ek.shape[0]
    slots = tiles.shape[0]
    heads = width // head_size
    f32 = jnp.float32

    per = 4 if heads % 4 == 0 else 1
    span = per * head_size

    def col(r):
        return pl.BlockSpec((r, span), lambda h, t: (0, h))

    def slot(s):
        return pl.BlockSpec((BLK, span), lambda h, t: (jnp.maximum(t[s], 0), h))

    whole = pl.BlockSpec((1, head_size), lambda h, t: (0, 0))
    grid_spec = pltpu.PrefetchScalarGridSpec(
        num_scalar_prefetch=1,
        grid=(heads // per,),
        in_specs=[col(rows), col(window), col(window), slot(0), slot(1), slot(0), slot(1), col(rows),
                  pl.BlockSpec((1, keep.shape[1]), lambda h, t: (0, 0)), whole, whole],
        out_specs=[col(rows), col(rows), col(window), col(window),
                   pl.BlockSpec((2, lyric_rows, span), lambda h, t: (0, 0, h)), col(8)],
    )
    return pl.pallas_call(
        lambda *refs: attention_kernel(*refs, scale=scale),
        grid_spec=grid_spec,
        out_shape=[
            jax.ShapeDtypeStruct((rows, width), jnp.bfloat16),
            jax.ShapeDtypeStruct((rows, width), jnp.bfloat16),
            jax.ShapeDtypeStruct((window, width), f32),
            jax.ShapeDtypeStruct((window, width), f32),
            jax.ShapeDtypeStruct((2, lyric_rows, width), jnp.bfloat16),
            jax.ShapeDtypeStruct((8, width), f32),
        ],
    )(tiles, q, ek, ev, lk, lk, lv, lv, g, keep, q_gain.reshape(1, head_size), k_gain.reshape(1, head_size))


def body(
    queries, keys, values, lyric_keys, lyric_values, q_gain, k_gain, cotangent, alignment, lyric_len
):
    head_size = q_gain.shape[0]
    model_width = queries.shape[2]
    head_count = model_width // head_size
    frames = queries.shape[1]
    lyric_local = lyric_keys.shape[1]
    seq_count = lax.axis_size("seq")
    border_rows = WIN * BLK
    window_extent = (2 * WIN + 1) * BLK
    score_scale = head_size ** (-0.5)
    total_frames = frames * seq_count
    first_frame = lax.axis_index("seq") * frames
    lyric_total = lyric_local * seq_count
    lyric_blocks = lyric_total // BLK
    masks = seq_masks(seq_count)

    lyric_pair = jnp.stack([lyric_keys[0], lyric_values[0]])
    lyric_all = gather_doubling(lyric_pair, "seq", masks[::-1])
    lyric_all = jnp.swapaxes(lyric_all, 0, 1).reshape(2, lyric_total, model_width)

    query_raw = queries[0]
    lyric_inv = norm_heads(lyric_keys[0], k_gain)[1]

    stacked = jnp.stack([keys[0], values[0]])
    extended = extended_2(stacked, (("seq", 1),), border_rows)
    key_raw = keys[0]
    key_inv = norm_heads(key_raw, k_gain)[1]
    length = lyric_len[0]

    position = first_frame - border_rows + jnp.arange(window_extent, dtype=jnp.int32)
    audio_mask = (position >= 0) & (position < total_frames)
    tile_ids = alignment[0, 0]
    tiles = jnp.maximum(tile_ids, 0)
    lyric_mask = jnp.concatenate(
        [(tile_ids[s] >= 0) & (tiles[s] * BLK + jnp.arange(BLK, dtype=jnp.int32) < length) for s in range(TILES)]
    )
    keep_mask = jnp.concatenate([audio_mask, lyric_mask], axis=0).astype(jnp.float32)[None]
    block_output, unnormed_query_gradient, ext_grad_key, ext_grad_val, parts, gain_rows = attention_block(
        tile_ids,
        query_raw,
        extended[0],
        extended[1],
        lyric_all[0],
        lyric_all[1],
        cotangent[0],
        keep_mask,
        q_gain,
        k_gain,
        score_scale,
    )
    ext_grad_key = ext_grad_key.reshape(window_extent, head_count, head_size)
    ext_grad_val = ext_grad_val.reshape(window_extent, head_count, head_size)
    gains = jnp.sum(gain_rows[:2].reshape(2, head_count, head_size), axis=1)
    summed, gains = scatter_halving(parts.reshape(2, seq_count, lyric_local, model_width), "seq", masks, gains)
    total_gains = sum_doubling(gains, ("song",))
    summed_key = summed[0].reshape(lyric_local, head_count, head_size)
    summed_val = summed[1]

    own_grad_key = ext_grad_key[border_rows : border_rows + frames]
    own_grad_val = ext_grad_val[border_rows : border_rows + frames]
    rims = jnp.stack(
        [
            jnp.concatenate(
                [ext_grad_key[:border_rows], ext_grad_key[border_rows + frames :]], axis=0
            ).reshape(2 * border_rows, model_width),
            jnp.concatenate(
                [ext_grad_val[:border_rows], ext_grad_val[border_rows + frames :]], axis=0
            ).reshape(2 * border_rows, model_width),
        ]
    )
    received = extended_2(rims.astype(jnp.bfloat16), (("seq", 1),), border_rows).astype(rims.dtype)
    from_left = received[:, :border_rows].reshape(2, border_rows, head_count, head_size)
    from_right = received[:, 3 * border_rows :].reshape(2, border_rows, head_count, head_size)
    own_grad_key = (
        own_grad_key.at[:border_rows]
        .add(from_left[0])
        .at[frames - border_rows :]
        .add(from_right[0])
    )
    own_grad_val = (
        own_grad_val.at[:border_rows]
        .add(from_left[1])
        .at[frames - border_rows :]
        .add(from_right[1])
    )
    unnormed_key_gradient = norm_back(key_raw, key_inv, k_gain, own_grad_key)[0]
    unnormed_lyric_gradient = norm_back(lyric_keys[0], lyric_inv, k_gain, summed_key)[0]
    return (
        block_output.reshape(1, frames, model_width),
        unnormed_query_gradient[None],
        unnormed_key_gradient.astype(jnp.bfloat16)[None],
        own_grad_val.reshape(1, frames, model_width).astype(jnp.bfloat16),
        unnormed_lyric_gradient.astype(jnp.bfloat16)[None],
        summed_val.astype(jnp.bfloat16)[None],
        total_gains[0],
        total_gains[1],
    )


def solution(mesh):
    in_specs = (
        P("song", "seq", None),
        P("song", "seq", None),
        P("song", "seq", None),
        P("song", "seq", None),
        P("song", "seq", None),
        P(),
        P(),
        P("song", "seq", None),
        P("song", "seq", None),
        P("song"),
    )
    out_specs = (
        P("song", "seq", None),
        P("song", "seq", None),
        P("song", "seq", None),
        P("song", "seq", None),
        P("song", "seq", None),
        P("song", "seq", None),
        P(),
        P(),
    )
    return jax.shard_map(body, mesh=mesh, in_specs=in_specs, out_specs=out_specs, check_vma=False)
```

```python
import jax
import jax.numpy as jnp
from jax import lax
from jax.sharding import PartitionSpec as P
from jax.experimental import pallas as pl
from jax.experimental.pallas import tpu as pltpu

BLK = 128
WIN = 1
TILES = 2


NORM_EPS = 1e-06


def extended_2(block, sides, width):
    for axis, dim in sides:
        count = lax.axis_size(axis)
        forward = [(i, i + 1) for i in range(count - 1)]
        backward = [(target, source) for source, target in forward]
        low = lax.ppermute(
            lax.slice_in_dim(block, block.shape[dim] - width, None, axis=dim), axis, forward
        )
        high = lax.ppermute(lax.slice_in_dim(block, 0, width, axis=dim), axis, backward)
        block = jnp.concatenate([low, block, high], axis=dim)
    return block


def seq_masks(count):
    masks = []
    m = 1
    while m < count:
        masks.append(m)
        m *= 2
    return masks


def swap_with(x, axis, mask):
    count = lax.axis_size(axis)
    return lax.ppermute(x, axis, [(i, i ^ mask) for i in range(count)])


def gather_doubling(chunk, axis, order):
    idx = lax.axis_index(axis)
    buf = chunk[None]
    for mask in order:
        other = swap_with(buf, axis, mask)
        high = (idx & mask) != 0
        buf = jnp.where(high, jnp.concatenate([other, buf]), jnp.concatenate([buf, other]))
    steps = len(order)
    buf = buf.reshape((2,) * steps + chunk.shape)
    held = [order[steps - 1 - k] for k in range(steps)]
    perm = sorted(range(steps), key=lambda k: -held[k])
    buf = jnp.transpose(buf, perm + list(range(steps, buf.ndim)))
    return buf.reshape((2 ** steps,) + chunk.shape)


def scatter_halving(parts, axis, order, rider):
    idx = lax.axis_index(axis)
    steps = len(order)
    buf = parts.reshape(parts.shape[:1] + (2,) * steps + parts.shape[2:])
    held = sorted(order, reverse=True)
    for mask in order:
        a = held.index(mask) + 1
        high = ((idx & mask) != 0).astype(jnp.int32)
        keep = lax.dynamic_index_in_dim(buf, high, axis=a, keepdims=False)
        send = lax.dynamic_index_in_dim(buf, 1 - high, axis=a, keepdims=False)
        got, other = swap_with((send.astype(jnp.bfloat16), rider), axis, mask)
        buf = keep.astype(jnp.float32) + got.astype(jnp.float32)
        rider = rider + other
        held.pop(a - 1)
    return buf, rider


def sum_doubling(x, axes):
    for axis in axes:
        for mask in seq_masks(lax.axis_size(axis)):
            x = x + swap_with(x, axis, mask)
    return x


def norm_heads(inputs, norm_gain):
    row_values = inputs.astype(jnp.float32).reshape(inputs.shape[0], -1, norm_gain.shape[0])
    inverse = lax.rsqrt(jnp.mean(row_values * row_values, axis=-1, keepdims=True) + NORM_EPS)
    return (row_values * inverse * norm_gain, inverse)


def norm_back(inputs, inverse, norm_gain, grad_out):
    row_values = inputs.astype(jnp.float32).reshape(grad_out.shape)
    scaled = grad_out * norm_gain
    grad_input = inverse * scaled - row_values * inverse * inverse * inverse * jnp.mean(
        scaled * row_values, axis=-1, keepdims=True
    )
    grad_gain = jnp.sum(grad_out * row_values * inverse, axis=(0, 1))
    return (grad_input.reshape(inputs.shape), grad_gain)


def block_pass(query_rows, key_rows, value_rows, keep_mask, grad_rows, score_scale):
    scores = (
        jnp.einsum("qhd,khd->hqk", query_rows, key_rows, preferred_element_type=jnp.float32)
        * score_scale
    )
    exp_scores = jnp.where(keep_mask[None, None, :], jnp.exp(scores), 0.0)
    totals = jnp.sum(exp_scores, axis=2)
    prob_full = exp_scores / totals[:, :, None]
    prob_low = prob_full.astype(jnp.bfloat16)
    block_output = jnp.einsum(
        "hqk,khd->qhd", prob_low, value_rows, preferred_element_type=jnp.float32
    ).astype(jnp.bfloat16)
    delta_rows = jnp.sum(grad_rows.astype(jnp.float32) * block_output.astype(jnp.float32), axis=2).T
    grad_prob = jnp.einsum(
        "qhd,khd->hqk", grad_rows, value_rows, preferred_element_type=jnp.float32
    )
    grad_score = (prob_full * (grad_prob - delta_rows[:, :, None])).astype(jnp.bfloat16)
    query_gradient = (
        jnp.einsum("hqk,khd->qhd", grad_score, key_rows, preferred_element_type=jnp.float32)
        * score_scale
    )
    grad_key = (
        jnp.einsum("hqk,qhd->khd", grad_score, query_rows, preferred_element_type=jnp.float32)
        * score_scale
    )
    value_gradient = jnp.einsum(
        "hqk,qhd->khd", prob_low, grad_rows, preferred_element_type=jnp.float32
    )
    return (block_output, query_gradient, grad_key, value_gradient)


def attention_kernel(
    tiles_ref, q_ref, ek_ref, ev_ref, lk0_ref, lk1_ref, lv0_ref, lv1_ref, g_ref, m_ref, qg_ref, kg_ref,
    o_ref, dqi_ref, dke_ref, dve_ref, part_ref, gain_ref, *, scale
):
    f32 = jnp.float32
    window = ek_ref.shape[0]
    head_size = qg_ref.shape[1]
    q_gain = qg_ref[...]
    k_gain = kg_ref[...]
    keep = m_ref[...] > 0.0
    nt = (((1,), (1,)), ((), ()))
    tn = (((0,), (0,)), ((), ()))

    def normed(x_ref, cols, gain):
        x = x_ref[:, cols].astype(f32)
        inv = lax.rsqrt(jnp.mean(x * x, axis=1, keepdims=True) + NORM_EPS)
        return x, inv, (x * inv * gain).astype(jnp.bfloat16)

    for i in range(q_ref.shape[1] // head_size):
        cols = slice(i * head_size, (i + 1) * head_size)
        qx, qinv, q = normed(q_ref, cols, q_gain)
        kx, kinv, kn = normed(ek_ref, cols, k_gain)
        lx0, linv0, ln0 = normed(lk0_ref, cols, k_gain)
        lx1, linv1, ln1 = normed(lk1_ref, cols, k_gain)
        g = g_ref[:, cols]
        k = jnp.concatenate([kn, ln0, ln1], axis=0)
        v = jnp.concatenate([ev_ref[:, cols], lv0_ref[:, cols], lv1_ref[:, cols]], axis=0)
        s = lax.dot_general(q, k, nt, preferred_element_type=f32) * scale
        e = jnp.where(keep, jnp.exp(s), 0.0)
        tot = jnp.sum(e, axis=1, keepdims=True)
        p = e / tot
        p_low = p.astype(jnp.bfloat16)
        o = jnp.dot(p_low, v, preferred_element_type=f32).astype(jnp.bfloat16)
        o_ref[:, cols] = o
        delta = jnp.sum(g.astype(f32) * o.astype(f32), axis=1, keepdims=True)
        dp = lax.dot_general(g, v, nt, preferred_element_type=f32)
        ds = (p * (dp - delta)).astype(jnp.bfloat16)
        dq = jnp.dot(ds, k, preferred_element_type=f32) * scale
        dk = lax.dot_general(ds, q, tn, preferred_element_type=f32) * scale
        dv = lax.dot_general(p_low, g, tn, preferred_element_type=f32)
        scaled = dq * q_gain
        dqi_ref[:, cols] = (
            qinv * scaled - qx * qinv * qinv * qinv * jnp.mean(scaled * qx, axis=1, keepdims=True)
        ).astype(jnp.bfloat16)
        dke_ref[:, cols] = dk[:window]
        dve_ref[:, cols] = dv[:window]
        for j in range(part_ref.shape[1] // BLK):
            for c, d in enumerate((dk, dv)):
                placed = jnp.zeros((BLK, head_size), f32)
                for s_ in range(tiles_ref.shape[0]):
                    rows = d[window + s_ * BLK : window + (s_ + 1) * BLK]
                    placed = placed + jnp.where(tiles_ref[s_] == j, rows, 0.0)
                part_ref[c, j * BLK : (j + 1) * BLK, cols] = placed.astype(part_ref.dtype)
        gq = jnp.sum(dq * qx * qinv, axis=0, keepdims=True)
        gk = (
            jnp.sum(dk[:window] * kx * kinv, axis=0, keepdims=True)
            + jnp.sum(dk[window : window + BLK] * lx0 * linv0, axis=0, keepdims=True)
            + jnp.sum(dk[window + BLK :] * lx1 * linv1, axis=0, keepdims=True)
        )
        gain_ref[:, cols] = jnp.concatenate([gq, gk, jnp.zeros((6, head_size), f32)], axis=0)


def attention_block(tiles, q, ext, lyr, g, keep, q_gain, k_gain, scale):
    lyric_rows = lyr.shape[1]
    rows, width = q.shape
    head_size = q_gain.shape[0]
    window = ext.shape[1]
    slots = tiles.shape[0]
    heads = width // head_size
    f32 = jnp.float32

    per = 4 if heads % 4 == 0 else 1
    span = per * head_size

    def col(r):
        return pl.BlockSpec((r, span), lambda h, t: (0, h))

    def slot(c, s):
        return pl.BlockSpec((None, BLK, span), lambda h, t: (c, jnp.maximum(t[s], 0), h))

    def side(c):
        return pl.BlockSpec((None, window, span), lambda h, t: (c, 0, h))

    whole = pl.BlockSpec((1, head_size), lambda h, t: (0, 0))
    grid_spec = pltpu.PrefetchScalarGridSpec(
        num_scalar_prefetch=1,
        grid=(heads // per,),
        in_specs=[col(rows), side(0), side(1), slot(0, 0), slot(0, 1), slot(1, 0), slot(1, 1), col(rows),
                  pl.BlockSpec((1, keep.shape[1]), lambda h, t: (0, 0)), whole, whole],
        out_specs=[col(rows), col(rows), col(window), col(window),
                   pl.BlockSpec((2, lyric_rows, span), lambda h, t: (0, 0, h)), col(8)],
    )
    return pl.pallas_call(
        lambda *refs: attention_kernel(*refs, scale=scale),
        grid_spec=grid_spec,
        out_shape=[
            jax.ShapeDtypeStruct((rows, width), jnp.bfloat16),
            jax.ShapeDtypeStruct((rows, width), jnp.bfloat16),
            jax.ShapeDtypeStruct((window, width), f32),
            jax.ShapeDtypeStruct((window, width), f32),
            jax.ShapeDtypeStruct((2, lyric_rows, width), jnp.bfloat16),
            jax.ShapeDtypeStruct((8, width), f32),
        ],
    )(tiles, q, ext, ext, lyr, lyr, lyr, lyr, g, keep, q_gain.reshape(1, head_size), k_gain.reshape(1, head_size))


def body(
    queries, keys, values, lyric_keys, lyric_values, q_gain, k_gain, cotangent, alignment, lyric_len
):
    head_size = q_gain.shape[0]
    model_width = queries.shape[2]
    head_count = model_width // head_size
    frames = queries.shape[1]
    lyric_local = lyric_keys.shape[1]
    seq_count = lax.axis_size("seq")
    border_rows = WIN * BLK
    window_extent = (2 * WIN + 1) * BLK
    score_scale = head_size ** (-0.5)
    total_frames = frames * seq_count
    first_frame = lax.axis_index("seq") * frames
    lyric_total = lyric_local * seq_count
    lyric_blocks = lyric_total // BLK
    masks = seq_masks(seq_count)

    lyric_pair = jnp.stack([lyric_keys[0], lyric_values[0]])
    lyric_all = gather_doubling(lyric_pair, "seq", masks[::-1])
    lyric_all = jnp.swapaxes(lyric_all, 0, 1).reshape(2, lyric_total, model_width)

    query_raw = queries[0]
    lyric_inv = norm_heads(lyric_keys[0], k_gain)[1]

    stacked = jnp.stack([keys[0], values[0]])
    extended = extended_2(stacked, (("seq", 1),), border_rows)
    key_raw = keys[0]
    key_inv = norm_heads(key_raw, k_gain)[1]
    length = lyric_len[0]

    position = first_frame - border_rows + jnp.arange(window_extent, dtype=jnp.int32)
    audio_mask = (position >= 0) & (position < total_frames)
    tile_ids = alignment[0, 0]
    tiles = jnp.maximum(tile_ids, 0)
    lyric_mask = jnp.concatenate(
        [(tile_ids[s] >= 0) & (tiles[s] * BLK + jnp.arange(BLK, dtype=jnp.int32) < length) for s in range(TILES)]
    )
    keep_mask = jnp.concatenate([audio_mask, lyric_mask], axis=0).astype(jnp.float32)[None]
    block_output, unnormed_query_gradient, ext_grad_key, ext_grad_val, parts, gain_rows = attention_block(
        tile_ids,
        query_raw,
        extended,
        lyric_all,
        cotangent[0],
        keep_mask,
        q_gain,
        k_gain,
        score_scale,
    )
    ext_grad_key = ext_grad_key.reshape(window_extent, head_count, head_size)
    ext_grad_val = ext_grad_val.reshape(window_extent, head_count, head_size)
    gains = jnp.sum(gain_rows[:2].reshape(2, head_count, head_size), axis=1)
    summed, gains = scatter_halving(parts.reshape(2, seq_count, lyric_local, model_width), "seq", masks, gains)
    total_gains = sum_doubling(gains, ("song",))
    summed_key = summed[0].reshape(lyric_local, head_count, head_size)
    summed_val = summed[1]

    own_grad_key = ext_grad_key[border_rows : border_rows + frames]
    own_grad_val = ext_grad_val[border_rows : border_rows + frames]
    rims = jnp.stack(
        [
            jnp.concatenate(
                [ext_grad_key[:border_rows], ext_grad_key[border_rows + frames :]], axis=0
            ).reshape(2 * border_rows, model_width),
            jnp.concatenate(
                [ext_grad_val[:border_rows], ext_grad_val[border_rows + frames :]], axis=0
            ).reshape(2 * border_rows, model_width),
        ]
    )
    received = extended_2(rims.astype(jnp.bfloat16), (("seq", 1),), border_rows).astype(rims.dtype)
    from_left = received[:, :border_rows].reshape(2, border_rows, head_count, head_size)
    from_right = received[:, 3 * border_rows :].reshape(2, border_rows, head_count, head_size)
    own_grad_key = (
        own_grad_key.at[:border_rows]
        .add(from_left[0])
        .at[frames - border_rows :]
        .add(from_right[0])
    )
    own_grad_val = (
        own_grad_val.at[:border_rows]
        .add(from_left[1])
        .at[frames - border_rows :]
        .add(from_right[1])
    )
    unnormed_key_gradient = norm_back(key_raw, key_inv, k_gain, own_grad_key)[0]
    unnormed_lyric_gradient = norm_back(lyric_keys[0], lyric_inv, k_gain, summed_key)[0]
    return (
        block_output.reshape(1, frames, model_width),
        unnormed_query_gradient[None],
        unnormed_key_gradient.astype(jnp.bfloat16)[None],
        own_grad_val.reshape(1, frames, model_width).astype(jnp.bfloat16),
        unnormed_lyric_gradient.astype(jnp.bfloat16)[None],
        summed_val.astype(jnp.bfloat16)[None],
        total_gains[0],
        total_gains[1],
    )


def solution(mesh):
    in_specs = (
        P("song", "seq", None),
        P("song", "seq", None),
        P("song", "seq", None),
        P("song", "seq", None),
        P("song", "seq", None),
        P(),
        P(),
        P("song", "seq", None),
        P("song", "seq", None),
        P("song"),
    )
    out_specs = (
        P("song", "seq", None),
        P("song", "seq", None),
        P("song", "seq", None),
        P("song", "seq", None),
        P("song", "seq", None),
        P("song", "seq", None),
        P(),
        P(),
    )
    return jax.shard_map(body, mesh=mesh, in_specs=in_specs, out_specs=out_specs, check_vma=False)
```

```python
import jax
import jax.numpy as jnp
from jax import lax
from jax.sharding import PartitionSpec as P
from jax.experimental import pallas as pl
from jax.experimental.pallas import tpu as pltpu

BLK = 128
WIN = 1
TILES = 2


NORM_EPS = 1e-06


def extended_2(block, sides, width):
    for axis, dim in sides:
        count = lax.axis_size(axis)
        forward = [(i, i + 1) for i in range(count - 1)]
        backward = [(target, source) for source, target in forward]
        low = lax.ppermute(
            lax.slice_in_dim(block, block.shape[dim] - width, None, axis=dim), axis, forward
        )
        high = lax.ppermute(lax.slice_in_dim(block, 0, width, axis=dim), axis, backward)
        block = jnp.concatenate([low, block, high], axis=dim)
    return block


def seq_masks(count):
    masks = []
    m = 1
    while m < count:
        masks.append(m)
        m *= 2
    return masks


def swap_with(x, axis, mask):
    count = lax.axis_size(axis)
    return lax.ppermute(x, axis, [(i, i ^ mask) for i in range(count)])


def gather_doubling(chunk, axis, order):
    idx = lax.axis_index(axis)
    buf = chunk[None]
    for mask in order:
        other = swap_with(buf, axis, mask)
        high = (idx & mask) != 0
        buf = jnp.where(high, jnp.concatenate([other, buf]), jnp.concatenate([buf, other]))
    steps = len(order)
    buf = buf.reshape((2,) * steps + chunk.shape)
    held = [order[steps - 1 - k] for k in range(steps)]
    perm = sorted(range(steps), key=lambda k: -held[k])
    buf = jnp.transpose(buf, perm + list(range(steps, buf.ndim)))
    return buf.reshape((2 ** steps,) + chunk.shape)


def scatter_halving(parts, axis, order, rider):
    idx = lax.axis_index(axis)
    steps = len(order)
    buf = parts.reshape(parts.shape[:1] + (2,) * steps + parts.shape[2:])
    held = sorted(order, reverse=True)
    for mask in order:
        a = held.index(mask) + 1
        high = ((idx & mask) != 0).astype(jnp.int32)
        keep = lax.dynamic_index_in_dim(buf, high, axis=a, keepdims=False)
        send = lax.dynamic_index_in_dim(buf, 1 - high, axis=a, keepdims=False)
        got, other = swap_with((send.astype(jnp.bfloat16), rider), axis, mask)
        buf = keep.astype(jnp.float32) + got.astype(jnp.float32)
        rider = rider + other
        held.pop(a - 1)
    return buf, rider


def sum_doubling(x, axes):
    for axis in axes:
        for mask in seq_masks(lax.axis_size(axis)):
            x = x + swap_with(x, axis, mask)
    return x


def norm_heads(inputs, norm_gain):
    row_values = inputs.astype(jnp.float32).reshape(inputs.shape[0], -1, norm_gain.shape[0])
    inverse = lax.rsqrt(jnp.mean(row_values * row_values, axis=-1, keepdims=True) + NORM_EPS)
    return (row_values * inverse * norm_gain, inverse)


def norm_back(inputs, inverse, norm_gain, grad_out):
    row_values = inputs.astype(jnp.float32).reshape(grad_out.shape)
    scaled = grad_out * norm_gain
    grad_input = inverse * scaled - row_values * inverse * inverse * inverse * jnp.mean(
        scaled * row_values, axis=-1, keepdims=True
    )
    grad_gain = jnp.sum(grad_out * row_values * inverse, axis=(0, 1))
    return (grad_input.reshape(inputs.shape), grad_gain)


def block_pass(query_rows, key_rows, value_rows, keep_mask, grad_rows, score_scale):
    scores = (
        jnp.einsum("qhd,khd->hqk", query_rows, key_rows, preferred_element_type=jnp.float32)
        * score_scale
    )
    exp_scores = jnp.where(keep_mask[None, None, :], jnp.exp(scores), 0.0)
    totals = jnp.sum(exp_scores, axis=2)
    prob_full = exp_scores / totals[:, :, None]
    prob_low = prob_full.astype(jnp.bfloat16)
    block_output = jnp.einsum(
        "hqk,khd->qhd", prob_low, value_rows, preferred_element_type=jnp.float32
    ).astype(jnp.bfloat16)
    delta_rows = jnp.sum(grad_rows.astype(jnp.float32) * block_output.astype(jnp.float32), axis=2).T
    grad_prob = jnp.einsum(
        "qhd,khd->hqk", grad_rows, value_rows, preferred_element_type=jnp.float32
    )
    grad_score = (prob_full * (grad_prob - delta_rows[:, :, None])).astype(jnp.bfloat16)
    query_gradient = (
        jnp.einsum("hqk,khd->qhd", grad_score, key_rows, preferred_element_type=jnp.float32)
        * score_scale
    )
    grad_key = (
        jnp.einsum("hqk,qhd->khd", grad_score, query_rows, preferred_element_type=jnp.float32)
        * score_scale
    )
    value_gradient = jnp.einsum(
        "hqk,qhd->khd", prob_low, grad_rows, preferred_element_type=jnp.float32
    )
    return (block_output, query_gradient, grad_key, value_gradient)


def attention_kernel(
    tiles_ref, q_ref, ek_ref, ev_ref, lk0_ref, lk1_ref, lv0_ref, lv1_ref, g_ref, m_ref, qg_ref, kg_ref,
    o_ref, dqi_ref, dke_ref, dve_ref, part_ref, gain_ref, *, scale
):
    f32 = jnp.float32
    window = ek_ref.shape[0]
    head_size = qg_ref.shape[1]
    q_gain = qg_ref[...]
    k_gain = kg_ref[...]
    keep = m_ref[...] > 0.0
    nt = (((1,), (1,)), ((), ()))
    tn = (((0,), (0,)), ((), ()))

    def normed(x_ref, cols, gain):
        x = x_ref[:, cols].astype(f32)
        inv = lax.rsqrt(jnp.mean(x * x, axis=1, keepdims=True) + NORM_EPS)
        return x, inv, (x * inv * gain).astype(jnp.bfloat16)

    for i in range(q_ref.shape[1] // head_size):
        cols = slice(i * head_size, (i + 1) * head_size)
        qx, qinv, q = normed(q_ref, cols, q_gain)
        kx, kinv, kn = normed(ek_ref, cols, k_gain)
        lx0, linv0, ln0 = normed(lk0_ref, cols, k_gain)
        lx1, linv1, ln1 = normed(lk1_ref, cols, k_gain)
        g = g_ref[:, cols]
        k = jnp.concatenate([kn, ln0, ln1], axis=0)
        v = jnp.concatenate([ev_ref[:, cols], lv0_ref[:, cols], lv1_ref[:, cols]], axis=0)
        s = lax.dot_general(q, k, nt, preferred_element_type=f32) * scale
        e = jnp.where(keep, jnp.exp(s), 0.0)
        tot = jnp.sum(e, axis=1, keepdims=True)
        p = e / tot
        p_low = p.astype(jnp.bfloat16)
        o = jnp.dot(p_low, v, preferred_element_type=f32).astype(jnp.bfloat16)
        o_ref[:, cols] = o
        delta = jnp.sum(g.astype(f32) * o.astype(f32), axis=1, keepdims=True)
        dp = lax.dot_general(g, v, nt, preferred_element_type=f32)
        ds = (p * (dp - delta)).astype(jnp.bfloat16)
        dq = jnp.dot(ds, k, preferred_element_type=f32) * scale
        dk = lax.dot_general(ds, q, tn, preferred_element_type=f32) * scale
        dv = lax.dot_general(p_low, g, tn, preferred_element_type=f32)
        scaled = dq * q_gain
        dqi_ref[:, cols] = (
            qinv * scaled - qx * qinv * qinv * qinv * jnp.mean(scaled * qx, axis=1, keepdims=True)
        ).astype(jnp.bfloat16)
        dke_ref[:, cols] = dk[:window]
        dve_ref[:, cols] = dv[:window]
        for j in range(part_ref.shape[1] // BLK):
            for c, d in enumerate((dk, dv)):
                placed = jnp.zeros((BLK, head_size), f32)
                for s_ in range(tiles_ref.shape[0]):
                    rows = d[window + s_ * BLK : window + (s_ + 1) * BLK]
                    placed = placed + jnp.where(tiles_ref[s_] == j, rows, 0.0)
                part_ref[c, j * BLK : (j + 1) * BLK, cols] = placed.astype(part_ref.dtype)
        gq = jnp.sum(dq * qx * qinv, axis=0, keepdims=True)
        gk = (
            jnp.sum(dk[:window] * kx * kinv, axis=0, keepdims=True)
            + jnp.sum(dk[window : window + BLK] * lx0 * linv0, axis=0, keepdims=True)
            + jnp.sum(dk[window + BLK :] * lx1 * linv1, axis=0, keepdims=True)
        )
        gain_ref[:, cols] = jnp.concatenate([gq, gk, jnp.zeros((6, head_size), f32)], axis=0)


def attention_block(tiles, q, ek, ev, lk, lv, g, keep, q_gain, k_gain, scale):
    lyric_rows = lk.shape[0]
    rows, width = q.shape
    head_size = q_gain.shape[0]
    window = ek.shape[0]
    slots = tiles.shape[0]
    heads = width // head_size
    f32 = jnp.float32

    per = 8 if heads % 8 == 0 else 1
    span = per * head_size

    def col(r):
        return pl.BlockSpec((r, span), lambda h, t: (0, h))

    def slot(s):
        return pl.BlockSpec((BLK, span), lambda h, t: (jnp.maximum(t[s], 0), h))

    whole = pl.BlockSpec((1, head_size), lambda h, t: (0, 0))
    grid_spec = pltpu.PrefetchScalarGridSpec(
        num_scalar_prefetch=1,
        grid=(heads // per,),
        in_specs=[col(rows), col(window), col(window), slot(0), slot(1), slot(0), slot(1), col(rows),
                  pl.BlockSpec((1, keep.shape[1]), lambda h, t: (0, 0)), whole, whole],
        out_specs=[col(rows), col(rows), col(window), col(window),
                   pl.BlockSpec((2, lyric_rows, span), lambda h, t: (0, 0, h)), col(8)],
    )
    return pl.pallas_call(
        lambda *refs: attention_kernel(*refs, scale=scale),
        grid_spec=grid_spec,
        out_shape=[
            jax.ShapeDtypeStruct((rows, width), jnp.bfloat16),
            jax.ShapeDtypeStruct((rows, width), jnp.bfloat16),
            jax.ShapeDtypeStruct((window, width), f32),
            jax.ShapeDtypeStruct((window, width), f32),
            jax.ShapeDtypeStruct((2, lyric_rows, width), jnp.bfloat16),
            jax.ShapeDtypeStruct((8, width), f32),
        ],
    )(tiles, q, ek, ev, lk, lk, lv, lv, g, keep, q_gain.reshape(1, head_size), k_gain.reshape(1, head_size))


def body(
    queries, keys, values, lyric_keys, lyric_values, q_gain, k_gain, cotangent, alignment, lyric_len
):
    head_size = q_gain.shape[0]
    model_width = queries.shape[2]
    head_count = model_width // head_size
    frames = queries.shape[1]
    lyric_local = lyric_keys.shape[1]
    seq_count = lax.axis_size("seq")
    border_rows = WIN * BLK
    window_extent = (2 * WIN + 1) * BLK
    score_scale = head_size ** (-0.5)
    total_frames = frames * seq_count
    first_frame = lax.axis_index("seq") * frames
    lyric_total = lyric_local * seq_count
    lyric_blocks = lyric_total // BLK
    masks = seq_masks(seq_count)

    lyric_pair = jnp.stack([lyric_keys[0], lyric_values[0]])
    lyric_all = gather_doubling(lyric_pair, "seq", masks[::-1])
    lyric_all = jnp.swapaxes(lyric_all, 0, 1).reshape(2, lyric_total, model_width)

    query_raw = queries[0]
    lyric_inv = norm_heads(lyric_keys[0], k_gain)[1]

    stacked = jnp.stack([keys[0], values[0]])
    extended = extended_2(stacked, (("seq", 1),), border_rows)
    key_raw = keys[0]
    key_inv = norm_heads(key_raw, k_gain)[1]
    length = lyric_len[0]

    position = first_frame - border_rows + jnp.arange(window_extent, dtype=jnp.int32)
    audio_mask = (position >= 0) & (position < total_frames)
    tile_ids = alignment[0, 0]
    tiles = jnp.maximum(tile_ids, 0)
    lyric_mask = jnp.concatenate(
        [(tile_ids[s] >= 0) & (tiles[s] * BLK + jnp.arange(BLK, dtype=jnp.int32) < length) for s in range(TILES)]
    )
    keep_mask = jnp.concatenate([audio_mask, lyric_mask], axis=0).astype(jnp.float32)[None]
    block_output, unnormed_query_gradient, ext_grad_key, ext_grad_val, parts, gain_rows = attention_block(
        tile_ids,
        query_raw,
        extended[0],
        extended[1],
        lyric_all[0],
        lyric_all[1],
        cotangent[0],
        keep_mask,
        q_gain,
        k_gain,
        score_scale,
    )
    ext_grad_key = ext_grad_key.reshape(window_extent, head_count, head_size)
    ext_grad_val = ext_grad_val.reshape(window_extent, head_count, head_size)
    gains = jnp.sum(gain_rows[:2].reshape(2, head_count, head_size), axis=1)
    summed, gains = scatter_halving(parts.reshape(2, seq_count, lyric_local, model_width), "seq", masks, gains)
    total_gains = sum_doubling(gains, ("song",))
    summed_key = summed[0].reshape(lyric_local, head_count, head_size)
    summed_val = summed[1]

    own_grad_key = ext_grad_key[border_rows : border_rows + frames]
    own_grad_val = ext_grad_val[border_rows : border_rows + frames]
    rims = jnp.stack(
        [
            jnp.concatenate(
                [ext_grad_key[:border_rows], ext_grad_key[border_rows + frames :]], axis=0
            ).reshape(2 * border_rows, model_width),
            jnp.concatenate(
                [ext_grad_val[:border_rows], ext_grad_val[border_rows + frames :]], axis=0
            ).reshape(2 * border_rows, model_width),
        ]
    )
    received = extended_2(rims.astype(jnp.bfloat16), (("seq", 1),), border_rows).astype(rims.dtype)
    from_left = received[:, :border_rows].reshape(2, border_rows, head_count, head_size)
    from_right = received[:, 3 * border_rows :].reshape(2, border_rows, head_count, head_size)
    own_grad_key = (
        own_grad_key.at[:border_rows]
        .add(from_left[0])
        .at[frames - border_rows :]
        .add(from_right[0])
    )
    own_grad_val = (
        own_grad_val.at[:border_rows]
        .add(from_left[1])
        .at[frames - border_rows :]
        .add(from_right[1])
    )
    unnormed_key_gradient = norm_back(key_raw, key_inv, k_gain, own_grad_key)[0]
    unnormed_lyric_gradient = norm_back(lyric_keys[0], lyric_inv, k_gain, summed_key)[0]
    return (
        block_output.reshape(1, frames, model_width),
        unnormed_query_gradient[None],
        unnormed_key_gradient.astype(jnp.bfloat16)[None],
        own_grad_val.reshape(1, frames, model_width).astype(jnp.bfloat16),
        unnormed_lyric_gradient.astype(jnp.bfloat16)[None],
        summed_val.astype(jnp.bfloat16)[None],
        total_gains[0],
        total_gains[1],
    )


def solution(mesh):
    in_specs = (
        P("song", "seq", None),
        P("song", "seq", None),
        P("song", "seq", None),
        P("song", "seq", None),
        P("song", "seq", None),
        P(),
        P(),
        P("song", "seq", None),
        P("song", "seq", None),
        P("song"),
    )
    out_specs = (
        P("song", "seq", None),
        P("song", "seq", None),
        P("song", "seq", None),
        P("song", "seq", None),
        P("song", "seq", None),
        P("song", "seq", None),
        P(),
        P(),
    )
    return jax.shard_map(body, mesh=mesh, in_specs=in_specs, out_specs=out_specs, check_vma=False)
```

```python
import jax
import jax.numpy as jnp
from jax import lax
from jax.sharding import PartitionSpec as P
from jax.experimental import pallas as pl
from jax.experimental.pallas import tpu as pltpu

BLK = 128
WIN = 1
TILES = 2


NORM_EPS = 1e-06


def extended_2(block, sides, width):
    for axis, dim in sides:
        count = lax.axis_size(axis)
        forward = [(i, i + 1) for i in range(count - 1)]
        backward = [(target, source) for source, target in forward]
        low = lax.ppermute(
            lax.slice_in_dim(block, block.shape[dim] - width, None, axis=dim), axis, forward
        )
        high = lax.ppermute(lax.slice_in_dim(block, 0, width, axis=dim), axis, backward)
        block = jnp.concatenate([low, block, high], axis=dim)
    return block


def seq_masks(count):
    masks = []
    m = 1
    while m < count:
        masks.append(m)
        m *= 2
    return masks


def swap_with(x, axis, mask):
    count = lax.axis_size(axis)
    return lax.ppermute(x, axis, [(i, i ^ mask) for i in range(count)])


def gather_doubling(chunk, axis, order):
    idx = lax.axis_index(axis)
    buf = chunk[None]
    for mask in order:
        other = swap_with(buf, axis, mask)
        high = (idx & mask) != 0
        buf = jnp.where(high, jnp.concatenate([other, buf]), jnp.concatenate([buf, other]))
    steps = len(order)
    buf = buf.reshape((2,) * steps + chunk.shape)
    held = [order[steps - 1 - k] for k in range(steps)]
    perm = sorted(range(steps), key=lambda k: -held[k])
    buf = jnp.transpose(buf, perm + list(range(steps, buf.ndim)))
    return buf.reshape((2 ** steps,) + chunk.shape)


def scatter_halving(parts, axis, order, rider, hold):
    idx = lax.axis_index(axis)
    steps = len(order)
    buf = parts.reshape(parts.shape[:1] + (2,) * steps + parts.shape[2:])
    held = sorted(order, reverse=True)
    for step, mask in enumerate(order):
        if step == 2:
            hold, buf = lax.optimization_barrier((hold, buf))
        a = held.index(mask) + 1
        high = ((idx & mask) != 0).astype(jnp.int32)
        keep = lax.dynamic_index_in_dim(buf, high, axis=a, keepdims=False)
        send = lax.dynamic_index_in_dim(buf, 1 - high, axis=a, keepdims=False)
        got, other = swap_with((send.astype(jnp.bfloat16), rider), axis, mask)
        buf = keep.astype(jnp.float32) + got.astype(jnp.float32)
        rider = rider + other
        held.pop(a - 1)
    return buf, rider, hold


def sum_doubling(x, axes):
    for axis in axes:
        for mask in seq_masks(lax.axis_size(axis)):
            x = x + swap_with(x, axis, mask)
    return x


def norm_heads(inputs, norm_gain):
    row_values = inputs.astype(jnp.float32).reshape(inputs.shape[0], -1, norm_gain.shape[0])
    inverse = lax.rsqrt(jnp.mean(row_values * row_values, axis=-1, keepdims=True) + NORM_EPS)
    return (row_values * inverse * norm_gain, inverse)


def norm_back(inputs, inverse, norm_gain, grad_out):
    row_values = inputs.astype(jnp.float32).reshape(grad_out.shape)
    scaled = grad_out * norm_gain
    grad_input = inverse * scaled - row_values * inverse * inverse * inverse * jnp.mean(
        scaled * row_values, axis=-1, keepdims=True
    )
    grad_gain = jnp.sum(grad_out * row_values * inverse, axis=(0, 1))
    return (grad_input.reshape(inputs.shape), grad_gain)


def block_pass(query_rows, key_rows, value_rows, keep_mask, grad_rows, score_scale):
    scores = (
        jnp.einsum("qhd,khd->hqk", query_rows, key_rows, preferred_element_type=jnp.float32)
        * score_scale
    )
    exp_scores = jnp.where(keep_mask[None, None, :], jnp.exp(scores), 0.0)
    totals = jnp.sum(exp_scores, axis=2)
    prob_full = exp_scores / totals[:, :, None]
    prob_low = prob_full.astype(jnp.bfloat16)
    block_output = jnp.einsum(
        "hqk,khd->qhd", prob_low, value_rows, preferred_element_type=jnp.float32
    ).astype(jnp.bfloat16)
    delta_rows = jnp.sum(grad_rows.astype(jnp.float32) * block_output.astype(jnp.float32), axis=2).T
    grad_prob = jnp.einsum(
        "qhd,khd->hqk", grad_rows, value_rows, preferred_element_type=jnp.float32
    )
    grad_score = (prob_full * (grad_prob - delta_rows[:, :, None])).astype(jnp.bfloat16)
    query_gradient = (
        jnp.einsum("hqk,khd->qhd", grad_score, key_rows, preferred_element_type=jnp.float32)
        * score_scale
    )
    grad_key = (
        jnp.einsum("hqk,qhd->khd", grad_score, query_rows, preferred_element_type=jnp.float32)
        * score_scale
    )
    value_gradient = jnp.einsum(
        "hqk,qhd->khd", prob_low, grad_rows, preferred_element_type=jnp.float32
    )
    return (block_output, query_gradient, grad_key, value_gradient)


def attention_kernel(
    tiles_ref, q_ref, ek_ref, ev_ref, lk0_ref, lk1_ref, lv0_ref, lv1_ref, g_ref, m_ref, qg_ref, kg_ref,
    o_ref, dqi_ref, dke_ref, dve_ref, part_ref, gain_ref, *, scale
):
    f32 = jnp.float32
    window = ek_ref.shape[0]
    head_size = qg_ref.shape[1]
    q_gain = qg_ref[...]
    k_gain = kg_ref[...]
    keep = m_ref[...] > 0.0
    nt = (((1,), (1,)), ((), ()))
    tn = (((0,), (0,)), ((), ()))

    def normed(x_ref, cols, gain):
        x = x_ref[:, cols].astype(f32)
        inv = lax.rsqrt(jnp.mean(x * x, axis=1, keepdims=True) + NORM_EPS)
        return x, inv, (x * inv * gain).astype(jnp.bfloat16)

    for i in range(q_ref.shape[1] // head_size):
        cols = slice(i * head_size, (i + 1) * head_size)
        qx, qinv, q = normed(q_ref, cols, q_gain)
        kx, kinv, kn = normed(ek_ref, cols, k_gain)
        lx0, linv0, ln0 = normed(lk0_ref, cols, k_gain)
        lx1, linv1, ln1 = normed(lk1_ref, cols, k_gain)
        g = g_ref[:, cols]
        k = jnp.concatenate([kn, ln0, ln1], axis=0)
        v = jnp.concatenate([ev_ref[:, cols], lv0_ref[:, cols], lv1_ref[:, cols]], axis=0)
        s = lax.dot_general(q, k, nt, preferred_element_type=f32) * scale
        e = jnp.where(keep, jnp.exp(s), 0.0)
        tot = jnp.sum(e, axis=1, keepdims=True)
        p = e / tot
        p_low = p.astype(jnp.bfloat16)
        o = jnp.dot(p_low, v, preferred_element_type=f32).astype(jnp.bfloat16)
        o_ref[:, cols] = o
        delta = jnp.sum(g.astype(f32) * o.astype(f32), axis=1, keepdims=True)
        dp = lax.dot_general(g, v, nt, preferred_element_type=f32)
        ds = (p * (dp - delta)).astype(jnp.bfloat16)
        dq = jnp.dot(ds, k, preferred_element_type=f32) * scale
        dk = lax.dot_general(ds, q, tn, preferred_element_type=f32) * scale
        dv = lax.dot_general(p_low, g, tn, preferred_element_type=f32)
        scaled = dq * q_gain
        dqi_ref[:, cols] = (
            qinv * scaled - qx * qinv * qinv * qinv * jnp.mean(scaled * qx, axis=1, keepdims=True)
        ).astype(jnp.bfloat16)
        dke_ref[:, cols] = dk[:window]
        dve_ref[:, cols] = dv[:window]
        for j in range(part_ref.shape[1] // BLK):
            for c, d in enumerate((dk, dv)):
                placed = jnp.zeros((BLK, head_size), f32)
                for s_ in range(tiles_ref.shape[0]):
                    rows = d[window + s_ * BLK : window + (s_ + 1) * BLK]
                    placed = placed + jnp.where(tiles_ref[s_] == j, rows, 0.0)
                part_ref[c, j * BLK : (j + 1) * BLK, cols] = placed.astype(part_ref.dtype)
        gq = jnp.sum(dq * qx * qinv, axis=0, keepdims=True)
        gk = (
            jnp.sum(dk[:window] * kx * kinv, axis=0, keepdims=True)
            + jnp.sum(dk[window : window + BLK] * lx0 * linv0, axis=0, keepdims=True)
            + jnp.sum(dk[window + BLK :] * lx1 * linv1, axis=0, keepdims=True)
        )
        gain_ref[:, cols] = jnp.concatenate([gq, gk, jnp.zeros((6, head_size), f32)], axis=0)


def attention_block(tiles, q, ek, ev, lk, lv, g, keep, q_gain, k_gain, scale):
    lyric_rows = lk.shape[0]
    rows, width = q.shape
    head_size = q_gain.shape[0]
    window = ek.shape[0]
    slots = tiles.shape[0]
    heads = width // head_size
    f32 = jnp.float32

    per = 4 if heads % 4 == 0 else 1
    span = per * head_size

    def col(r):
        return pl.BlockSpec((r, span), lambda h, t: (0, h))

    def slot(s):
        return pl.BlockSpec((BLK, span), lambda h, t: (jnp.maximum(t[s], 0), h))

    whole = pl.BlockSpec((1, head_size), lambda h, t: (0, 0))
    grid_spec = pltpu.PrefetchScalarGridSpec(
        num_scalar_prefetch=1,
        grid=(heads // per,),
        in_specs=[col(rows), col(window), col(window), slot(0), slot(1), slot(0), slot(1), col(rows),
                  pl.BlockSpec((1, keep.shape[1]), lambda h, t: (0, 0)), whole, whole],
        out_specs=[col(rows), col(rows), col(window), col(window),
                   pl.BlockSpec((2, lyric_rows, span), lambda h, t: (0, 0, h)), col(8)],
    )
    return pl.pallas_call(
        lambda *refs: attention_kernel(*refs, scale=scale),
        grid_spec=grid_spec,
        out_shape=[
            jax.ShapeDtypeStruct((rows, width), jnp.bfloat16),
            jax.ShapeDtypeStruct((rows, width), jnp.bfloat16),
            jax.ShapeDtypeStruct((window, width), f32),
            jax.ShapeDtypeStruct((window, width), f32),
            jax.ShapeDtypeStruct((2, lyric_rows, width), jnp.bfloat16),
            jax.ShapeDtypeStruct((8, width), f32),
        ],
    )(tiles, q, ek, ev, lk, lk, lv, lv, g, keep, q_gain.reshape(1, head_size), k_gain.reshape(1, head_size))


def body(
    queries, keys, values, lyric_keys, lyric_values, q_gain, k_gain, cotangent, alignment, lyric_len
):
    head_size = q_gain.shape[0]
    model_width = queries.shape[2]
    head_count = model_width // head_size
    frames = queries.shape[1]
    lyric_local = lyric_keys.shape[1]
    seq_count = lax.axis_size("seq")
    border_rows = WIN * BLK
    window_extent = (2 * WIN + 1) * BLK
    score_scale = head_size ** (-0.5)
    total_frames = frames * seq_count
    first_frame = lax.axis_index("seq") * frames
    lyric_total = lyric_local * seq_count
    lyric_blocks = lyric_total // BLK
    masks = seq_masks(seq_count)

    lyric_pair = jnp.stack([lyric_keys[0], lyric_values[0]])
    lyric_all = gather_doubling(lyric_pair, "seq", masks[::-1])
    lyric_all = jnp.swapaxes(lyric_all, 0, 1).reshape(2, lyric_total, model_width)

    query_raw = queries[0]
    lyric_inv = norm_heads(lyric_keys[0], k_gain)[1]

    stacked = jnp.stack([keys[0], values[0]])
    extended = extended_2(stacked, (("seq", 1),), border_rows)
    key_raw = keys[0]
    key_inv = norm_heads(key_raw, k_gain)[1]
    length = lyric_len[0]

    position = first_frame - border_rows + jnp.arange(window_extent, dtype=jnp.int32)
    audio_mask = (position >= 0) & (position < total_frames)
    tile_ids = alignment[0, 0]
    tiles = jnp.maximum(tile_ids, 0)
    lyric_mask = jnp.concatenate(
        [(tile_ids[s] >= 0) & (tiles[s] * BLK + jnp.arange(BLK, dtype=jnp.int32) < length) for s in range(TILES)]
    )
    keep_mask = jnp.concatenate([audio_mask, lyric_mask], axis=0).astype(jnp.float32)[None]
    block_output, unnormed_query_gradient, ext_grad_key, ext_grad_val, parts, gain_rows = attention_block(
        tile_ids,
        query_raw,
        extended[0],
        extended[1],
        lyric_all[0],
        lyric_all[1],
        cotangent[0],
        keep_mask,
        q_gain,
        k_gain,
        score_scale,
    )
    ext_grad_key = ext_grad_key.reshape(window_extent, head_count, head_size)
    ext_grad_val = ext_grad_val.reshape(window_extent, head_count, head_size)
    gains = jnp.sum(gain_rows[:2].reshape(2, head_count, head_size), axis=1)
    own_grad_key = ext_grad_key[border_rows : border_rows + frames]
    own_grad_val = ext_grad_val[border_rows : border_rows + frames]
    rims = jnp.stack(
        [
            jnp.concatenate(
                [ext_grad_key[:border_rows], ext_grad_key[border_rows + frames :]], axis=0
            ).reshape(2 * border_rows, model_width),
            jnp.concatenate(
                [ext_grad_val[:border_rows], ext_grad_val[border_rows + frames :]], axis=0
            ).reshape(2 * border_rows, model_width),
        ]
    )
    summed, gains, rims = scatter_halving(
        parts.reshape(2, seq_count, lyric_local, model_width), "seq", masks, gains, rims
    )
    total_gains = sum_doubling(gains, ("song",))
    summed_key = summed[0].reshape(lyric_local, head_count, head_size)
    summed_val = summed[1]

    own_grad_key = ext_grad_key[border_rows : border_rows + frames]
    own_grad_val = ext_grad_val[border_rows : border_rows + frames]
    received = extended_2(rims.astype(jnp.bfloat16), (("seq", 1),), border_rows).astype(rims.dtype)
    from_left = received[:, :border_rows].reshape(2, border_rows, head_count, head_size)
    from_right = received[:, 3 * border_rows :].reshape(2, border_rows, head_count, head_size)
    own_grad_key = (
        own_grad_key.at[:border_rows]
        .add(from_left[0])
        .at[frames - border_rows :]
        .add(from_right[0])
    )
    own_grad_val = (
        own_grad_val.at[:border_rows]
        .add(from_left[1])
        .at[frames - border_rows :]
        .add(from_right[1])
    )
    unnormed_key_gradient = norm_back(key_raw, key_inv, k_gain, own_grad_key)[0]
    unnormed_lyric_gradient = norm_back(lyric_keys[0], lyric_inv, k_gain, summed_key)[0]
    return (
        block_output.reshape(1, frames, model_width),
        unnormed_query_gradient[None],
        unnormed_key_gradient.astype(jnp.bfloat16)[None],
        own_grad_val.reshape(1, frames, model_width).astype(jnp.bfloat16),
        unnormed_lyric_gradient.astype(jnp.bfloat16)[None],
        summed_val.astype(jnp.bfloat16)[None],
        total_gains[0],
        total_gains[1],
    )


def solution(mesh):
    in_specs = (
        P("song", "seq", None),
        P("song", "seq", None),
        P("song", "seq", None),
        P("song", "seq", None),
        P("song", "seq", None),
        P(),
        P(),
        P("song", "seq", None),
        P("song", "seq", None),
        P("song"),
    )
    out_specs = (
        P("song", "seq", None),
        P("song", "seq", None),
        P("song", "seq", None),
        P("song", "seq", None),
        P("song", "seq", None),
        P("song", "seq", None),
        P(),
        P(),
    )
    return jax.shard_map(body, mesh=mesh, in_specs=in_specs, out_specs=out_specs, check_vma=False)
```
